32 devices in a mesh: doc: 8 (over y, x, core), ctx: 4 (over z).
Axes of the slice: x: 2, y: 2, z: 4, core: 2. Of those that a mesh axis runs over, the one named last changes fastest.
Arguments:
- layer_input: bfloat16 [16, 576, 1024], P('doc', 'ctx'), may hold values from -6 to 6
- text_count: int32 [16], P('doc'), may hold values from 51 to 512
- coords: int32 [16, 2, 576], P('doc'), may hold values from 0 to 31
- w_qkv: bfloat16 [2, 1024, 3072], P(None, ('doc', 'ctx')), may hold values from -0.1875 to 0.1875
- w_out: bfloat16 [2, 1024, 1024], P(None, ('doc', 'ctx')), may hold values from -0.5 to 0.5
- w_in: bfloat16 [2, 1024, 4096], P(None, ('doc', 'ctx')), may hold values from -0.1875 to 0.1875
- w_down: bfloat16 [2, 4096, 1024], P(None, ('doc', 'ctx')), may hold values from -0.09375 to 0.09375
- rel_tables: bfloat16 [2, 2, 128, 1024], P(None, None, None, ('doc', 'ctx')), may hold values from -6 to 6
- ln_gains: bfloat16 [2, 2, 1024], P(None, None, ('doc', 'ctx')), may hold values from 0.5 to 1.5
- biases: bfloat16 [2, 7, 1024], P(None, None, ('doc', 'ctx')), may hold values from -3 to 3
- b_in: bfloat16 [2, 4096], P(None, ('doc', 'ctx')), may hold values from -3 to 3
- cotangent: bfloat16 [16, 576, 1024], P('doc', 'ctx'), may hold values from -6 to 6
Outputs:
- out_first: float32 [16, 576, 1024], P('doc', 'ctx')
- out_second: float32 [16, 576, 1024], P('doc', 'ctx')
- grad_input: float32 [16, 576, 1024], P('doc', 'ctx')
- grad_w_qkv: float32 [2, 1024, 3072], P(None, ('doc', 'ctx'))
- grad_w_out: float32 [2, 1024, 1024], P(None, ('doc', 'ctx'))
- grad_w_in: float32 [2, 1024, 4096], P(None, ('doc', 'ctx'))
- grad_w_down: float32 [2, 4096, 1024], P(None, ('doc', 'ctx'))
- grad_rel_tables: float32 [2, 2, 128, 1024], P(None, None, None, ('doc', 'ctx'))
- grad_ln_gains: float32 [2, 2, 1024], P(None, None, ('doc', 'ctx'))
- grad_biases: float32 [2, 7, 1024], P(None, None, ('doc', 'ctx'))
- grad_b_in: float32 [2, 4096], P(None, ('doc', 'ctx'))
The draws below stay inside these ranges and needn't reach their ends.
All inputs are finite; a program needn't handle non-finite values.
Results may differ from the reference program's by a relative error of at most 0.028.
Values may be sent and summed in bfloat16 or wider, within the bound.
No kernel may reach another device: no remote copies, remote signals or barrier semaphores. Data moves between devices by JAX's collectives and lax.ppermute only.
A program may use at most 384 MiB of HBM per device.

```python
import jax
import jax.numpy as jnp
from jax import lax

D = 1024
HEADS = 16
HEAD_DIM = 64
FF = 4096
BUCKETS = 128
TEXT = 512
PATCH = 49
SEQ = 576
LAYERS = 2
DOCS = 16


def touch_ends(values, rng, least, top_value):
    dims = values.shape
    index_at = [jax.random.randint(jax.random.fold_in(rng, axis), (), 0, dims[axis]) for axis in range(len(dims))]
    values = values.at[tuple(index_at)].set(least)
    longest = dims.index(max(dims))
    index_at[longest] = (index_at[longest] + 1) % dims[longest]
    return values.at[tuple(index_at)].set(top_value)


def steps_of(rng, shape, cuts, low, top_value):
    loudness, own = 1.0, jax.random.fold_in(rng, 6)
    for position, parts in cuts:
        heights = jnp.exp(jax.random.uniform(jax.random.fold_in(own, position), (parts,), jnp.float32, low / len(cuts), top_value / len(cuts)))
        loudness = loudness * jnp.repeat(heights, shape[position] // parts).reshape([-1 if axis == position else 1 for axis in range(len(shape))])
    return loudness


def bell_draw(key, dims, deviation, most, cuts=(), kind=jnp.bfloat16):
    loudness = steps_of(key, dims, cuts, -0.22, 0.18) if cuts else 1.0
    values = jax.random.normal(key, dims, jnp.float32) * deviation * loudness
    return jnp.minimum(jnp.maximum(values, -most), most).astype(kind)


def setup_inputs(seed: int = 0) -> dict:
    key_list = jax.random.split(jax.random.key(seed), 13)
    layer_input = bell_draw(key_list[0], (DOCS, SEQ, D), 1.0, 6.0, ((0, 8), (1, 4)))
    text_count = touch_ends(jax.random.randint(key_list[1], (DOCS,), TEXT // 10, TEXT + 1), jax.random.fold_in(key_list[1], 1), TEXT // 10, TEXT).astype(jnp.int32)
    coords = touch_ends(jax.random.randint(key_list[2], (DOCS, 2, SEQ), 0, 32), jax.random.fold_in(key_list[2], 1), 0, 31).astype(jnp.int32)
    w_qkv = bell_draw(key_list[3], (LAYERS, D, 3 * D), D ** -0.5, 0.1875, ((1, 32),))
    w_out = bell_draw(key_list[4], (LAYERS, D, D), (D // 8) ** -0.5, 0.5, ((1, 32),))
    w_in = bell_draw(key_list[5], (LAYERS, D, FF), D ** -0.5, 0.1875, ((1, 32),))
    w_down = bell_draw(key_list[6], (LAYERS, FF, D), FF ** -0.5, 0.09375, ((1, 32),))
    rel_tables = bell_draw(key_list[7], (LAYERS, 2, BUCKETS, D), 1.0, 6.0, ((3, 32),))
    ln_gains = jnp.clip(1.0 + 0.1 * jax.random.normal(key_list[8], (LAYERS, 2, D), jnp.float32), 0.5, 1.5).astype(jnp.bfloat16)
    biases = bell_draw(key_list[9], (LAYERS, 7, D), 0.5, 3.0, ((2, 32),))
    b_in = bell_draw(key_list[10], (LAYERS, FF), 0.5, 3.0, ((1, 32),))
    cotangent = bell_draw(key_list[11], (DOCS, SEQ, D), 1.0, 6.0, ((0, 8), (1, 4)))
    return dict(layer_input=layer_input, text_count=text_count, coords=coords, w_qkv=w_qkv, w_out=w_out, w_in=w_in, w_down=w_down, rel_tables=rel_tables, ln_gains=ln_gains, biases=biases, b_in=b_in, cotangent=cotangent)


@jax.custom_vjp
def low(v):
    return lax.optimization_barrier(v.astype(jnp.bfloat16)).astype(jnp.float32)

@jax.custom_vjp
def low_back(v):
    return v

def low_keep(v):
    return (low(v), None)

def low_pass(kept, grad):
    return (grad,)

def back_keep(v):
    return (v, None)

def back_low(kept, grad):
    return (low(grad),)
low.defvjp(low_keep, low_pass)
low_back.defvjp(back_keep, back_low)
NORM_EPSILON = 1e-05
TOP_PRECISION = lax.Precision.HIGHEST

def norm_rows(values_in, scale_gain, offset):
    centered = values_in - lax.optimization_barrier(jnp.mean(values_in, axis=-1, keepdims=True))
    spread = lax.optimization_barrier(jnp.mean(centered * centered, axis=-1, keepdims=True))
    return centered * lax.rsqrt(spread + NORM_EPSILON) * scale_gain + offset

def bucket_ids(doc_coords):
    places = jnp.arange(SEQ, dtype=jnp.int32)
    half_range = BUCKETS // 2
    linear = jnp.clip(places[:, None] - places[None, :], -half_range, half_range - 1) + half_range
    across = jnp.clip(doc_coords[0][:, None] - doc_coords[0][None, :], -8, 7) + 8
    upward = jnp.clip(doc_coords[1][:, None] - doc_coords[1][None, :], -4, 3) + 4
    return (linear, across * 8 + upward)

def doc_layer(weights, rel_key, rel_query, rows_in, doc_count, doc_coords):
    w_qkv, w_out, w_in, w_down, gains, biases, b_in = weights
    rows_low = low(rows_in)
    projected = jnp.dot(rows_low, w_qkv, precision=TOP_PRECISION) + jnp.concatenate([biases[0], biases[1], biases[2]])
    query_heads = low(low_back(projected[:, :D])).reshape(SEQ, HEADS, HEAD_DIM)
    key_heads = low(low_back(projected[:, D:2 * D])).reshape(SEQ, HEADS, HEAD_DIM)
    value_heads = low(low_back(projected[:, 2 * D:])).reshape(SEQ, HEADS, HEAD_DIM)
    query_rel = low(low_back(jnp.einsum('ihe,tbhe->thib', query_heads, rel_key, precision=TOP_PRECISION)))
    key_rel = low(jnp.einsum('jhe,tbhe->thjb', key_heads, rel_query, precision=TOP_PRECISION))
    raw_scores = jnp.einsum('ihe,jhe->hij', query_heads, key_heads, precision=TOP_PRECISION)
    buckets = bucket_ids(doc_coords)
    for kind_index in range(2):
        index_map = buckets[kind_index]
        raw_scores = raw_scores + jnp.take_along_axis(query_rel[kind_index], jnp.broadcast_to(index_map[None], (HEADS, SEQ, SEQ)), axis=2)
        key_part = jnp.take_along_axis(key_rel[kind_index], jnp.broadcast_to(index_map.T[None], (HEADS, SEQ, SEQ)), axis=2)
        raw_scores = raw_scores + jnp.swapaxes(key_part, 1, 2)
    raw_scores = low_back(raw_scores)
    places = jnp.arange(SEQ, dtype=jnp.int32)
    key_valid = (places < doc_count) | (places >= TEXT) & (places < TEXT + PATCH)
    scaled = jnp.where(key_valid[None, None, :], raw_scores * (3.0 * HEAD_DIM) ** (-0.5), -jnp.inf)
    shifted = scaled - lax.optimization_barrier(jnp.max(scaled, axis=-1, keepdims=True))
    exponent = jnp.exp(shifted)
    soft_weights = low(exponent / lax.optimization_barrier(jnp.sum(exponent, axis=-1, keepdims=True)))
    mixed_rows = low(low_back(jnp.einsum('hij,jhe->ihe', soft_weights, value_heads, precision=TOP_PRECISION).reshape(SEQ, D)))
    attended = low_back(jnp.dot(mixed_rows, w_out, precision=TOP_PRECISION) + biases[3])
    first_norm = norm_rows(rows_in + attended, gains[0], biases[5])
    hidden_pre = low_back(jnp.dot(low(first_norm), w_in, precision=TOP_PRECISION) + b_in)
    active = low(jax.nn.gelu(hidden_pre, approximate=False))
    down_rows = low_back(jnp.dot(active, w_down, precision=TOP_PRECISION) + biases[4])
    return norm_rows(first_norm + down_rows, gains[1], biases[6])

def whole_layer(weights, tables, rows_all, counts, coords):
    w_qkv = weights[0]
    rel_key = low(jnp.einsum('tbd,de->tbe', tables, w_qkv[:, D:2 * D], precision=TOP_PRECISION)).reshape(2, BUCKETS, HEADS, HEAD_DIM)
    rel_query = low(jnp.einsum('tbd,de->tbe', tables, w_qkv[:, :D], precision=TOP_PRECISION)).reshape(2, BUCKETS, HEADS, HEAD_DIM)

    def one_doc(carried, doc_item):
        return (carried, doc_layer(weights, rel_key, rel_query, doc_item[0], doc_item[1], doc_item[2]))
    _, result = lax.scan(jax.checkpoint(one_doc), jnp.zeros((), jnp.float32), (rows_all, counts, coords))
    return result

def reference(layer_input, text_count, coords, w_qkv, w_out, w_in, w_down, rel_tables, ln_gains, biases, b_in, cotangent):
    floats = tuple((array.astype(jnp.float32) for array in (layer_input, w_qkv, w_out, w_in, w_down, rel_tables, ln_gains, biases, b_in)))

    def forward(rows_all, qkv_all, out_all, in_all, down_all, tables_all, gains_all, biases_all, b_in_all):
        outputs = []
        current = rows_all
        for layer_index in range(LAYERS):
            weights = (qkv_all[layer_index], out_all[layer_index], in_all[layer_index], down_all[layer_index], gains_all[layer_index], biases_all[layer_index], b_in_all[layer_index])
            current = whole_layer(weights, tables_all[layer_index], current, text_count, coords)
            outputs.append(current)
        return (outputs[0], outputs[-1])
    (first_out, second_out), pullback = jax.vjp(forward, *floats)
    gradients = pullback((jnp.zeros_like(first_out), cotangent.astype(jnp.float32)))
    return (first_out, second_out, gradients[0], gradients[1], gradients[2], gradients[3], gradients[4], gradients[5], gradients[6], gradients[7], gradients[8])
```

```python
import functools

import jax
import jax.numpy as jnp
from jax import lax
from jax.experimental import pallas as pl
from jax.experimental.pallas import tpu as pltpu
from jax.sharding import PartitionSpec as P

HEADS = 16
HEAD_DIM = 64
BUCKETS = 128
TEXT = 512
PATCH = 49
GRID_SIDE = 32
CELLS = GRID_SIDE * GRID_SIDE
LANES = 128
PAIR = 2 * HEAD_DIM
NORM_EPSILON = 1e-05
SCORE_SCALE = (3.0 * HEAD_DIM) ** (-0.5)
MASKED = -1e30
BF16 = jnp.bfloat16
F32 = jnp.float32
BOTH = ("doc", "ctx")


def pad_lanes(count):
    return -(-count // LANES) * LANES


def norm_rows(values_in, scale_gain, offset):
    centered = values_in - jnp.mean(values_in, axis=-1, keepdims=True)
    spread = jnp.mean(centered * centered, axis=-1, keepdims=True)
    return centered * lax.rsqrt(spread + NORM_EPSILON) * scale_gain + offset


def exact_gelu(values_in):
    return jax.nn.gelu(values_in, approximate=False)


def dot(left, right, left_axis, right_axis):
    return lax.dot_general(
        left, right, (((left_axis,), (right_axis,)), ((), ())), preferred_element_type=F32
    )


def lookup(table, index):
    return jnp.take_along_axis(table, index, axis=1, mode="promise_in_bounds")


def head_lanes(head, rows):
    lane = lax.broadcasted_iota(jnp.int32, (rows, PAIR), 1)
    return (lane >= head * HEAD_DIM) & (lane < (head + 1) * HEAD_DIM)


def keep_head(values, head):
    return jnp.where(head_lanes(head, values.shape[0]), values, jnp.zeros_like(values))


def attend_kernel(
    chunks,
    q_ref,
    *refs,
):
    k_refs = refs[:chunks]
    v_refs = refs[chunks : 2 * chunks]
    (
        rel_key_ref,
        rel_query_ref,
        index_linear_ref,
        index_planar_ref,
        turned_linear_ref,
        turned_planar_ref,
        mask_ref,
        mixed_ref,
        prob_ref,
        left_scr,
        right_scr,
        value_scr,
        score_scr,
    ) = refs[2 * chunks :]
    rows = q_ref.shape[0]
    keys = rows * chunks
    keys_wide = score_scr.shape[1]
    rows_wide = left_scr.shape[1] - PAIR

    @pl.when(pl.program_id(0) == 0)
    def _():
        row_at = lax.broadcasted_iota(jnp.int32, (rows, rows_wide), 0)
        lane_at = lax.broadcasted_iota(jnp.int32, (rows, rows_wide), 1)
        left_scr[:, PAIR:] = jnp.where(row_at == lane_at, 1.0, 0.0).astype(BF16)
        right_scr[keys:, :] = jnp.zeros((keys_wide - keys, PAIR + rows_wide), BF16)
        value_scr[keys:, :] = jnp.zeros((keys_wide - keys, PAIR), BF16)

    for chunk in range(chunks):
        right_scr[chunk * rows : (chunk + 1) * rows, :PAIR] = k_refs[chunk][...]
        value_scr[chunk * rows : (chunk + 1) * rows, :] = v_refs[chunk][...]

    for head in range(2):
        left_scr[:, :PAIR] = keep_head(q_ref[...], head)
        rel_query = [keep_head(rel_query_ref[kind], head) for kind in range(2)]
        rel_key = [keep_head(rel_key_ref[kind], head) for kind in range(2)]

        key_step = 48

        def key_block(block, carry):
            at = pl.multiple_of(block * key_step, key_step)
            key_rows = right_scr[pl.ds(at, key_step), :PAIR]
            first = dot(key_rows, rel_query[0], 1, 1).astype(BF16).astype(F32)
            second = dot(key_rows, rel_query[1], 1, 1).astype(BF16).astype(F32)
            biased = lookup(first, turned_linear_ref[pl.ds(at, key_step), :]) + lookup(
                second, turned_planar_ref[pl.ds(at, key_step), :]
            )
            right_scr[pl.ds(at, key_step), PAIR:] = biased.astype(BF16)
            return carry

        lax.fori_loop(0, keys // key_step, key_block, 0)
        score_scr[...] = dot(left_scr[...], right_scr[...], 1, 1)

        row_step = 48

        def row_block(block, carry):
            at = pl.multiple_of(block * row_step, row_step)
            query_rows = left_scr[pl.ds(at, row_step), :PAIR]
            first = dot(query_rows, rel_key[0], 1, 1).astype(BF16).astype(F32)
            second = dot(query_rows, rel_key[1], 1, 1).astype(BF16).astype(F32)
            raw = score_scr[pl.ds(at, row_step), :]
            raw = raw + lookup(first, index_linear_ref[pl.ds(at, row_step), :])
            raw = raw + lookup(second, index_planar_ref[pl.ds(at, row_step), :])
            scaled = raw * SCORE_SCALE + mask_ref[...]
            shifted = scaled - jnp.max(scaled, axis=-1, keepdims=True)
            exponent = jnp.exp(shifted)
            inverse = 1.0 / jnp.sum(exponent, axis=-1, keepdims=True)
            prob_ref[head, pl.ds(at, row_step), :] = (exponent * inverse).astype(BF16)
            return carry

        lax.fori_loop(0, rows // row_step, row_block, 0)
        mixed = dot(prob_ref[head], value_scr[...], 1, 0)
        if head == 0:
            mixed_ref[...] = mixed.astype(BF16)
        else:
            mixed_ref[...] = jnp.where(head_lanes(1, rows), mixed, mixed_ref[...].astype(F32)).astype(BF16)


def whole_spec(array):
    return pl.BlockSpec(array.shape, lambda step: (0,) * array.ndim)


def attend(qkv, other_kv, rel_key, rel_query, lookups):
    rows = qkv.shape[0]
    width = qkv.shape[1] // 3
    pairs = width // PAIR
    chunks = 1 + len(other_kv)
    keys_wide = pad_lanes(rows * chunks)
    rows_wide = pad_lanes(rows)

    def column(offset):
        return pl.BlockSpec((rows, PAIR), lambda step: (0, offset + step))

    rel_spec = pl.BlockSpec((2, BUCKETS, PAIR), lambda step: (0, 0, step))
    small = (
        lookups["index_linear"],
        lookups["index_planar"],
        lookups["turned_linear"],
        lookups["turned_planar"],
        lookups["mask"],
    )
    return pl.pallas_call(
        functools.partial(attend_kernel, chunks),
        grid=(pairs,),
        in_specs=[column(0), column(pairs)]
        + [column(0)] * (chunks - 1)
        + [column(2 * pairs)]
        + [column(pairs)] * (chunks - 1)
        + [rel_spec, rel_spec]
        + [whole_spec(item) for item in small],
        out_specs=[
            pl.BlockSpec((rows, PAIR), lambda step: (0, step)),
            pl.BlockSpec((2, rows, keys_wide), lambda step: (step, 0, 0)),
        ],
        out_shape=[
            jax.ShapeDtypeStruct((rows, width), BF16),
            jax.ShapeDtypeStruct((2 * pairs, rows, keys_wide), BF16),
        ],
        scratch_shapes=[
            pltpu.VMEM((rows, PAIR + rows_wide), BF16),
            pltpu.VMEM((keys_wide, PAIR + rows_wide), BF16),
            pltpu.VMEM((keys_wide, PAIR), BF16),
            pltpu.VMEM((rows, keys_wide), F32),
        ],
        compiler_params=pltpu.CompilerParams(vmem_limit_bytes=40 << 20),
        cost_estimate=pl.CostEstimate(
            flops=20 * rows * rows * chunks * width,
            bytes_accessed=4 * pairs * rows * keys_wide + 8 * rows * width,
            transcendentals=2 * pairs * rows * keys_wide,
        ),
        name="attend",
    )(qkv, qkv, *other_kv, qkv, *other_kv, rel_key, rel_query, *small)


def bucket_sums(cells, pos, sums_out):
    spot = pos & (LANES - 1)
    part = pos >> 7
    total = jnp.zeros(spot.shape, F32)
    for chunk in range(CELLS // LANES):
        total = jnp.where(
            part == chunk, lookup(cells[:, chunk * LANES : (chunk + 1) * LANES], spot), total
        )
    lane = lax.broadcasted_iota(jnp.int32, total.shape, 1)
    total = total - jnp.where(lane < BUCKETS - 8, pltpu.roll(total, BUCKETS - 8, 1), 0.0)
    return total - jnp.where((lane & 7) < 7, pltpu.roll(total, BUCKETS - 1, 1), 0.0)


def band_sums(values, index, pos):
    spot = pos & (LANES - 1)
    part = pos >> 7
    total = jnp.zeros(spot.shape, F32)
    for chunk in range(values.shape[1] // LANES):
        total = jnp.where(
            part == chunk, lookup(values[:, chunk * LANES : (chunk + 1) * LANES], spot), total
        )
    low = jnp.sum(jnp.where(index == 0, values, 0.0), axis=-1, keepdims=True)
    high = jnp.sum(jnp.where(index == BUCKETS - 1, values, 0.0), axis=-1, keepdims=True)
    lane = lax.broadcasted_iota(jnp.int32, total.shape, 1)
    return jnp.where(lane == 0, low, jnp.where(lane == BUCKETS - 1, high, total))


def attend_back_kernel(
    chunks,
    q_ref,
    *refs,
):
    k_refs = refs[:chunks]
    v_refs = refs[chunks : 2 * chunks]
    (
        grad_ref,
        prob_ref,
        rel_key_ref,
        rel_query_ref,
        index_linear_ref,
        turned_linear_ref,
        key_cells_ref,
        row_cells_ref,
        planar_pos_ref,
        linear_pos_ref,
        turned_planar_pos_ref,
        turned_linear_pos_ref,
        grad_query_ref,
        grad_key_ref,
        grad_value_ref,
        grad_rel_key_ref,
        grad_rel_query_ref,
        key_scr,
        value_scr,
        raw_scr,
        low_scr,
        turned_scr,
        cell_scr,
        row_bucket_scr,
        key_bucket_scr,
    ) = refs[2 * chunks :]
    rows = q_ref.shape[0]
    keys = rows * chunks
    keys_wide = key_scr.shape[0]
    rows_wide = raw_scr.shape[0]

    @pl.when(pl.program_id(0) == 0)
    def _():
        key_scr[keys:, :] = jnp.zeros((keys_wide - keys, PAIR), BF16)
        value_scr[keys:, :] = jnp.zeros((keys_wide - keys, PAIR), BF16)
        raw_scr[rows:, :] = jnp.zeros((rows_wide - rows, keys_wide), F32)

    for chunk in range(chunks):
        key_scr[chunk * rows : (chunk + 1) * rows, :] = k_refs[chunk][...]
        value_scr[chunk * rows : (chunk + 1) * rows, :] = v_refs[chunk][...]

    for head in range(2):
        query = keep_head(q_ref[...], head)
        grad = keep_head(grad_ref[...], head)
        raw_scr[:rows, :] = dot(grad, value_scr[...], 1, 1)
        row_step = 48

        def row_block(block, carry):
            at = pl.multiple_of(block * row_step, row_step)
            prob = prob_ref[head, pl.ds(at, row_step), :].astype(F32)
            grad_prob = raw_scr[pl.ds(at, row_step), :]
            inner = jnp.sum(prob * grad_prob, axis=-1, keepdims=True)
            grad_raw = (prob * (grad_prob - inner) * SCORE_SCALE).astype(BF16)
            low_scr[pl.ds(at, row_step), :] = grad_raw
            raw_scr[pl.ds(at, row_step), :] = grad_raw.astype(F32)
            return carry

        lax.fori_loop(0, rows // row_step, row_block, 0)

        cell_scr[:rows, :] = dot(low_scr[...], key_cells_ref[...], 1, 0)
        step = 16

        def query_block(block, carry):
            at = pl.multiple_of(block * step, step)
            planar = bucket_sums(
                cell_scr[pl.ds(at, step), :], planar_pos_ref[pl.ds(at, step), :], None
            )
            linear = band_sums(
                raw_scr[pl.ds(at, step), :],
                index_linear_ref[pl.ds(at, step), :],
                linear_pos_ref[pl.ds(at, step), :],
            )
            row_bucket_scr[pl.ds(at, step), :BUCKETS] = linear.astype(BF16)
            row_bucket_scr[pl.ds(at, step), BUCKETS:] = planar.astype(BF16)
            return carry

        lax.fori_loop(0, rows // step, query_block, 0)
        row_bucket = row_bucket_scr[...]
        rel_key = keep_head(rel_key_ref[...].reshape(2 * BUCKETS, PAIR), head)
        rel_query = keep_head(rel_query_ref[...].reshape(2 * BUCKETS, PAIR), head)
        grad_query = dot(low_scr[...], key_scr[...], 1, 0) + dot(row_bucket, rel_key, 1, 0)
        grad_rel_key = dot(row_bucket, query, 0, 0)

        turned_scr[...] = raw_scr[...].T[:keys]
        turned_low = turned_scr[...].astype(BF16)
        cell_scr[...] = dot(turned_low, row_cells_ref[...], 1, 0)

        def key_block(block, carry):
            at = pl.multiple_of(block * step, step)
            planar = bucket_sums(
                cell_scr[pl.ds(at, step), :], turned_planar_pos_ref[pl.ds(at, step), :], None
            )
            linear = band_sums(
                turned_scr[pl.ds(at, step), :],
                turned_linear_ref[pl.ds(at, step), :],
                turned_linear_pos_ref[pl.ds(at, step), :],
            )
            key_bucket_scr[pl.ds(at, step), :BUCKETS] = linear.astype(BF16)
            key_bucket_scr[pl.ds(at, step), BUCKETS:] = planar.astype(BF16)
            return carry

        lax.fori_loop(0, keys // step, key_block, 0)
        key_bucket = key_bucket_scr[...]
        grad_key = dot(turned_low[:, :rows], query, 1, 0) + dot(key_bucket, rel_query, 1, 0)
        grad_value = dot(prob_ref[head], grad, 0, 0)[:keys]
        grad_rel_query = dot(key_bucket, key_scr[:keys, :], 0, 0)
        results = (
            (grad_query_ref, grad_query),
            (grad_key_ref, grad_key),
            (grad_value_ref, grad_value),
            (grad_rel_key_ref, grad_rel_key.reshape(2, BUCKETS, PAIR)),
            (grad_rel_query_ref, grad_rel_query.reshape(2, BUCKETS, PAIR)),
        )
        for target, found in results:
            if head == 0:
                target[...] = found
            else:
                lane = lax.broadcasted_iota(jnp.int32, found.shape, found.ndim - 1)
                target[...] = jnp.where(lane >= HEAD_DIM, found, target[...])


def attend_back(qkv, other_kv, grad_mixed, prob, rel_key, rel_query, lookups):
    rows = qkv.shape[0]
    width = qkv.shape[1] // 3
    pairs = width // PAIR
    chunks = 1 + len(other_kv)
    keys = rows * chunks
    keys_wide = pad_lanes(keys)
    rows_wide = pad_lanes(rows)

    def column(offset):
        return pl.BlockSpec((rows, PAIR), lambda step: (0, offset + step))

    rel_spec = pl.BlockSpec((2, BUCKETS, PAIR), lambda step: (0, 0, step))
    key_spec = pl.BlockSpec((keys, PAIR), lambda step: (0, step))
    small = (
        lookups["index_linear"],
        lookups["turned_linear"],
        lookups["key_cells"],
        lookups["row_cells"],
        lookups["planar_pos"],
        lookups["linear_pos"],
        lookups["turned_planar_pos"],
        lookups["turned_linear_pos"],
    )
    return pl.pallas_call(
        functools.partial(attend_back_kernel, chunks),
        grid=(pairs,),
        in_specs=[column(0), column(pairs)]
        + [column(0)] * (chunks - 1)
        + [column(2 * pairs)]
        + [column(pairs)] * (chunks - 1)
        + [
            column(0),
            pl.BlockSpec((2, rows, keys_wide), lambda step: (step, 0, 0)),
            rel_spec,
            rel_spec,
        ]
        + [whole_spec(item) for item in small],
        out_specs=[column(0), key_spec, key_spec, rel_spec, rel_spec],
        out_shape=[
            jax.ShapeDtypeStruct((rows, width), F32),
            jax.ShapeDtypeStruct((keys, width), F32),
            jax.ShapeDtypeStruct((keys, width), F32),
            jax.ShapeDtypeStruct((2, BUCKETS, width), F32),
            jax.ShapeDtypeStruct((2, BUCKETS, width), F32),
        ],
        scratch_shapes=[
            pltpu.VMEM((keys_wide, PAIR), BF16),
            pltpu.VMEM((keys_wide, PAIR), BF16),
            pltpu.VMEM((rows_wide, keys_wide), F32),
            pltpu.VMEM((rows, keys_wide), BF16),
            pltpu.VMEM((keys, rows_wide), F32),
            pltpu.VMEM((keys, CELLS), F32),
            pltpu.VMEM((rows, 2 * BUCKETS), BF16),
            pltpu.VMEM((keys, 2 * BUCKETS), BF16),
        ],
        compiler_params=pltpu.CompilerParams(vmem_limit_bytes=56 << 20),
        cost_estimate=pl.CostEstimate(
            flops=80 * rows * rows * chunks * width,
            bytes_accessed=4 * pairs * rows * keys_wide + 24 * rows * width,
            transcendentals=0,
        ),
        name="attend_back",
    )(qkv, qkv, *other_kv, qkv, *other_kv, grad_mixed, prob, rel_key, rel_query, *small)


def make_lookups(cells_x, cells_y, count, place, row_count):
    seq_len = place.shape[0]
    keys_wide = pad_lanes(seq_len)
    rows_wide = pad_lanes(row_count)
    half_range = BUCKETS // 2

    def wide(values, total):
        return jnp.pad(values, ((0, total - values.shape[0]),))

    key_place, key_x, key_y = (wide(item, keys_wide) for item in (place, cells_x, cells_y))
    row_place, row_x, row_y = (item[:row_count] for item in (place, cells_x, cells_y))
    wide_place, wide_x, wide_y = (wide(item, rows_wide) for item in (row_place, row_x, row_y))

    def linear(i, j):
        return jnp.clip(i - j, -half_range, half_range - 1) + half_range

    def planar(ix, iy, jx, jy):
        return (jnp.clip(ix - jx, -8, 7) + 8) * 8 + jnp.clip(iy - jy, -4, 3) + 4

    out = {}
    out["index_linear"] = linear(row_place[:, None], key_place[None, :])
    out["index_planar"] = planar(row_x[:, None], row_y[:, None], key_x[None, :], key_y[None, :])
    out["turned_linear"] = linear(wide_place[None, :], place[:, None])
    out["turned_planar"] = planar(
        wide_x[None, :], wide_y[None, :], cells_x[:, None], cells_y[:, None]
    )
    valid = (place < count) | ((place >= TEXT) & (place < TEXT + PATCH))
    out["mask"] = jnp.pad(
        jnp.where(valid, 0.0, MASKED).astype(F32),
        ((0, keys_wide - seq_len),),
        constant_values=MASKED,
    )[None]
    key_live = jnp.arange(keys_wide) < seq_len
    row_live = jnp.arange(rows_wide) < row_count
    cell = jnp.arange(CELLS, dtype=jnp.int32)
    cell_x, cell_y = cell // GRID_SIDE, cell % GRID_SIDE
    out["key_cells"] = (
        key_live[:, None] & (key_x[:, None] <= cell_x) & (key_y[:, None] <= cell_y)
    ).astype(BF16)
    out["row_cells"] = (
        row_live[:, None] & (wide_x[:, None] >= cell_x) & (wide_y[:, None] >= cell_y)
    ).astype(BF16)
    bucket = jnp.arange(BUCKETS, dtype=jnp.int32)
    bucket_x, bucket_y = bucket // 8, bucket % 8
    top = GRID_SIDE - 1
    to_x = jnp.where(bucket_x == 0, top, jnp.minimum(row_x[:, None] - bucket_x + 8, top))
    to_y = jnp.where(bucket_y == 0, top, jnp.minimum(row_y[:, None] - bucket_y + 4, top))
    out["planar_pos"] = jnp.where((to_x >= 0) & (to_y >= 0), to_x * GRID_SIDE + to_y, -1)
    from_x = jnp.where(bucket_x == 0, 0, jnp.maximum(cells_x[:, None] + bucket_x - 8, 0))
    from_y = jnp.where(bucket_y == 0, 0, jnp.maximum(cells_y[:, None] + bucket_y - 4, 0))
    out["turned_planar_pos"] = jnp.where(
        (from_x <= top) & (from_y <= top), from_x * GRID_SIDE + from_y, -1
    )
    first_place = place[0]
    target = row_place[:, None] - bucket + half_range
    out["linear_pos"] = jnp.where(
        (target >= 0) & (target < seq_len), (target - first_place) % seq_len, -1
    )
    source = place[:, None] + bucket - half_range - first_place
    out["turned_linear_pos"] = jnp.where((source >= 0) & (source < row_count), source, -1)
    return out


class Home:
    def __init__(self, mesh_shape, local_docs, block_rows):
        self.doc_size = mesh_shape["doc"]
        self.ctx_size = mesh_shape["ctx"]
        self.block = block_rows
        self.docs = 2 * local_docs
        self.span = self.ctx_size // self.docs
        self.group = 2 * self.span
        self.rows = 2 * block_rows
        self.seq = block_rows * self.ctx_size

    def flat(self, doc, ctx):
        return doc * self.ctx_size + ctx

    def move_pairs(self, turn):
        pairs = []
        for pair in range(self.doc_size // 2):
            for core in range(2):
                for block in range(self.ctx_size):
                    slot = (block + turn) % 2
                    doc = 2 * core + slot
                    place = block // 2
                    target = self.flat(
                        2 * pair + place // self.span, doc * self.span + place % self.span
                    )
                    pairs.append((self.flat(2 * pair + core, block), target))
        return pairs

    def to_home(self, local):
        ctx = lax.axis_index("ctx")
        doc_here = ctx // self.span
        pieces = []
        for turn in range(2):
            piece = lax.dynamic_index_in_dim(local, (ctx + turn) % 2, 0, keepdims=False)
            pieces.append(lax.ppermute(piece, BOTH, self.move_pairs(turn)))
        swap = (doc_here % 2) == 1
        low_half = jnp.where(swap, pieces[1], pieces[0])
        high_half = jnp.where(swap, pieces[0], pieces[1])
        return jnp.concatenate([low_half, high_half], axis=0)

    def from_home(self, rows):
        ctx = lax.axis_index("ctx")
        doc_here = ctx // self.span
        halves = rows.reshape(2, self.block, rows.shape[1])
        pieces = []
        for turn in range(2):
            piece = lax.dynamic_index_in_dim(halves, (doc_here + turn) % 2, 0, keepdims=False)
            back = [(target, source) for source, target in self.move_pairs(turn)]
            pieces.append(lax.ppermute(piece, BOTH, back))
        swap = (ctx % 2) == 1
        first = jnp.where(swap, pieces[1], pieces[0])
        second = jnp.where(swap, pieces[0], pieces[1])
        return jnp.stack([first, second])

    def position(self):
        core = lax.axis_index("doc") % 2
        return core * self.span + lax.axis_index("ctx") % self.span

    def ring_pairs(self, shift):
        pairs = []
        for doc in range(self.doc_size):
            for ctx in range(self.ctx_size):
                place = (doc % 2) * self.span + ctx % self.span
                other = (place + shift) % self.group
                pairs.append(
                    (
                        self.flat(doc, ctx),
                        self.flat(
                            doc - doc % 2 + other // self.span,
                            ctx - ctx % self.span + other % self.span,
                        ),
                    )
                )
        return pairs

    def fetch(self, values):
        return [
            lax.ppermute(values, BOTH, self.ring_pairs(-shift)) for shift in range(1, self.group)
        ]

    def give_back(self, pieces):
        return [
            lax.ppermute(piece, BOTH, self.ring_pairs(shift))
            for shift, piece in enumerate(pieces, 1)
        ]


def pack_layer(w_qkv, w_out, w_in, w_down, tables, gains, biases, b_in):
    shard = w_qkv.shape[0]
    down = w_down.reshape(-1, shard, w_down.shape[1])
    down = jnp.concatenate([down[part] for part in range(down.shape[0])], axis=1)
    small = jnp.concatenate(
        [tables.reshape(-1, shard).T, gains.T, biases.T, b_in.reshape(shard, -1)], axis=1
    )
    small = jnp.pad(small, ((0, 0), (0, pad_lanes(small.shape[1]) - small.shape[1])))
    return jnp.concatenate([w_qkv, w_out, w_in, down, small], axis=1)


def unpack_layer(packed, device_count):
    width = packed.shape[0]
    shard = width // device_count
    qkv = packed[:, : 3 * width]
    out = packed[:, 3 * width : 4 * width]
    rest = packed.shape[1] - 4 * width
    hidden = (rest // (2 * width)) * width
    w_in = packed[:, 4 * width : 4 * width + hidden]
    down = packed[:, 4 * width + hidden : 4 * width + 2 * hidden]
    down = (
        down.reshape(device_count, shard, hidden // width, width)
        .transpose(0, 2, 1, 3)
        .reshape(hidden, width)
    )
    small = packed[:, 4 * width + 2 * hidden :]
    table_cols = 2 * BUCKETS
    tables = small[:, :table_cols]
    gains = small[:, table_cols : table_cols + 2].T.astype(F32)
    biases = small[:, table_cols + 2 : table_cols + 9].T.astype(F32)
    b_in = small[:, table_cols + 9 : table_cols + 9 + hidden // width].astype(F32).reshape(hidden)
    return dict(
        qkv=qkv, out=out, w_in=w_in, down=down, tables=tables, gains=gains, biases=biases, b_in=b_in
    )


def doc_flip(doc_size, bit):
    return [(index, index ^ bit) for index in range(doc_size)]


def halve(values, axis, mine, send):
    kept = lax.dynamic_index_in_dim(values, mine, axis, keepdims=False)
    sent = lax.dynamic_index_in_dim(values, 1 - mine, axis, keepdims=False)
    return kept, send(sent.astype(BF16))


def scatter_sum(parts, doc_size, ctx_size):
    doc = lax.axis_index("doc")
    ctx = lax.axis_index("ctx")

    def doc_step(values, axis, bit):
        def send(half):
            return lax.ppermute(half, "doc", doc_flip(doc_size, bit))

        kept, got = halve(values, axis, (doc // bit) % 2, send)
        return (kept.astype(F32) + got.astype(F32)).astype(BF16)

    def ctx_step(values, axis, bit):
        def send(half):
            return lax.ppermute(half, "ctx", doc_flip(ctx_size, bit))

        kept, got = halve(values, axis, (ctx // bit) % 2, send)
        return kept.astype(F32) + got.astype(F32)

    high_bits = []
    bit = 2
    while bit < doc_size:
        high_bits.append(bit)
        bit *= 2
    results = []
    for part in parts:
        rows, columns = part.shape
        block = rows // (doc_size * ctx_size)
        values = part.reshape(doc_size // 2, 2, ctx_size * block, columns)
        values = doc_step(values, 1, 1)
        colored = []
        half_columns = columns // 2
        for color in range(2):
            piece = values[:, :, color * half_columns : (color + 1) * half_columns]
            order = list(reversed(high_bits)) if color == 0 else list(high_bits)
            left = sorted(high_bits, reverse=True)
            piece = piece.reshape((2,) * len(high_bits) + piece.shape[1:])
            for bit in order:
                axis = left.index(bit)
                piece = doc_step(piece, axis, bit)
                left.remove(bit)
            colored.append(piece)
        values = jnp.concatenate(colored, axis=1).reshape(ctx_size, block, columns)
        size = ctx_size
        while size > 1:
            values = values.reshape(2, size // 2, block, columns)
            values = ctx_step(values, 0, size // 2)
            size //= 2
        results.append(values.reshape(block, columns).astype(F32))
    return results


def layer_forward(home, rows_in, rows_low, weights, lookups):
    width = rows_in.shape[1]
    gains, biases = weights["gains"], weights["biases"]
    qkv = (dot(rows_low, weights["qkv"], 1, 0) + biases[:3].reshape(1, -1)).astype(BF16)
    other_kv = home.fetch(qkv[:, width:])
    tables = weights["tables"]
    rel_both = dot(tables, weights["qkv"][:, : 2 * width], 0, 0).astype(BF16)
    rel_query = rel_both[:, :width].reshape(2, BUCKETS, width)
    rel_key = rel_both[:, width:].reshape(2, BUCKETS, width)
    mixed, prob = attend(qkv, other_kv, rel_key, rel_query, lookups)
    first_sum = rows_in + (dot(mixed, weights["out"], 1, 0) + biases[3])
    first_norm = norm_rows(first_sum, gains[0], biases[5])
    norm_low = first_norm.astype(BF16)
    hidden_pre = dot(norm_low, weights["w_in"], 1, 0) + weights["b_in"]
    active = exact_gelu(hidden_pre).astype(BF16)
    second_sum = first_norm + (dot(active, weights["down"], 1, 0) + biases[4])
    result = norm_rows(second_sum, gains[1], biases[6])
    kept = dict(
        rows_low=rows_low,
        qkv=qkv,
        other_kv=other_kv,
        rel_key=rel_key,
        rel_query=rel_query,
        prob=prob,
        mixed=mixed,
        first_sum=first_sum,
        norm_low=norm_low,
        hidden_pre=hidden_pre,
        active=active,
        second_sum=second_sum,
    )
    return result, kept


def layer_backward(home, grad_out, kept, weights, lookups):
    width = grad_out.shape[1]
    gains, biases = weights["gains"], weights["biases"]
    _, second_pull = jax.vjp(norm_rows, kept["second_sum"], gains[1], biases[6])
    grad_second, grad_gain_two, grad_offset_two = second_pull(grad_out)
    grad_down = grad_second.astype(BF16)
    grad_w_down = dot(kept["active"], grad_down, 0, 0)
    grad_b_down = jnp.sum(grad_down.astype(F32), axis=0)
    grad_active = dot(grad_down, weights["down"], 1, 1)
    _, gelu_pull = jax.vjp(exact_gelu, kept["hidden_pre"])
    grad_hidden = gelu_pull(grad_active)[0].astype(BF16)
    grad_w_in = dot(kept["norm_low"], grad_hidden, 0, 0)
    grad_b_in = jnp.sum(grad_hidden.astype(F32), axis=0)
    grad_first_norm = grad_second + dot(grad_hidden, weights["w_in"], 1, 1)
    _, first_pull = jax.vjp(norm_rows, kept["first_sum"], gains[0], biases[5])
    grad_first, grad_gain_one, grad_offset_one = first_pull(grad_first_norm)
    grad_att = grad_first.astype(BF16)
    grad_w_out = dot(kept["mixed"], grad_att, 0, 0)
    grad_b_out = jnp.sum(grad_att.astype(F32), axis=0)
    grad_mixed = dot(grad_att, weights["out"], 1, 1).astype(BF16)
    grad_query, grad_key, grad_value, grad_rel_key, grad_rel_query = attend_back(
        kept["qkv"],
        kept["other_kv"],
        grad_mixed,
        kept["prob"],
        kept["rel_key"],
        kept["rel_query"],
        lookups,
    )
    rows = grad_out.shape[0]
    grad_kv = jnp.concatenate([grad_key, grad_value], axis=1)
    sent = [
        grad_kv[chunk * rows : (chunk + 1) * rows].astype(BF16)
        for chunk in range(1, grad_kv.shape[0] // rows)
    ]
    grad_own = grad_kv[:rows]
    for piece in home.give_back(sent):
        grad_own = grad_own + piece.astype(F32)
    grad_qkv = jnp.concatenate([grad_query, grad_own], axis=1).astype(BF16)
    tables = weights["tables"]
    rel_both = jnp.concatenate(
        [
            grad_rel_query.reshape(2 * BUCKETS, width),
            grad_rel_key.reshape(2 * BUCKETS, width),
        ],
        axis=1,
    ).astype(BF16)
    grad_tables = dot(weights["qkv"][:, :width], rel_both[:, :width], 1, 1) + dot(
        weights["qkv"][:, width : 2 * width], rel_both[:, width:], 1, 1
    )
    grad_w_qk = dot(kept["rows_low"], grad_qkv[:, : 2 * width], 0, 0) + dot(tables, rel_both, 1, 0)
    grad_w_v = dot(kept["rows_low"], grad_qkv[:, 2 * width :], 0, 0)
    grad_w_qkv = jnp.concatenate([grad_w_qk, grad_w_v], axis=1)
    bias_sums = jnp.sum(grad_qkv.astype(F32), axis=0).reshape(3, width)
    grad_rows = grad_first + dot(grad_qkv, weights["qkv"], 1, 1)
    small = jnp.concatenate(
        [
            grad_tables,
            grad_gain_one[:, None],
            grad_gain_two[:, None],
            bias_sums.T,
            grad_b_out[:, None],
            grad_b_down[:, None],
            grad_offset_one[:, None],
            grad_offset_two[:, None],
            grad_b_in.reshape(width, -1),
        ],
        axis=1,
    )
    small = jnp.pad(small, ((0, 0), (0, 2 * LANES * (-(-small.shape[1] // (2 * LANES))) - small.shape[1])))
    return grad_rows, (grad_w_down, grad_w_in, grad_w_out, grad_w_qkv, small)


def unpack_small(small, shard, hidden_shard):
    tables = small[:, : 2 * BUCKETS].T.reshape(2, BUCKETS, shard)
    gains = small[:, 2 * BUCKETS : 2 * BUCKETS + 2].T
    biases = small[:, 2 * BUCKETS + 2 : 2 * BUCKETS + 9].T
    b_in = small[:, 2 * BUCKETS + 9 : 2 * BUCKETS + 9 + hidden_shard // shard].reshape(hidden_shard)
    return tables, gains, biases, b_in


def body(
    mesh_shape,
    layer_input,
    text_count,
    coords,
    w_qkv,
    w_out,
    w_in,
    w_down,
    rel_tables,
    ln_gains,
    biases,
    b_in,
    cotangent,
):
    doc_size, ctx_size = mesh_shape["doc"], mesh_shape["ctx"]
    device_count = doc_size * ctx_size
    local_docs, block_rows, width = layer_input.shape
    layer_count = w_qkv.shape[0]
    home = Home(mesh_shape, local_docs, block_rows)

    packed = [
        pack_layer(
            w_qkv[layer],
            w_out[layer],
            w_in[layer],
            w_down[layer],
            rel_tables[layer],
            ln_gains[layer],
            biases[layer],
            b_in[layer],
        )
        for layer in range(layer_count)
    ]

    core = lax.axis_index("doc") % 2
    doc_here = lax.axis_index("ctx") // home.span
    swap = doc_flip(doc_size, 1)
    facts = jnp.concatenate(
        [coords.reshape(local_docs, -1), text_count[:, None]], axis=1
    )
    other_facts = lax.ppermute(facts, "doc", swap)
    mine = jnp.where(
        doc_here // local_docs == core,
        lax.dynamic_index_in_dim(facts, doc_here % local_docs, 0, keepdims=False),
        lax.dynamic_index_in_dim(other_facts, doc_here % local_docs, 0, keepdims=False),
    )
    place = (jnp.arange(home.seq, dtype=jnp.int32) + home.position() * home.rows) % home.seq

    def turned(values):
        twice = jnp.concatenate([values, values])
        return lax.dynamic_slice_in_dim(twice, home.position() * home.rows, home.seq)

    lookups = make_lookups(
        turned(mine[: home.seq]),
        turned(mine[home.seq : 2 * home.seq]),
        mine[2 * home.seq],
        place,
        home.rows,
    )

    rows_low = home.to_home(layer_input)
    current = rows_low.astype(F32)
    all_weights = []
    kept_all = []
    outputs = []
    gathered = None
    for layer in range(layer_count):
        shard = packed[layer]
        if gathered is not None:
            shard, gathered = lax.optimization_barrier((shard, gathered))
            all_weights[-1] = unpack_layer(gathered, device_count)
        gathered = lax.all_gather(shard, BOTH, axis=0, tiled=True)
        all_weights.append(unpack_layer(gathered, device_count))
    for layer in range(layer_count):
        current, kept = layer_forward(home, current, rows_low, all_weights[layer], lookups)
        rows_low = current.astype(BF16)
        outputs.append(home.from_home(rows_low).astype(F32))
        kept_all.append(kept)
    grad_rows = home.to_home(cotangent).astype(F32)
    totals = [None] * layer_count
    for layer in reversed(range(layer_count)):
        grad_rows, parts = layer_backward(
            home, grad_rows, kept_all[layer], all_weights[layer], lookups
        )
        totals[layer] = scatter_sum(parts, doc_size, ctx_size)
    grad_input = home.from_home(grad_rows.astype(BF16)).astype(F32)
    shard_rows = w_qkv.shape[1]
    smalls = [unpack_small(totals[layer][4], shard_rows, b_in.shape[1]) for layer in range(layer_count)]

    def stack(member):
        return jnp.stack([totals[layer][member] for layer in range(layer_count)])

    def stack_small(member):
        return jnp.stack([smalls[layer][member] for layer in range(layer_count)])

    return (
        outputs[0],
        outputs[-1],
        grad_input,
        stack(3),
        stack(2),
        stack(1),
        stack(0),
        stack_small(0),
        stack_small(1),
        stack_small(2),
        stack_small(3),
    )


def solution(mesh):
    placed = (
        P("doc", "ctx", None),
        P("doc"),
        P("doc", None, None),
        P(None, BOTH, None),
        P(None, BOTH, None),
        P(None, BOTH, None),
        P(None, BOTH, None),
        P(None, None, None, BOTH),
        P(None, None, BOTH),
        P(None, None, BOTH),
        P(None, BOTH),
        P("doc", "ctx", None),
    )
    return jax.shard_map(
        functools.partial(body, dict(mesh.shape)),
        mesh=mesh,
        in_specs=placed,
        out_specs=(
            P("doc", "ctx", None),
            P("doc", "ctx", None),
            P("doc", "ctx", None),
            P(None, BOTH, None),
            P(None, BOTH, None),
            P(None, BOTH, None),
            P(None, BOTH, None),
            P(None, None, None, BOTH),
            P(None, None, BOTH),
            P(None, None, BOTH),
            P(None, BOTH),
        ),
        check_vma=False,
    )
```

```python
import functools

import jax
import jax.numpy as jnp
from jax import lax
from jax.experimental import pallas as pl
from jax.experimental.pallas import tpu as pltpu
from jax.sharding import PartitionSpec as P

HEADS = 16
HEAD_DIM = 64
BUCKETS = 128
TEXT = 512
PATCH = 49
GRID_SIDE = 32
CELLS = GRID_SIDE * GRID_SIDE
LANES = 128
PAIR = 2 * HEAD_DIM
NORM_EPSILON = 1e-05
SCORE_SCALE = (3.0 * HEAD_DIM) ** (-0.5)
MASKED = -1e30
FIXED_TOP = 16000.0
BF16 = jnp.bfloat16
F32 = jnp.float32
BOTH = ("doc", "ctx")


def pad_lanes(count):
    return -(-count // LANES) * LANES


def norm_rows(values_in, scale_gain, offset):
    centered = values_in - jnp.mean(values_in, axis=-1, keepdims=True)
    spread = jnp.mean(centered * centered, axis=-1, keepdims=True)
    return centered * lax.rsqrt(spread + NORM_EPSILON) * scale_gain + offset


def exact_gelu(values_in):
    return jax.nn.gelu(values_in, approximate=False)


def dot(left, right, left_axis, right_axis):
    return lax.dot_general(
        left, right, (((left_axis,), (right_axis,)), ((), ())), preferred_element_type=F32
    )


def lookup(table, index):
    return jnp.take_along_axis(table, index, axis=1, mode="promise_in_bounds")


def head_lanes(head, rows):
    lane = lax.broadcasted_iota(jnp.int32, (rows, PAIR), 1)
    return (lane >= head * HEAD_DIM) & (lane < (head + 1) * HEAD_DIM)


def keep_head(values, head):
    return jnp.where(head_lanes(head, values.shape[0]), values, jnp.zeros_like(values))


def keep_both(table):
    return jnp.concatenate([keep_head(table, 0), keep_head(table, 1)], axis=0)


def paired_lookup(tables, indices):
    top = [jnp.max(jnp.abs(table)) for table in tables]
    top = jnp.maximum(jnp.maximum(top[0], top[1]), 1e-30)
    fine = FIXED_TOP / top
    total = None
    for table, index in zip(tables, indices):
        steps = jnp.round(table * fine).astype(jnp.int32)
        both = steps[:, :BUCKETS] * 65536 + steps[:, BUCKETS:]
        found = lookup(both, index)
        total = found if total is None else total + found
    coarse = top / FIXED_TOP
    first = (total + 32768) >> 16
    second = (total << 16) >> 16
    return first.astype(F32) * coarse, second.astype(F32) * coarse


def attend_kernel(
    chunks,
    q_ref,
    *refs,
):
    k_refs = refs[:chunks]
    v_refs = refs[chunks : 2 * chunks]
    (
        rel_key_ref,
        rel_query_ref,
        index_linear_ref,
        index_planar_ref,
        turned_linear_ref,
        turned_planar_ref,
        mask_ref,
        mixed_ref,
        prob_ref,
        left_scr,
        right_scr,
        value_scr,
    ) = refs[2 * chunks :]
    rows = q_ref.shape[0]
    keys = rows * chunks
    keys_wide = right_scr.shape[0]
    rows_wide = left_scr.shape[1] - PAIR

    @pl.when(pl.program_id(0) == 0)
    def _():
        row_at = lax.broadcasted_iota(jnp.int32, (rows, rows_wide), 0)
        lane_at = lax.broadcasted_iota(jnp.int32, (rows, rows_wide), 1)
        left_scr[:, PAIR:] = jnp.where(row_at == lane_at, 1.0, 0.0).astype(BF16)
        right_scr[keys:, :] = jnp.zeros((keys_wide - keys, PAIR + rows_wide), BF16)
        value_scr[keys:, :] = jnp.zeros((keys_wide - keys, PAIR), BF16)

    for chunk in range(chunks):
        right_scr[chunk * rows : (chunk + 1) * rows, :PAIR] = k_refs[chunk][...]
        value_scr[chunk * rows : (chunk + 1) * rows, :] = v_refs[chunk][...]

    query = q_ref[...]
    key = right_scr[:keys, :PAIR]
    key_bias = paired_lookup(
        [dot(key, keep_both(rel_query_ref[kind]), 1, 1) for kind in range(2)],
        [turned_linear_ref[...], turned_planar_ref[...]],
    )
    query_bias = paired_lookup(
        [dot(query, keep_both(rel_key_ref[kind]), 1, 1) for kind in range(2)],
        [index_linear_ref[...], index_planar_ref[...]],
    )
    mixed = []
    for head in range(2):
        left_scr[:, :PAIR] = keep_head(query, head)
        right_scr[:keys, PAIR:] = key_bias[head].astype(BF16)
        raw = dot(left_scr[...], right_scr[...], 1, 1) + query_bias[head]
        scaled = raw * SCORE_SCALE + mask_ref[...]
        shifted = scaled - jnp.max(scaled, axis=-1, keepdims=True)
        exponent = jnp.exp(shifted)
        inverse = 1.0 / jnp.sum(exponent, axis=-1, keepdims=True)
        prob = (exponent * inverse).astype(BF16)
        prob_ref[head] = prob
        mixed.append(dot(prob, value_scr[...], 1, 0))
    mixed_ref[...] = jnp.where(head_lanes(1, rows), mixed[1], mixed[0]).astype(BF16)


def whole_spec(array):
    return pl.BlockSpec(array.shape, lambda step: (0,) * array.ndim)


def attend(qkv, other_kv, rel_key, rel_query, lookups):
    rows = qkv.shape[0]
    width = qkv.shape[1] // 3
    pairs = width // PAIR
    chunks = 1 + len(other_kv)
    keys_wide = pad_lanes(rows * chunks)
    rows_wide = pad_lanes(rows)

    def column(offset):
        return pl.BlockSpec((rows, PAIR), lambda step: (0, offset + step))

    rel_spec = pl.BlockSpec((2, BUCKETS, PAIR), lambda step: (0, 0, step))
    small = (
        lookups["index_linear"],
        lookups["index_planar"],
        lookups["turned_linear"],
        lookups["turned_planar"],
        lookups["mask"],
    )
    return pl.pallas_call(
        functools.partial(attend_kernel, chunks),
        grid=(pairs,),
        in_specs=[column(0), column(pairs)]
        + [column(0)] * (chunks - 1)
        + [column(2 * pairs)]
        + [column(pairs)] * (chunks - 1)
        + [rel_spec, rel_spec]
        + [whole_spec(item) for item in small],
        out_specs=[
            pl.BlockSpec((rows, PAIR), lambda step: (0, step)),
            pl.BlockSpec((2, rows, keys_wide), lambda step: (step, 0, 0)),
        ],
        out_shape=[
            jax.ShapeDtypeStruct((rows, width), BF16),
            jax.ShapeDtypeStruct((2 * pairs, rows, keys_wide), BF16),
        ],
        scratch_shapes=[
            pltpu.VMEM((rows, PAIR + rows_wide), BF16),
            pltpu.VMEM((keys_wide, PAIR + rows_wide), BF16),
            pltpu.VMEM((keys_wide, PAIR), BF16),
        ],
        compiler_params=pltpu.CompilerParams(vmem_limit_bytes=40 << 20),
        cost_estimate=pl.CostEstimate(
            flops=20 * rows * rows * chunks * width,
            bytes_accessed=4 * pairs * rows * keys_wide + 8 * rows * width,
            transcendentals=2 * pairs * rows * keys_wide,
        ),
        name="attend",
    )(qkv, qkv, *other_kv, qkv, *other_kv, rel_key, rel_query, *small)


def bucket_sums(cells, pos):
    spot = pos & (LANES - 1)
    part = pos >> 7
    total = jnp.zeros(spot.shape, F32)
    for chunk in range(CELLS // LANES):
        total = jnp.where(
            part == chunk, lookup(cells[:, chunk * LANES : (chunk + 1) * LANES], spot), total
        )
    lane = lax.broadcasted_iota(jnp.int32, total.shape, 1)
    total = total - jnp.where(lane < BUCKETS - 8, pltpu.roll(total, BUCKETS - 8, 1), 0.0)
    return total - jnp.where((lane & 7) < 7, pltpu.roll(total, BUCKETS - 1, 1), 0.0)


def band_sums(values, index, pos):
    spot = pos & (LANES - 1)
    part = pos >> 7
    total = jnp.zeros(spot.shape, F32)
    for chunk in range(values.shape[1] // LANES):
        total = jnp.where(
            part == chunk, lookup(values[:, chunk * LANES : (chunk + 1) * LANES], spot), total
        )
    low = jnp.sum(jnp.where(index == 0, values, 0.0), axis=-1, keepdims=True)
    high = jnp.sum(jnp.where(index == BUCKETS - 1, values, 0.0), axis=-1, keepdims=True)
    lane = lax.broadcasted_iota(jnp.int32, total.shape, 1)
    return jnp.where(lane == 0, low, jnp.where(lane == BUCKETS - 1, high, total))


def attend_back_kernel(
    chunks,
    q_ref,
    *refs,
):
    k_refs = refs[:chunks]
    v_refs = refs[chunks : 2 * chunks]
    (
        grad_ref,
        prob_ref,
        rel_key_ref,
        rel_query_ref,
        index_linear_ref,
        turned_linear_ref,
        key_cells_ref,
        row_cells_ref,
        planar_pos_ref,
        linear_pos_ref,
        turned_planar_pos_ref,
        turned_linear_pos_ref,
        grad_query_ref,
        grad_kv_ref,
        grad_rel_ref,
        key_scr,
        value_scr,
        raw_scr,
        low_scr,
        turned_scr,
        cell_scr,
    ) = refs[2 * chunks :]
    rows = q_ref.shape[0]
    keys = rows * chunks
    keys_wide = key_scr.shape[0]
    rows_wide = raw_scr.shape[0]

    @pl.when(pl.program_id(0) == 0)
    def _():
        key_scr[keys:, :] = jnp.zeros((keys_wide - keys, PAIR), BF16)
        value_scr[keys:, :] = jnp.zeros((keys_wide - keys, PAIR), BF16)
        raw_scr[rows:, :] = jnp.zeros((rows_wide - rows, keys_wide), F32)

    for chunk in range(chunks):
        key_scr[chunk * rows : (chunk + 1) * rows, :] = k_refs[chunk][...]
        value_scr[chunk * rows : (chunk + 1) * rows, :] = v_refs[chunk][...]

    found = []
    for head in range(2):
        query = keep_head(q_ref[...], head)
        grad = keep_head(grad_ref[...], head)
        raw_scr[:rows, :] = dot(grad, value_scr[...], 1, 1)
        prob = prob_ref[head].astype(F32)
        grad_prob = raw_scr[:rows, :]
        inner = jnp.sum(prob * grad_prob, axis=-1, keepdims=True)
        grad_raw = (prob * (grad_prob - inner) * SCORE_SCALE).astype(BF16)
        low_scr[...] = grad_raw
        raw_scr[:rows, :] = grad_raw.astype(F32)

        cell_scr[:rows, :] = dot(low_scr[...], key_cells_ref[...], 1, 0)
        planar = bucket_sums(cell_scr[:rows, :], planar_pos_ref[...])
        linear = band_sums(raw_scr[:rows, :], index_linear_ref[...], linear_pos_ref[...])
        row_bucket = jnp.concatenate([linear.astype(BF16), planar.astype(BF16)], axis=1)
        rel_key = keep_head(rel_key_ref[...].reshape(2 * BUCKETS, PAIR), head)
        rel_query = keep_head(rel_query_ref[...].reshape(2 * BUCKETS, PAIR), head)
        grad_query = dot(low_scr[...], key_scr[...], 1, 0) + dot(row_bucket, rel_key, 1, 0)
        grad_rel_key = dot(row_bucket, query, 0, 0)

        turned_scr[...] = raw_scr[...].T[:keys]
        turned_low = turned_scr[...].astype(BF16)
        cell_scr[...] = dot(turned_low, row_cells_ref[...], 1, 0)
        planar = bucket_sums(cell_scr[...], turned_planar_pos_ref[...])
        linear = band_sums(turned_scr[...], turned_linear_ref[...], turned_linear_pos_ref[...])
        key_bucket = jnp.concatenate([linear.astype(BF16), planar.astype(BF16)], axis=1)
        grad_key = dot(turned_low[:, :rows], query, 1, 0) + dot(key_bucket, rel_query, 1, 0)
        grad_value = dot(prob_ref[head], grad, 0, 0)[:keys]
        grad_rel_query = dot(key_bucket, key_scr[:keys, :], 0, 0)
        found.append((grad_query, grad_key, grad_value, grad_rel_query, grad_rel_key))

    def joined(member):
        first, second = found[0][member], found[1][member]
        return jnp.where(head_lanes(1, first.shape[0]), second, first).astype(BF16)

    grad_query_ref[...] = joined(0)
    grad_key, grad_value = joined(1), joined(2)
    for chunk in range(chunks):
        grad_kv_ref[chunk, 0] = grad_key[chunk * rows : (chunk + 1) * rows]
        grad_kv_ref[chunk, 1] = grad_value[chunk * rows : (chunk + 1) * rows]
    grad_rel_ref[0] = joined(3)
    grad_rel_ref[1] = joined(4)


def attend_back(qkv, other_kv, grad_mixed, prob, rel_key, rel_query, lookups, first, count):
    rows = qkv.shape[0]
    width = qkv.shape[1] // 3
    pairs = width // PAIR
    chunks = 1 + len(other_kv)
    keys = rows * chunks
    keys_wide = pad_lanes(keys)
    rows_wide = pad_lanes(rows)
    part = count * PAIR

    def column(offset):
        return pl.BlockSpec((rows, PAIR), lambda step: (0, offset + first + step))

    rel_spec = pl.BlockSpec((2, BUCKETS, PAIR), lambda step: (0, 0, first + step))
    small = (
        lookups["index_linear"],
        lookups["turned_linear"],
        lookups["key_cells"],
        lookups["row_cells"],
        lookups["planar_pos"],
        lookups["linear_pos"],
        lookups["turned_planar_pos"],
        lookups["turned_linear_pos"],
    )
    return pl.pallas_call(
        functools.partial(attend_back_kernel, chunks),
        grid=(count,),
        in_specs=[column(0), column(pairs)]
        + [column(0)] * (chunks - 1)
        + [column(2 * pairs)]
        + [column(pairs)] * (chunks - 1)
        + [
            column(0),
            pl.BlockSpec((2, rows, keys_wide), lambda step: (first + step, 0, 0)),
            rel_spec,
            rel_spec,
        ]
        + [whole_spec(item) for item in small],
        out_specs=[
            pl.BlockSpec((rows, PAIR), lambda step: (0, step)),
            pl.BlockSpec((chunks, 2, rows, PAIR), lambda step: (0, 0, 0, step)),
            pl.BlockSpec((2, 2 * BUCKETS, PAIR), lambda step: (0, 0, step)),
        ],
        out_shape=[
            jax.ShapeDtypeStruct((rows, part), BF16),
            jax.ShapeDtypeStruct((chunks, 2, rows, part), BF16),
            jax.ShapeDtypeStruct((2, 2 * BUCKETS, part), BF16),
        ],
        scratch_shapes=[
            pltpu.VMEM((keys_wide, PAIR), BF16),
            pltpu.VMEM((keys_wide, PAIR), BF16),
            pltpu.VMEM((rows_wide, keys_wide), F32),
            pltpu.VMEM((rows, keys_wide), BF16),
            pltpu.VMEM((keys, rows_wide), F32),
            pltpu.VMEM((keys, CELLS), F32),
        ],
        compiler_params=pltpu.CompilerParams(vmem_limit_bytes=56 << 20),
        cost_estimate=pl.CostEstimate(
            flops=80 * rows * rows * chunks * part,
            bytes_accessed=4 * count * rows * keys_wide + 24 * rows * part,
            transcendentals=0,
        ),
        name="attend_back",
    )(qkv, qkv, *other_kv, qkv, *other_kv, grad_mixed, prob, rel_key, rel_query, *small)


def make_lookups(cells_x, cells_y, count, place, row_count):
    seq_len = place.shape[0]
    keys_wide = pad_lanes(seq_len)
    rows_wide = pad_lanes(row_count)
    half_range = BUCKETS // 2

    def wide(values, total):
        return jnp.pad(values, ((0, total - values.shape[0]),))

    key_place, key_x, key_y = (wide(item, keys_wide) for item in (place, cells_x, cells_y))
    row_place, row_x, row_y = (item[:row_count] for item in (place, cells_x, cells_y))
    wide_place, wide_x, wide_y = (wide(item, rows_wide) for item in (row_place, row_x, row_y))

    def linear(i, j):
        return jnp.clip(i - j, -half_range, half_range - 1) + half_range

    def planar(ix, iy, jx, jy):
        return (jnp.clip(ix - jx, -8, 7) + 8) * 8 + jnp.clip(iy - jy, -4, 3) + 4

    out = {}
    out["index_linear"] = linear(row_place[:, None], key_place[None, :])
    out["index_planar"] = planar(row_x[:, None], row_y[:, None], key_x[None, :], key_y[None, :])
    out["turned_linear"] = linear(wide_place[None, :], place[:, None])
    out["turned_planar"] = planar(
        wide_x[None, :], wide_y[None, :], cells_x[:, None], cells_y[:, None]
    )
    valid = (place < count) | ((place >= TEXT) & (place < TEXT + PATCH))
    out["mask"] = jnp.pad(
        jnp.where(valid, 0.0, MASKED).astype(F32),
        ((0, keys_wide - seq_len),),
        constant_values=MASKED,
    )[None]
    key_live = jnp.arange(keys_wide) < seq_len
    row_live = jnp.arange(rows_wide) < row_count
    cell = jnp.arange(CELLS, dtype=jnp.int32)
    cell_x, cell_y = cell // GRID_SIDE, cell % GRID_SIDE
    out["key_cells"] = (
        key_live[:, None] & (key_x[:, None] <= cell_x) & (key_y[:, None] <= cell_y)
    ).astype(BF16)
    out["row_cells"] = (
        row_live[:, None] & (wide_x[:, None] >= cell_x) & (wide_y[:, None] >= cell_y)
    ).astype(BF16)
    bucket = jnp.arange(BUCKETS, dtype=jnp.int32)
    bucket_x, bucket_y = bucket // 8, bucket % 8
    top = GRID_SIDE - 1
    to_x = jnp.where(bucket_x == 0, top, jnp.minimum(row_x[:, None] - bucket_x + 8, top))
    to_y = jnp.where(bucket_y == 0, top, jnp.minimum(row_y[:, None] - bucket_y + 4, top))
    out["planar_pos"] = jnp.where((to_x >= 0) & (to_y >= 0), to_x * GRID_SIDE + to_y, -1)
    from_x = jnp.where(bucket_x == 0, 0, jnp.maximum(cells_x[:, None] + bucket_x - 8, 0))
    from_y = jnp.where(bucket_y == 0, 0, jnp.maximum(cells_y[:, None] + bucket_y - 4, 0))
    out["turned_planar_pos"] = jnp.where(
        (from_x <= top) & (from_y <= top), from_x * GRID_SIDE + from_y, -1
    )
    first_place = place[0]
    target = row_place[:, None] - bucket + half_range
    out["linear_pos"] = jnp.where(
        (target >= 0) & (target < seq_len), (target - first_place) % seq_len, -1
    )
    source = place[:, None] + bucket - half_range - first_place
    out["turned_linear_pos"] = jnp.where((source >= 0) & (source < row_count), source, -1)
    return out


class Home:
    def __init__(self, mesh_shape, local_docs, block_rows, width):
        self.width = width
        self.doc_size = mesh_shape["doc"]
        self.ctx_size = mesh_shape["ctx"]
        self.block = block_rows
        self.docs = 2 * local_docs
        self.span = self.ctx_size // self.docs
        self.group = 2 * self.span
        self.rows = 2 * block_rows
        self.seq = block_rows * self.ctx_size

    def flat(self, doc, ctx):
        return doc * self.ctx_size + ctx

    def move_pairs(self, turn):
        pairs = []
        for pair in range(self.doc_size // 2):
            for core in range(2):
                for block in range(self.ctx_size):
                    slot = (block + turn) % 2
                    doc = 2 * core + slot
                    place = block // 2
                    target = self.flat(
                        2 * pair + place // self.span, doc * self.span + place % self.span
                    )
                    pairs.append((self.flat(2 * pair + core, block), target))
        return pairs

    def to_home(self, local):
        ctx = lax.axis_index("ctx")
        doc_here = ctx // self.span
        pieces = []
        for turn in range(2):
            piece = lax.dynamic_index_in_dim(local, (ctx + turn) % 2, 0, keepdims=False)
            pieces.append(lax.ppermute(piece, BOTH, self.move_pairs(turn)))
        swap = (doc_here % 2) == 1
        low_half = jnp.where(swap, pieces[1], pieces[0])
        high_half = jnp.where(swap, pieces[0], pieces[1])
        return jnp.concatenate([low_half, high_half], axis=0)

    def from_home(self, rows):
        ctx = lax.axis_index("ctx")
        doc_here = ctx // self.span
        halves = rows.reshape(2, self.block, rows.shape[1])
        pieces = []
        for turn in range(2):
            piece = lax.dynamic_index_in_dim(halves, (doc_here + turn) % 2, 0, keepdims=False)
            back = [(target, source) for source, target in self.move_pairs(turn)]
            pieces.append(lax.ppermute(piece, BOTH, back))
        swap = (ctx % 2) == 1
        first = jnp.where(swap, pieces[1], pieces[0])
        second = jnp.where(swap, pieces[0], pieces[1])
        return jnp.stack([first, second])

    def core_half(self, values, core):
        block = self.width // self.doc_size
        pieces = []
        for start in range(0, values.shape[1], 2 * block):
            first = values[:, start : start + block]
            second = values[:, start + block : start + 2 * block]
            pieces.append(jnp.where(core == 0, first, second))
        return jnp.concatenate(pieces, axis=1)

    def position(self):
        core = lax.axis_index("doc") % 2
        return core * self.span + lax.axis_index("ctx") % self.span

    def ring_pairs(self, shift):
        pairs = []
        for doc in range(self.doc_size):
            for ctx in range(self.ctx_size):
                place = (doc % 2) * self.span + ctx % self.span
                other = (place + shift) % self.group
                pairs.append(
                    (
                        self.flat(doc, ctx),
                        self.flat(
                            doc - doc % 2 + other // self.span,
                            ctx - ctx % self.span + other % self.span,
                        ),
                    )
                )
        return pairs

    def fetch(self, values):
        return [
            lax.ppermute(values, BOTH, self.ring_pairs(-shift)) for shift in range(1, self.group)
        ]

    def give_back(self, pieces):
        return [
            lax.ppermute(piece, BOTH, self.ring_pairs(shift))
            for shift, piece in enumerate(pieces, 1)
        ]


def to_part_order(columns, devices, shard):
    rows, hidden = columns.shape
    split = columns.reshape(rows, devices, hidden // (devices * shard), shard)
    return split.transpose(0, 2, 1, 3).reshape(rows, hidden)


def to_device_order(columns, devices, shard):
    rows, hidden = columns.shape
    split = columns.reshape(rows, hidden // (devices * shard), devices, shard)
    return split.transpose(0, 2, 1, 3).reshape(rows, hidden)


def pack_layer(devices, w_qkv, w_out, w_in, w_down, tables, gains, biases, b_in):
    shard = w_qkv.shape[0]
    down = w_down.reshape(-1, shard, w_down.shape[1])
    down = [down[part] for part in range(down.shape[0])]
    small = jnp.concatenate(
        [tables.reshape(-1, shard).T, gains.T, biases.T, b_in.reshape(-1, shard).T], axis=1
    )
    small = jnp.pad(small, ((0, 0), (0, pad_lanes(small.shape[1]) - small.shape[1])))
    return jnp.concatenate(
        [w_qkv, w_out, to_part_order(w_in, devices, shard), *down, small], axis=1
    )


def unpack_layer(packed):
    width = packed.shape[0]
    hidden = ((packed.shape[1] - 4 * width) // (2 * width)) * width
    start = 4 * width + hidden
    small = packed[:, start + hidden :]
    table_cols = 2 * BUCKETS
    rows = small[:, table_cols:].astype(F32).T
    return dict(
        qkv=packed[:, : 3 * width],
        out=packed[:, 3 * width : 4 * width],
        w_in=packed[:, 4 * width : start],
        down=[packed[:, start + at : start + at + width] for at in range(0, hidden, width)],
        tables=small[:, :table_cols],
        gains=rows[:2],
        biases=rows[2:9],
        b_in=rows[9 : 9 + hidden // width].reshape(hidden),
    )


def flips(size, bit):
    return [(index, index ^ bit) for index in range(size)]


class Scatter:
    def __init__(self, shape, order):
        self.doc_size, self.ctx_size = shape
        self.order = order
        self.bits = [1 << at for at in range(self.doc_size.bit_length() - 2, 0, -1)]
        self.value = None
        self.got = None
        self.steps = None

    def begin(self, leading, half):
        columns = half.shape[-1]
        block = half.size // (columns * leading * (self.doc_size // 2) * self.ctx_size)
        self.value = half.reshape((leading,) + (2,) * len(self.bits) + (self.ctx_size, block, columns))
        self.left = list(self.bits)
        steps = [("doc", bit) for bit in (self.bits if self.order == 0 else reversed(self.bits))]
        size = self.ctx_size // 2
        while size:
            steps.append(("ctx", size))
            size //= 2
        self.steps = steps
        self.send()

    def send(self):
        self.kept = self.got = None
        if not self.steps:
            return
        axis_name, bit = self.steps.pop(0)
        value = self.value
        if axis_name == "doc":
            axis = 1 + self.left.index(bit)
            self.left.remove(bit)
            size = self.doc_size
        else:
            axis = 1
            value = value.reshape((value.shape[0], 2, value.shape[1] // 2) + value.shape[2:])
            size = self.ctx_size
        mine = (lax.axis_index(axis_name) // bit) % 2
        self.kept = lax.dynamic_index_in_dim(value, mine, axis, keepdims=False)
        sent = lax.dynamic_index_in_dim(value, 1 - mine, axis, keepdims=False)
        self.got = lax.ppermute(sent, axis_name, flips(size, bit))

    def advance(self):
        total = self.kept.astype(F32) + self.got.astype(F32)
        self.value = total.astype(BF16)
        if not self.steps:
            self.value = total
        self.send()

    def result(self):
        value = self.value
        return value.reshape((value.shape[0],) + value.shape[-2:])


class Flight:
    def __init__(self):
        self.moving = []

    def add(self, scatter):
        self.moving.append(scatter)

    def tick(self, values):
        got = [item.got for item in self.moving]
        values, got = lax.optimization_barrier((values, got))
        for item, piece in zip(self.moving, got):
            item.got = piece
            item.advance()
        self.moving = [item for item in self.moving if item.got is not None]
        return values


def layer_forward(home, rows_in, rows_low, weights, lookups):
    width = rows_in.shape[1]
    gains, biases = weights["gains"], weights["biases"]
    qkv = (dot(rows_low, weights["qkv"], 1, 0) + biases[:3].reshape(1, -1)).astype(BF16)
    other_kv = home.fetch(qkv[:, width:])
    rel_both = dot(weights["tables"], weights["qkv"][:, : 2 * width], 0, 0).astype(BF16)
    rel_query = rel_both[:, :width].reshape(2, BUCKETS, width)
    rel_key = rel_both[:, width:].reshape(2, BUCKETS, width)
    mixed, prob = attend(qkv, other_kv, rel_key, rel_query, lookups)
    first_sum = rows_in + (dot(mixed, weights["out"], 1, 0) + biases[3])
    first_norm = norm_rows(first_sum, gains[0], biases[5])
    norm_low = first_norm.astype(BF16)
    hidden_pre = dot(norm_low, weights["w_in"], 1, 0) + weights["b_in"]
    active = exact_gelu(hidden_pre).astype(BF16)
    down_rows = biases[4]
    for part, panel in enumerate(weights["down"]):
        down_rows = down_rows + dot(active[:, part * width : (part + 1) * width], panel, 1, 0)
    second_sum = first_norm + down_rows
    result = norm_rows(second_sum, gains[1], biases[6])
    kept = dict(
        rows_low=rows_low,
        qkv=qkv,
        other_kv=other_kv,
        rel_key=rel_key,
        rel_query=rel_query,
        prob=prob,
        mixed=mixed,
        first_sum=first_sum,
        norm_low=norm_low,
        hidden_pre=hidden_pre,
        active=active,
        second_sum=second_sum,
    )
    return result, kept


class CoreSum:
    def __init__(self, home, terms):
        self.home = home
        self.terms = terms
        core = lax.axis_index("doc") % 2
        self.core = core
        sent = self.product(1 - core).astype(BF16)
        self.got = lax.ppermute(sent, "doc", flips(home.doc_size, 1))

    def product(self, core):
        total = None
        for left, right in self.terms:
            piece = dot(self.home.core_half(left, core), right, 0, 0)
            total = piece if total is None else total + piece
        return total

    def finish(self):
        return (self.product(self.core) + self.got.astype(F32)).astype(BF16)


def layer_backward(home, flight, grad_out, kept, weights, lookups):
    width = grad_out.shape[1]
    shape = (home.doc_size, home.ctx_size)
    gains, biases = weights["gains"], weights["biases"]
    rows = grad_out.shape[0]
    parts = len(weights["down"])

    _, second_pull = jax.vjp(norm_rows, kept["second_sum"], gains[1], biases[6])
    grad_second, grad_gain_two, grad_offset_two = second_pull(grad_out)
    grad_down = grad_second.astype(BF16)
    sum_down = CoreSum(home, [(kept["active"], grad_down)])
    grad_active = jnp.concatenate(
        [dot(grad_down, panel, 1, 1) for panel in weights["down"]], axis=1
    )
    _, gelu_pull = jax.vjp(exact_gelu, kept["hidden_pre"])
    grad_hidden = gelu_pull(grad_active)[0].astype(BF16)
    grad_hidden, grad_down, sum_down.got = flight.tick((grad_hidden, grad_down, sum_down.got))

    sum_in = CoreSum(home, [(kept["norm_low"], grad_hidden)])
    grad_first_norm = grad_second + dot(grad_hidden, weights["w_in"], 1, 1)
    _, first_pull = jax.vjp(norm_rows, kept["first_sum"], gains[0], biases[5])
    grad_first, grad_gain_one, grad_offset_one = first_pull(grad_first_norm)
    grad_att = grad_first.astype(BF16)
    sum_out = CoreSum(home, [(kept["mixed"], grad_att)])
    grad_mixed = dot(grad_att, weights["out"], 1, 1).astype(BF16)
    half_down = sum_down.finish()
    grad_mixed, half_down, sum_in.got, sum_out.got = flight.tick(
        (grad_mixed, half_down, sum_in.got, sum_out.got)
    )
    scatter_down, scatter_in = Scatter(shape, 0), Scatter(shape, 1)
    scatter_down.begin(parts, half_down)
    half_in = jnp.concatenate([sum_in.finish(), sum_out.finish()], axis=1)
    scatter_in.begin(1, half_in)
    flight.add(scatter_down)
    flight.add(scatter_in)

    pairs = width // PAIR
    count = pairs // 2
    found = []
    moved = []
    for first in range(0, pairs, count):
        grad_query, grad_kv, grad_rel = attend_back(
            kept["qkv"],
            kept["other_kv"],
            grad_mixed,
            kept["prob"],
            kept["rel_key"],
            kept["rel_query"],
            lookups,
            first,
            count,
        )
        grad_query, grad_kv, grad_rel, grad_mixed = flight.tick(
            (grad_query, grad_kv, grad_rel, grad_mixed)
        )
        moved.append(home.give_back([grad_kv[chunk] for chunk in range(1, grad_kv.shape[0])]))
        found.append((grad_query, grad_kv[0], grad_rel))

    own = []
    for (_, grad_kv, _), pieces in zip(found, moved):
        total = grad_kv.astype(F32)
        for piece in pieces:
            total = total + piece.astype(F32)
        own.append(total.astype(BF16))
    grad_qkv = jnp.concatenate(
        [item[0] for item in found] + [item[0] for item in own] + [item[1] for item in own], axis=1
    )
    rel_both = [jnp.concatenate([item[2][kind] for item in found], axis=1) for kind in range(2)]
    tables = weights["tables"]
    grad_tables = dot(weights["qkv"][:, :width], rel_both[0], 1, 1) + dot(
        weights["qkv"][:, width : 2 * width], rel_both[1], 1, 1
    )
    bias_sums = jnp.sum(grad_qkv.astype(F32), axis=0).reshape(3, width)
    small = jnp.concatenate(
        [
            grad_gain_one[None],
            grad_gain_two[None],
            bias_sums,
            jnp.sum(grad_att.astype(F32), axis=0)[None],
            jnp.sum(grad_down.astype(F32), axis=0)[None],
            grad_offset_one[None],
            grad_offset_two[None],
            jnp.sum(grad_hidden.astype(F32), axis=0).reshape(parts, width),
        ],
        axis=0,
    ).T
    total_cols = 2 * BUCKETS + small.shape[1]
    small = jnp.concatenate([grad_tables, small], axis=1)
    small = jnp.pad(small, ((0, 0), (0, pad_lanes(total_cols) - total_cols)))
    split = small.astype(BF16).reshape(home.doc_size // 2, 2, -1, small.shape[1])
    core = lax.axis_index("doc") % 2
    small_sent = lax.dynamic_index_in_dim(split, 1 - core, 1, keepdims=False)
    small_kept = lax.dynamic_index_in_dim(split, core, 1, keepdims=False)
    small_got = lax.ppermute(small_sent, "doc", flips(home.doc_size, 1))
    rows_turned = kept["rows_low"]
    sum_qk = CoreSum(
        home,
        [
            (rows_turned, grad_qkv[:, : 2 * width]),
            (tables.T, jnp.concatenate(rel_both, axis=1)),
        ],
    )
    sum_v = CoreSum(home, [(rows_turned, grad_qkv[:, 2 * width :])])
    grad_rows = grad_first + dot(grad_qkv, weights["qkv"], 1, 1)
    grad_rows, sum_qk.got, sum_v.got, small_got = flight.tick(
        (grad_rows, sum_qk.got, sum_v.got, small_got)
    )
    small_half = (small_kept.astype(F32) + small_got.astype(F32)).astype(BF16)
    half_qk, half_v = sum_qk.finish(), sum_v.finish()
    cut = 7 * width // 4
    scatter_first, scatter_rest = Scatter(shape, 0), Scatter(shape, 1)
    scatter_first.begin(1, half_qk[:, :cut])
    scatter_rest.begin(
        1,
        jnp.concatenate(
            [half_qk[:, cut:], half_v, small_half.reshape(half_qk.shape[0], -1)], axis=1
        ),
    )
    flight.add(scatter_first)
    flight.add(scatter_rest)
    return grad_rows, (scatter_down, scatter_in, scatter_first, scatter_rest)


def collect(home, scatters, width, hidden):
    scatter_down, scatter_in, scatter_first, scatter_rest = scatters
    devices = home.doc_size * home.ctx_size
    down = scatter_down.result()
    shard = down.shape[1]
    down = down.reshape(-1, width)
    both = scatter_in.result()[0]
    grad_in = to_device_order(both[:, :hidden], devices, shard)
    grad_out = both[:, hidden:]
    rest = scatter_rest.result()[0]
    first = scatter_first.result()[0]
    qkv_left = 3 * width - first.shape[1]
    qkv = jnp.concatenate([first, rest[:, :qkv_left]], axis=1)
    small = rest[:, qkv_left:]
    table_cols = 2 * BUCKETS
    tables = small[:, :table_cols].T.reshape(2, BUCKETS, shard)
    rows = small[:, table_cols:].T
    gains, biases = rows[:2], rows[2:9]
    b_in = rows[9 : 9 + hidden // width].reshape(-1)
    return qkv, grad_out, grad_in, down, tables, gains, biases, b_in


def body(
    mesh_shape,
    layer_input,
    text_count,
    coords,
    w_qkv,
    w_out,
    w_in,
    w_down,
    rel_tables,
    ln_gains,
    biases,
    b_in,
    cotangent,
):
    doc_size, ctx_size = mesh_shape["doc"], mesh_shape["ctx"]
    device_count = doc_size * ctx_size
    local_docs, block_rows, width = layer_input.shape
    layer_count = w_qkv.shape[0]
    hidden = w_in.shape[2]
    home = Home(mesh_shape, local_docs, block_rows, width)

    packed = [
        pack_layer(
            device_count,
            w_qkv[layer],
            w_out[layer],
            w_in[layer],
            w_down[layer],
            rel_tables[layer],
            ln_gains[layer],
            biases[layer],
            b_in[layer],
        )
        for layer in range(layer_count)
    ]

    core = lax.axis_index("doc") % 2
    doc_here = lax.axis_index("ctx") // home.span
    facts = jnp.concatenate([coords.reshape(local_docs, -1), text_count[:, None]], axis=1)
    other_facts = lax.ppermute(facts, "doc", flips(doc_size, 1))
    mine = jnp.where(
        doc_here // local_docs == core,
        lax.dynamic_index_in_dim(facts, doc_here % local_docs, 0, keepdims=False),
        lax.dynamic_index_in_dim(other_facts, doc_here % local_docs, 0, keepdims=False),
    )
    place = (jnp.arange(home.seq, dtype=jnp.int32) + home.position() * home.rows) % home.seq

    def turned(values):
        twice = jnp.concatenate([values, values])
        return lax.dynamic_slice_in_dim(twice, home.position() * home.rows, home.seq)

    lookups = make_lookups(
        turned(mine[: home.seq]),
        turned(mine[home.seq : 2 * home.seq]),
        mine[2 * home.seq],
        place,
        home.rows,
    )

    rows_low = home.to_home(layer_input)
    current = rows_low.astype(F32)
    all_weights = []
    gathered = None
    for layer in range(layer_count):
        shard = packed[layer]
        if gathered is not None:
            shard, gathered = lax.optimization_barrier((shard, gathered))
            all_weights[-1] = unpack_layer(gathered)
        gathered = lax.all_gather(shard, BOTH, axis=0, tiled=True)
        all_weights.append(unpack_layer(gathered))
    kept_all = []
    outputs = []
    for layer in range(layer_count):
        current, kept = layer_forward(home, current, rows_low, all_weights[layer], lookups)
        rows_low = current.astype(BF16)
        outputs.append(home.from_home(rows_low).astype(F32))
        kept_all.append(kept)
    grad_rows = home.to_home(cotangent).astype(F32)
    scatters = [None] * layer_count
    flight = Flight()
    for layer in reversed(range(layer_count)):
        grad_rows, scatters[layer] = layer_backward(
            home, flight, grad_rows, kept_all[layer], all_weights[layer], lookups
        )
    grad_input = home.from_home(grad_rows.astype(BF16)).astype(F32)
    while flight.moving:
        flight.tick(())
    totals = [collect(home, item, width, hidden) for item in scatters]

    def stack(member):
        return jnp.stack([totals[layer][member] for layer in range(layer_count)])

    return (outputs[0], outputs[-1], grad_input) + tuple(stack(member) for member in range(8))


def solution(mesh):
    placed = (
        P("doc", "ctx", None),
        P("doc"),
        P("doc", None, None),
        P(None, BOTH, None),
        P(None, BOTH, None),
        P(None, BOTH, None),
        P(None, BOTH, None),
        P(None, None, None, BOTH),
        P(None, None, BOTH),
        P(None, None, BOTH),
        P(None, BOTH),
        P("doc", "ctx", None),
    )
    return jax.shard_map(
        functools.partial(body, dict(mesh.shape)),
        mesh=mesh,
        in_specs=placed,
        out_specs=(
            P("doc", "ctx", None),
            P("doc", "ctx", None),
            P("doc", "ctx", None),
            P(None, BOTH, None),
            P(None, BOTH, None),
            P(None, BOTH, None),
            P(None, BOTH, None),
            P(None, None, None, BOTH),
            P(None, None, BOTH),
            P(None, None, BOTH),
            P(None, BOTH),
        ),
        check_vma=False,
    )
```

```python
import functools

import jax
import jax.numpy as jnp
from jax import lax
from jax.experimental import pallas as pl
from jax.experimental.pallas import tpu as pltpu
from jax.sharding import PartitionSpec as P

HEADS = 16
HEAD_DIM = 64
BUCKETS = 128
TEXT = 512
PATCH = 49
GRID_SIDE = 32
CELLS = GRID_SIDE * GRID_SIDE
LANES = 128
PAIR = 2 * HEAD_DIM
NORM_EPSILON = 1e-05
SCORE_SCALE = (3.0 * HEAD_DIM) ** (-0.5)
MASKED = -1e30
FIXED_TOP = 16000.0
BF16 = jnp.bfloat16
F32 = jnp.float32
BOTH = ("doc", "ctx")


def pad_lanes(count):
    return -(-count // LANES) * LANES


def norm_rows(values_in, scale_gain, offset):
    centered = values_in - jnp.mean(values_in, axis=-1, keepdims=True)
    spread = jnp.mean(centered * centered, axis=-1, keepdims=True)
    return centered * lax.rsqrt(spread + NORM_EPSILON) * scale_gain + offset


def below(values_in):
    return 0.5 * lax.erf(values_in * (0.5**0.5)) + 0.5


def exact_gelu(values_in):
    return values_in * below(values_in)


def gelu_slope(values_in):
    bell = jnp.exp(-0.5 * values_in * values_in) * ((0.5 / jnp.pi) ** 0.5)
    return below(values_in) + values_in * bell


def dot(left, right, left_axis, right_axis):
    return lax.dot_general(
        left, right, (((left_axis,), (right_axis,)), ((), ())), preferred_element_type=F32
    )


def lookup(table, index):
    return jnp.take_along_axis(table, index, axis=1, mode="promise_in_bounds")


def head_lanes(head, rows):
    lane = lax.broadcasted_iota(jnp.int32, (rows, PAIR), 1)
    return (lane >= head * HEAD_DIM) & (lane < (head + 1) * HEAD_DIM)


def keep_head(values, head):
    return jnp.where(head_lanes(head, values.shape[0]), values, jnp.zeros_like(values))


def keep_both(table):
    return jnp.concatenate([keep_head(table, 0), keep_head(table, 1)], axis=0)


def paired_lookup(tables, indices):
    top = [jnp.max(jnp.abs(table)) for table in tables]
    top = jnp.maximum(jnp.maximum(top[0], top[1]), 1e-30)
    fine = FIXED_TOP / top
    total = None
    for table, index in zip(tables, indices):
        steps = jnp.round(table * fine).astype(jnp.int32)
        both = steps[:, :BUCKETS] * 65536 + steps[:, BUCKETS:]
        found = lookup(both, index)
        total = found if total is None else total + found
    coarse = top / FIXED_TOP
    first = (total + 32768) >> 16
    second = (total << 16) >> 16
    return first.astype(F32) * coarse, second.astype(F32) * coarse


def attend_kernel(
    chunks,
    q_ref,
    *refs,
):
    k_refs = refs[:chunks]
    v_refs = refs[chunks : 2 * chunks]
    (
        rel_key_ref,
        rel_query_ref,
        index_linear_ref,
        index_planar_ref,
        turned_linear_ref,
        turned_planar_ref,
        mask_ref,
        mixed_ref,
        prob_ref,
        left_scr,
        right_scr,
        value_scr,
    ) = refs[2 * chunks :]
    rows = q_ref.shape[0]
    keys = rows * chunks
    keys_wide = right_scr.shape[0]
    rows_wide = left_scr.shape[1] - PAIR

    @pl.when(pl.program_id(0) == 0)
    def _():
        row_at = lax.broadcasted_iota(jnp.int32, (rows, rows_wide), 0)
        lane_at = lax.broadcasted_iota(jnp.int32, (rows, rows_wide), 1)
        left_scr[:, PAIR:] = jnp.where(row_at == lane_at, 1.0, 0.0).astype(BF16)
        right_scr[keys:, :] = jnp.zeros((keys_wide - keys, PAIR + rows_wide), BF16)
        value_scr[keys:, :] = jnp.zeros((keys_wide - keys, PAIR), BF16)

    for chunk in range(chunks):
        right_scr[chunk * rows : (chunk + 1) * rows, :PAIR] = k_refs[chunk][...]
        value_scr[chunk * rows : (chunk + 1) * rows, :] = v_refs[chunk][...]

    query = q_ref[...]
    key = right_scr[:keys, :PAIR]
    key_bias = paired_lookup(
        [dot(key, keep_both(rel_query_ref[kind]), 1, 1) for kind in range(2)],
        [turned_linear_ref[...], turned_planar_ref[...]],
    )
    query_bias = paired_lookup(
        [dot(query, keep_both(rel_key_ref[kind]), 1, 1) for kind in range(2)],
        [index_linear_ref[...], index_planar_ref[...]],
    )
    mixed = []
    for head in range(2):
        left_scr[:, :PAIR] = keep_head(query, head)
        right_scr[:keys, PAIR:] = key_bias[head].astype(BF16)
        raw = dot(left_scr[...], right_scr[...], 1, 1) + query_bias[head]
        scaled = raw * SCORE_SCALE + mask_ref[...]
        shifted = scaled - jnp.max(scaled, axis=-1, keepdims=True)
        exponent = jnp.exp(shifted)
        inverse = 1.0 / jnp.sum(exponent, axis=-1, keepdims=True)
        prob = (exponent * inverse).astype(BF16)
        prob_ref[head] = prob
        mixed.append(dot(prob, value_scr[...], 1, 0))
    mixed_ref[...] = jnp.where(head_lanes(1, rows), mixed[1], mixed[0]).astype(BF16)


def whole_spec(array):
    return pl.BlockSpec(array.shape, lambda step: (0,) * array.ndim)


def attend(qkv, other_kv, rel_key, rel_query, lookups):
    rows = qkv.shape[0]
    width = qkv.shape[1] // 3
    pairs = width // PAIR
    chunks = 1 + len(other_kv)
    keys_wide = pad_lanes(rows * chunks)
    rows_wide = pad_lanes(rows)

    def column(offset):
        return pl.BlockSpec((rows, PAIR), lambda step: (0, offset + step))

    rel_spec = pl.BlockSpec((2, BUCKETS, PAIR), lambda step: (0, 0, step))
    small = (
        lookups["index_linear"],
        lookups["index_planar"],
        lookups["turned_linear"],
        lookups["turned_planar"],
        lookups["mask"],
    )
    return pl.pallas_call(
        functools.partial(attend_kernel, chunks),
        grid=(pairs,),
        in_specs=[column(0), column(pairs)]
        + [column(0)] * (chunks - 1)
        + [column(2 * pairs)]
        + [column(pairs)] * (chunks - 1)
        + [rel_spec, rel_spec]
        + [whole_spec(item) for item in small],
        out_specs=[
            pl.BlockSpec((rows, PAIR), lambda step: (0, step)),
            pl.BlockSpec((2, rows, keys_wide), lambda step: (step, 0, 0)),
        ],
        out_shape=[
            jax.ShapeDtypeStruct((rows, width), BF16),
            jax.ShapeDtypeStruct((2 * pairs, rows, keys_wide), BF16),
        ],
        scratch_shapes=[
            pltpu.VMEM((rows, PAIR + rows_wide), BF16),
            pltpu.VMEM((keys_wide, PAIR + rows_wide), BF16),
            pltpu.VMEM((keys_wide, PAIR), BF16),
        ],
        compiler_params=pltpu.CompilerParams(vmem_limit_bytes=40 << 20),
        cost_estimate=pl.CostEstimate(
            flops=20 * rows * rows * chunks * width,
            bytes_accessed=4 * pairs * rows * keys_wide + 8 * rows * width,
            transcendentals=2 * pairs * rows * keys_wide,
        ),
        name="attend",
    )(qkv, qkv, *other_kv, qkv, *other_kv, rel_key, rel_query, *small)


def bucket_sums(cells, pos):
    spot = pos & (LANES - 1)
    part = pos >> 7
    total = jnp.zeros(spot.shape, F32)
    for chunk in range(CELLS // LANES):
        total = jnp.where(
            part == chunk, lookup(cells[:, chunk * LANES : (chunk + 1) * LANES], spot), total
        )
    lane = lax.broadcasted_iota(jnp.int32, total.shape, 1)
    total = total - jnp.where(lane < BUCKETS - 8, pltpu.roll(total, BUCKETS - 8, 1), 0.0)
    return total - jnp.where((lane & 7) < 7, pltpu.roll(total, BUCKETS - 1, 1), 0.0)


def band_sums(values, index, pos):
    spot = pos & (LANES - 1)
    part = pos >> 7
    total = jnp.zeros(spot.shape, F32)
    for chunk in range(values.shape[1] // LANES):
        total = jnp.where(
            part == chunk, lookup(values[:, chunk * LANES : (chunk + 1) * LANES], spot), total
        )
    low = jnp.sum(jnp.where(index == 0, values, 0.0), axis=-1, keepdims=True)
    high = jnp.sum(jnp.where(index == BUCKETS - 1, values, 0.0), axis=-1, keepdims=True)
    lane = lax.broadcasted_iota(jnp.int32, total.shape, 1)
    return jnp.where(lane == 0, low, jnp.where(lane == BUCKETS - 1, high, total))


def attend_back_kernel(
    chunks,
    q_ref,
    *refs,
):
    k_refs = refs[:chunks]
    v_refs = refs[chunks : 2 * chunks]
    (
        grad_ref,
        prob_ref,
        rel_key_ref,
        rel_query_ref,
        index_linear_ref,
        turned_linear_ref,
        key_cells_ref,
        row_cells_ref,
        planar_pos_ref,
        linear_pos_ref,
        turned_planar_pos_ref,
        turned_linear_pos_ref,
        grad_query_ref,
        grad_kv_ref,
        grad_rel_ref,
        key_scr,
        value_scr,
        raw_scr,
        low_scr,
        turned_scr,
        cell_scr,
    ) = refs[2 * chunks :]
    rows = q_ref.shape[0]
    keys = rows * chunks
    keys_wide = key_scr.shape[0]
    rows_wide = raw_scr.shape[0]

    @pl.when(pl.program_id(0) == 0)
    def _():
        key_scr[keys:, :] = jnp.zeros((keys_wide - keys, PAIR), BF16)
        value_scr[keys:, :] = jnp.zeros((keys_wide - keys, PAIR), BF16)
        raw_scr[rows:, :] = jnp.zeros((rows_wide - rows, keys_wide), F32)

    for chunk in range(chunks):
        key_scr[chunk * rows : (chunk + 1) * rows, :] = k_refs[chunk][...]
        value_scr[chunk * rows : (chunk + 1) * rows, :] = v_refs[chunk][...]

    found = []
    for head in range(2):
        query = keep_head(q_ref[...], head)
        grad = keep_head(grad_ref[...], head)
        raw_scr[:rows, :] = dot(grad, value_scr[...], 1, 1)
        prob = prob_ref[head].astype(F32)
        grad_prob = raw_scr[:rows, :]
        inner = jnp.sum(prob * grad_prob, axis=-1, keepdims=True)
        grad_raw = (prob * (grad_prob - inner) * SCORE_SCALE).astype(BF16)
        low_scr[...] = grad_raw
        raw_scr[:rows, :] = grad_raw.astype(F32)

        cell_scr[:rows, :] = dot(low_scr[...], key_cells_ref[...], 1, 0)
        planar = bucket_sums(cell_scr[:rows, :], planar_pos_ref[...])
        linear = band_sums(raw_scr[:rows, :], index_linear_ref[...], linear_pos_ref[...])
        row_bucket = jnp.concatenate([linear.astype(BF16), planar.astype(BF16)], axis=1)
        rel_key = keep_head(rel_key_ref[...].reshape(2 * BUCKETS, PAIR), head)
        rel_query = keep_head(rel_query_ref[...].reshape(2 * BUCKETS, PAIR), head)
        grad_query = dot(low_scr[...], key_scr[...], 1, 0) + dot(row_bucket, rel_key, 1, 0)
        grad_rel_key = dot(row_bucket, query, 0, 0)

        turned_scr[...] = raw_scr[...].T[:keys]
        turned_low = turned_scr[...].astype(BF16)
        cell_scr[...] = dot(turned_low, row_cells_ref[...], 1, 0)
        planar = bucket_sums(cell_scr[...], turned_planar_pos_ref[...])
        linear = band_sums(turned_scr[...], turned_linear_ref[...], turned_linear_pos_ref[...])
        key_bucket = jnp.concatenate([linear.astype(BF16), planar.astype(BF16)], axis=1)
        grad_key = dot(turned_low[:, :rows], query, 1, 0) + dot(key_bucket, rel_query, 1, 0)
        grad_value = dot(prob_ref[head], grad, 0, 0)[:keys]
        grad_rel_query = dot(key_bucket, key_scr[:keys, :], 0, 0)
        found.append((grad_query, grad_key, grad_value, grad_rel_query, grad_rel_key))

    def joined(member):
        first, second = found[0][member], found[1][member]
        return jnp.where(head_lanes(1, first.shape[0]), second, first).astype(BF16)

    grad_query_ref[...] = joined(0)
    grad_key, grad_value = joined(1), joined(2)
    for chunk in range(chunks):
        grad_kv_ref[chunk, 0] = grad_key[chunk * rows : (chunk + 1) * rows]
        grad_kv_ref[chunk, 1] = grad_value[chunk * rows : (chunk + 1) * rows]
    grad_rel_ref[0] = joined(3)
    grad_rel_ref[1] = joined(4)


def attend_back(qkv, other_kv, grad_mixed, prob, rel_key, rel_query, lookups, first, count):
    rows = qkv.shape[0]
    width = qkv.shape[1] // 3
    pairs = width // PAIR
    chunks = 1 + len(other_kv)
    keys = rows * chunks
    keys_wide = pad_lanes(keys)
    rows_wide = pad_lanes(rows)
    part = count * PAIR

    def column(offset):
        return pl.BlockSpec((rows, PAIR), lambda step: (0, offset + first + step))

    rel_spec = pl.BlockSpec((2, BUCKETS, PAIR), lambda step: (0, 0, first + step))
    small = (
        lookups["index_linear"],
        lookups["turned_linear"],
        lookups["key_cells"],
        lookups["row_cells"],
        lookups["planar_pos"],
        lookups["linear_pos"],
        lookups["turned_planar_pos"],
        lookups["turned_linear_pos"],
    )
    return pl.pallas_call(
        functools.partial(attend_back_kernel, chunks),
        grid=(count,),
        in_specs=[column(0), column(pairs)]
        + [column(0)] * (chunks - 1)
        + [column(2 * pairs)]
        + [column(pairs)] * (chunks - 1)
        + [
            column(0),
            pl.BlockSpec((2, rows, keys_wide), lambda step: (first + step, 0, 0)),
            rel_spec,
            rel_spec,
        ]
        + [whole_spec(item) for item in small],
        out_specs=[
            pl.BlockSpec((rows, PAIR), lambda step: (0, step)),
            pl.BlockSpec((chunks, 2, rows, PAIR), lambda step: (0, 0, 0, step)),
            pl.BlockSpec((2, 2 * BUCKETS, PAIR), lambda step: (0, 0, step)),
        ],
        out_shape=[
            jax.ShapeDtypeStruct((rows, part), BF16),
            jax.ShapeDtypeStruct((chunks, 2, rows, part), BF16),
            jax.ShapeDtypeStruct((2, 2 * BUCKETS, part), BF16),
        ],
        scratch_shapes=[
            pltpu.VMEM((keys_wide, PAIR), BF16),
            pltpu.VMEM((keys_wide, PAIR), BF16),
            pltpu.VMEM((rows_wide, keys_wide), F32),
            pltpu.VMEM((rows, keys_wide), BF16),
            pltpu.VMEM((keys, rows_wide), F32),
            pltpu.VMEM((keys, CELLS), F32),
        ],
        compiler_params=pltpu.CompilerParams(vmem_limit_bytes=56 << 20),
        cost_estimate=pl.CostEstimate(
            flops=80 * rows * rows * chunks * part,
            bytes_accessed=4 * count * rows * keys_wide + 24 * rows * part,
            transcendentals=0,
        ),
        name="attend_back",
    )(qkv, qkv, *other_kv, qkv, *other_kv, grad_mixed, prob, rel_key, rel_query, *small)


def make_lookups(cells_x, cells_y, count, place, row_count):
    seq_len = place.shape[0]
    keys_wide = pad_lanes(seq_len)
    rows_wide = pad_lanes(row_count)
    half_range = BUCKETS // 2

    def wide(values, total):
        return jnp.pad(values, ((0, total - values.shape[0]),))

    key_place, key_x, key_y = (wide(item, keys_wide) for item in (place, cells_x, cells_y))
    row_place, row_x, row_y = (item[:row_count] for item in (place, cells_x, cells_y))
    wide_place, wide_x, wide_y = (wide(item, rows_wide) for item in (row_place, row_x, row_y))

    def linear(i, j):
        return jnp.clip(i - j, -half_range, half_range - 1) + half_range

    def planar(ix, iy, jx, jy):
        return (jnp.clip(ix - jx, -8, 7) + 8) * 8 + jnp.clip(iy - jy, -4, 3) + 4

    out = {}
    out["index_linear"] = linear(row_place[:, None], key_place[None, :])
    out["index_planar"] = planar(row_x[:, None], row_y[:, None], key_x[None, :], key_y[None, :])
    out["turned_linear"] = linear(wide_place[None, :], place[:, None])
    out["turned_planar"] = planar(
        wide_x[None, :], wide_y[None, :], cells_x[:, None], cells_y[:, None]
    )
    valid = (place < count) | ((place >= TEXT) & (place < TEXT + PATCH))
    out["mask"] = jnp.pad(
        jnp.where(valid, 0.0, MASKED).astype(F32),
        ((0, keys_wide - seq_len),),
        constant_values=MASKED,
    )[None]
    key_live = jnp.arange(keys_wide) < seq_len
    row_live = jnp.arange(rows_wide) < row_count
    cell = jnp.arange(CELLS, dtype=jnp.int32)
    cell_x, cell_y = cell // GRID_SIDE, cell % GRID_SIDE
    out["key_cells"] = (
        key_live[:, None] & (key_x[:, None] <= cell_x) & (key_y[:, None] <= cell_y)
    ).astype(BF16)
    out["row_cells"] = (
        row_live[:, None] & (wide_x[:, None] >= cell_x) & (wide_y[:, None] >= cell_y)
    ).astype(BF16)
    bucket = jnp.arange(BUCKETS, dtype=jnp.int32)
    bucket_x, bucket_y = bucket // 8, bucket % 8
    top = GRID_SIDE - 1
    to_x = jnp.where(bucket_x == 0, top, jnp.minimum(row_x[:, None] - bucket_x + 8, top))
    to_y = jnp.where(bucket_y == 0, top, jnp.minimum(row_y[:, None] - bucket_y + 4, top))
    out["planar_pos"] = jnp.where((to_x >= 0) & (to_y >= 0), to_x * GRID_SIDE + to_y, -1)
    from_x = jnp.where(bucket_x == 0, 0, jnp.maximum(cells_x[:, None] + bucket_x - 8, 0))
    from_y = jnp.where(bucket_y == 0, 0, jnp.maximum(cells_y[:, None] + bucket_y - 4, 0))
    out["turned_planar_pos"] = jnp.where(
        (from_x <= top) & (from_y <= top), from_x * GRID_SIDE + from_y, -1
    )
    first_place = place[0]
    target = row_place[:, None] - bucket + half_range
    out["linear_pos"] = jnp.where(
        (target >= 0) & (target < seq_len), (target - first_place) % seq_len, -1
    )
    source = place[:, None] + bucket - half_range - first_place
    out["turned_linear_pos"] = jnp.where((source >= 0) & (source < row_count), source, -1)
    return out


def split_kernel(block, core_ref, values_ref, mine_ref, other_ref):
    first_core = core_ref[0] == 0
    mine, other = [], []
    for start in range(0, values_ref.shape[1], 2 * block):
        first = values_ref[:, start : start + block]
        second = values_ref[:, start + block : start + 2 * block]
        mine.append(jnp.where(first_core, first, second))
        other.append(jnp.where(first_core, second, first))
    mine_ref[...] = jnp.concatenate(mine, axis=1)
    other_ref[...] = jnp.concatenate(other, axis=1)


def split_cores(values, block, core):
    rows, columns = values.shape
    step = min(columns, 8 * max(block, LANES))
    half = jax.ShapeDtypeStruct((rows, columns // 2), values.dtype)
    return pl.pallas_call(
        functools.partial(split_kernel, block),
        grid=(columns // step,),
        in_specs=[
            pl.BlockSpec(memory_space=pltpu.SMEM),
            pl.BlockSpec((rows, step), lambda at: (0, at)),
        ],
        out_specs=[pl.BlockSpec((rows, step // 2), lambda at: (0, at))] * 2,
        out_shape=[half, half],
        cost_estimate=pl.CostEstimate(
            flops=0, bytes_accessed=4 * rows * columns, transcendentals=0
        ),
        name="split_cores",
    )(core.reshape(1), values)


def product_kernel(left_count, grad_count, steps, own, *refs):
    picks_ref = refs[0]
    lefts = refs[1 : 1 + left_count]
    grads = refs[1 + left_count : 1 + left_count + grad_count]
    outs = refs[1 + left_count + grad_count :]
    del picks_ref
    at = pl.program_id(0)
    for lead in range(left_count * grad_count):
        found = dot(lefts[lead % left_count][...], grads[lead % grad_count][...], 0, 0)
        if not own:
            outs[0][lead, 0] = found.astype(BF16)
            continue
        got_ref, sent_ref, kept_ref = outs
        total = (found + got_ref[lead, 0].astype(F32)).astype(BF16)

        @pl.when(at < steps // 2)
        def _():
            sent_ref[lead, 0] = total

        @pl.when(at >= steps // 2)
        def _():
            kept_ref[lead, 0] = total


def half_product(home, lefts, grads, got=None, place=None):
    count = lefts[0].shape[0]
    columns = grads[0].shape[1]
    leading = len(lefts) * len(grads)
    chips = home.doc_size // 2
    block = home.width // home.doc_size
    own = got is not None
    doc = lax.axis_index("doc")
    core = doc % 2
    mine = (doc >> (1 + place)) & 1 if own else core
    picks = jnp.stack([core if own else 1 - core, mine]).astype(jnp.int32)

    def chip(at, picks_ref):
        if not own:
            return at
        half = chips // 2
        inner = jnp.where(at < half, at, at - half)
        bit = jnp.where(at < half, 1 - picks_ref[1], picks_ref[1])
        low = inner & ((1 << place) - 1)
        return ((inner >> place) << (place + 1)) | (bit << place) | low

    left_spec = pl.BlockSpec(
        (count, block), lambda at, picks_ref: (0, chip(at, picks_ref) * 2 + picks_ref[0])
    )
    piece = (leading, 1, block, columns)
    in_specs = [left_spec] * len(lefts) + [
        pl.BlockSpec(item.shape, lambda at, picks_ref: (0, 0)) for item in grads
    ]
    operands = [*lefts, *grads]
    if own:
        in_specs.append(pl.BlockSpec(piece, lambda at, picks_ref: (0, chip(at, picks_ref), 0, 0)))
        operands.append(got)
        half = chips // 2
        out_specs = [
            pl.BlockSpec(piece, lambda at, picks_ref: (0, jnp.minimum(at, half - 1), 0, 0)),
            pl.BlockSpec(piece, lambda at, picks_ref: (0, jnp.maximum(at - half, 0), 0, 0)),
        ]
        out_shape = [jax.ShapeDtypeStruct((leading, half, block, columns), BF16)] * 2
    else:
        out_specs = pl.BlockSpec(piece, lambda at, picks_ref: (0, at, 0, 0))
        out_shape = jax.ShapeDtypeStruct((leading, chips, block, columns), BF16)
    return pl.pallas_call(
        functools.partial(product_kernel, len(lefts), len(grads), chips, own),
        grid_spec=pltpu.PrefetchScalarGridSpec(
            num_scalar_prefetch=1, grid=(chips,), in_specs=in_specs, out_specs=out_specs
        ),
        out_shape=out_shape,
        compiler_params=pltpu.CompilerParams(vmem_limit_bytes=40 << 20),
        cost_estimate=pl.CostEstimate(
            flops=2 * leading * chips * block * count * columns,
            bytes_accessed=(6 if own else 2) * leading * chips * block * columns,
            transcendentals=0,
        ),
        name="half_product",
    )(picks, *operands)


def panels_kernel(picks, left_count, *refs):
    lefts, grads, out_ref = refs[:left_count], refs[left_count:-1], refs[-1]
    for panel, (left, right) in enumerate(picks):

        @pl.when(pl.program_id(0) == panel)
        def _():
            out_ref[...] = dot(lefts[left][...], grads[right][...], 0, 0).astype(BF16)


def panel_products(lefts, grads, picks):
    width, columns = lefts[0].shape[1], grads[0].shape[1]
    count = lefts[0].shape[0]
    return pl.pallas_call(
        functools.partial(panels_kernel, picks, len(lefts)),
        grid=(len(picks),),
        in_specs=[
            pl.BlockSpec(item.shape, lambda at: (0, 0), pipeline_mode=pl.Buffered(1))
            for item in (*lefts, *grads)
        ],
        out_specs=pl.BlockSpec((width, columns), lambda at: (0, at)),
        out_shape=jax.ShapeDtypeStruct((width, columns * len(picks)), BF16),
        compiler_params=pltpu.CompilerParams(vmem_limit_bytes=48 << 20),
        cost_estimate=pl.CostEstimate(
            flops=2 * len(picks) * width * count * columns,
            bytes_accessed=2 * len(picks) * width * columns,
            transcendentals=0,
        ),
        name="panel_products",
    )(*lefts, *grads)


def join_kernel(block, core_ref, mine_ref, other_ref, plus_ref, out_ref):
    first_core = core_ref[0] == 0
    pieces = []
    for start in range(0, mine_ref.shape[1], block):
        mine, other = mine_ref[:, start : start + block], other_ref[:, start : start + block]
        pieces.append(jnp.where(first_core, mine, other))
        pieces.append(jnp.where(first_core, other, mine))
    out_ref[...] = jnp.concatenate(pieces, axis=1) + plus_ref[...]


def join_cores(mine, other, plus, block, core):
    rows, columns = plus.shape
    step = min(columns, 4 * max(block, LANES))
    half = pl.BlockSpec((rows, step // 2), lambda at: (0, at))
    whole = pl.BlockSpec((rows, step), lambda at: (0, at))
    return pl.pallas_call(
        functools.partial(join_kernel, block),
        grid=(columns // step,),
        in_specs=[pl.BlockSpec(memory_space=pltpu.SMEM), half, half, whole],
        out_specs=whole,
        out_shape=jax.ShapeDtypeStruct(plus.shape, F32),
        cost_estimate=pl.CostEstimate(
            flops=0, bytes_accessed=12 * rows * columns, transcendentals=0
        ),
        name="join_cores",
    )(core.reshape(1), mine, other, plus)


class Move:
    def __init__(self, got, join, hold=0):
        self.hold = hold
        self.got = got
        self.join = join
        self.value = None

    def advance(self):
        self.value = self.join(self.got)
        self.got = None

    def result(self):
        if self.got is not None:
            self.advance()
        return self.value


class Home:
    def __init__(self, mesh_shape, local_docs, block_rows, width):
        self.width = width
        self.doc_size = mesh_shape["doc"]
        self.ctx_size = mesh_shape["ctx"]
        self.block = block_rows
        self.docs = 2 * local_docs
        self.span = self.ctx_size // self.docs
        self.group = 2 * self.span
        self.rows = 2 * block_rows
        self.seq = block_rows * self.ctx_size

    def flat(self, doc, ctx):
        return doc * self.ctx_size + ctx

    def move_pairs(self, turn):
        pairs = []
        for pair in range(self.doc_size // 2):
            for core in range(2):
                for block in range(self.ctx_size):
                    slot = (block + turn) % 2
                    doc = 2 * core + slot
                    place = block // 2
                    target = self.flat(
                        2 * pair + place // self.span, doc * self.span + place % self.span
                    )
                    pairs.append((self.flat(2 * pair + core, block), target))
        return pairs

    def to_home(self, local):
        ctx = lax.axis_index("ctx")
        swap = ((ctx // self.span) % 2) == 1
        pieces = []
        for turn in range(2):
            piece = lax.dynamic_index_in_dim(local, (ctx + turn) % 2, 0, keepdims=False)
            pieces.append(lax.ppermute(piece, BOTH, self.move_pairs(turn)))

        def join(got):
            low_half = jnp.where(swap, got[1], got[0])
            high_half = jnp.where(swap, got[0], got[1])
            return jnp.concatenate([low_half, high_half], axis=0)

        return Move(pieces, join)

    def from_home(self, rows):
        ctx = lax.axis_index("ctx")
        doc_here = ctx // self.span
        swap = (ctx % 2) == 1
        halves = rows.reshape(2, self.block, rows.shape[1])
        pieces = []
        for turn in range(2):
            piece = lax.dynamic_index_in_dim(halves, (doc_here + turn) % 2, 0, keepdims=False)
            back = [(target, source) for source, target in self.move_pairs(turn)]
            pieces.append(lax.ppermute(piece, BOTH, back))

        def join(got):
            first = jnp.where(swap, got[1], got[0])
            second = jnp.where(swap, got[0], got[1])
            return jnp.stack([first, second]).astype(F32)

        return Move(pieces, join)

    def halves(self, values):
        core = lax.axis_index("doc") % 2
        return split_cores(values, self.width // self.doc_size, core)

    def join_rows(self, mine, other):
        core = lax.axis_index("doc") % 2
        columns = mine.shape[1]
        mine, other = (item.reshape(self.doc_size // 2, 1, -1, columns) for item in (mine, other))
        both = jnp.concatenate(
            [jnp.where(core == 0, mine, other), jnp.where(core == 0, other, mine)], axis=1
        )
        return both.reshape(-1, columns)

    def core_join(self, mine, other, core):
        block = self.width // self.doc_size
        pieces = []
        for start in range(0, mine.shape[1], block):
            first, second = mine[:, start : start + block], other[:, start : start + block]
            pieces.append(jnp.where(core == 0, first, second))
            pieces.append(jnp.where(core == 0, second, first))
        return jnp.concatenate(pieces, axis=1)

    def position(self):
        core = lax.axis_index("doc") % 2
        return core * self.span + lax.axis_index("ctx") % self.span

    def ring_pairs(self, shift):
        pairs = []
        for doc in range(self.doc_size):
            for ctx in range(self.ctx_size):
                place = (doc % 2) * self.span + ctx % self.span
                other = (place + shift) % self.group
                pairs.append(
                    (
                        self.flat(doc, ctx),
                        self.flat(
                            doc - doc % 2 + other // self.span,
                            ctx - ctx % self.span + other % self.span,
                        ),
                    )
                )
        return pairs

    def fetch(self, values):
        return [
            lax.ppermute(values, BOTH, self.ring_pairs(-shift)) for shift in range(1, self.group)
        ]

    def give_back(self, pieces):
        return [
            lax.ppermute(piece, BOTH, self.ring_pairs(shift))
            for shift, piece in enumerate(pieces, 1)
        ]


def to_device_order(columns, devices, shard):
    rows, hidden = columns.shape
    split = columns.reshape(rows, hidden // (devices * shard), devices, shard)
    return split.transpose(0, 2, 1, 3).reshape(rows, hidden)


def pack_first(w_qkv, tables, gains, biases, b_in):
    shard = w_qkv.shape[0]
    small = jnp.concatenate(
        [tables.reshape(-1, shard).T, gains.T, biases.T, b_in.reshape(-1, shard).T], axis=1
    )
    small = jnp.pad(small, ((0, 0), (0, pad_lanes(small.shape[1]) - small.shape[1])))
    return jnp.concatenate([w_qkv, small], axis=1)


def pack_rest(devices, w_out, w_in, w_down):
    shard, width = w_out.shape
    split = w_in.reshape(shard, devices, -1, shard).transpose(2, 0, 1, 3)
    return jnp.concatenate(
        [w_out[None], split.reshape(-1, shard, width), w_down.reshape(-1, shard, width)]
    )


def unpack_rest(packed):
    parts = (packed.shape[0] - 1) // 2
    return dict(
        out=packed[0],
        w_in=[packed[1 + part] for part in range(parts)],
        down=[packed[1 + parts + part] for part in range(parts)],
    )


class Gather:
    def __init__(self, home, block, cut):
        self.home = home
        self.hold = 0
        self.values = [block[None]]
        self.cut = cut
        high = [1 << at for at in range(1, home.doc_size.bit_length() - 1)]
        self.high = high
        self.orders = [list(high), list(reversed(high))]
        self.seen = [[], []]
        self.steps = [("ctx", 0)] + [("doc", at) for at in range(len(high))] + [("core", 0)]
        self.send()

    def send(self):
        kind, at = self.step = self.steps.pop(0)
        if kind == "doc" and len(self.values) == 1:
            value = self.values[0]
            self.values = [value[:, :, : self.cut], value[:, :, self.cut :]]
        doc_size = self.home.doc_size
        if kind == "ctx":
            size = self.home.ctx_size
            self.got = [
                lax.ppermute(self.values[0], "ctx", flips(size, far)) for far in range(1, size)
            ]
            return
        if kind == "doc":
            pairs = [("doc", flips(doc_size, order[at])) for order in self.orders]
        else:
            pairs = [("doc", flips(doc_size, 1))] * 2
        self.got = [
            lax.ppermute(value, *pair) for value, pair in zip(self.values, pairs)
        ]

    def joined(self, own, got, mine, axis):
        return jnp.stack(
            [jnp.where(mine == 0, own, got), jnp.where(mine == 0, got, own)], axis=axis
        )

    def advance(self):
        kind, at = self.step
        if kind == "ctx":
            mine = lax.axis_index("ctx")
            near = self.values + self.got
            size = self.home.ctx_size
            rows = []
            for place in range(size):
                found = near[place]
                for here in range(1, size):
                    found = jnp.where(mine == here, near[place ^ here], found)
                rows.append(found)
            self.values = [jnp.concatenate(rows, axis=0)]
        elif kind == "doc":
            values = []
            for color in range(2):
                bit = self.orders[color][at]
                mine = (lax.axis_index("doc") // bit) % 2
                axis = sum(1 for other in self.seen[color] if other > bit)
                self.seen[color].append(bit)
                values.append(self.joined(self.values[color], self.got[color], mine, axis))
            self.values = values
        else:
            self.other = [self.flat(value) for value in self.got]
            self.mine = [self.flat(value) for value in self.values]
            self.got = None
            return
        self.send()

    def flat(self, value):
        return value.reshape(-1, value.shape[-1])

    def finish(self):
        while self.got is not None:
            self.advance()
        return First(self)


class First:
    def __init__(self, gather):
        home = self.home = gather.home
        self.core = lax.axis_index("doc") % 2
        width = home.width
        cut = gather.cut
        self.cut = cut
        left = 3 * width - cut
        self.weights = [
            (half[0], half[1][:, :left]) for half in (gather.mine, gather.other)
        ]
        small = [half[1][:, left:] for half in (gather.mine, gather.other)]
        table_cols = 2 * BUCKETS
        self.tables = [half[:, :table_cols] for half in small]
        rows = [half[:, table_cols:].astype(F32).T for half in small]
        rows = home.core_join(rows[0], rows[1], self.core)
        self.gains = rows[:2]
        self.biases = rows[2:9]
        self.b_in = rows[9:]

    def project(self, rows):
        mine, other = rows
        return jnp.concatenate(
            [
                dot(mine, first, 1, 0) + dot(other, second, 1, 0)
                for first, second in zip(*self.weights)
            ],
            axis=1,
        )

    def relative(self):
        width = self.home.width
        cut = self.cut
        mine, other = self.weights
        wanted = 2 * width - cut
        return jnp.concatenate(
            [
                dot(self.tables[0], mine[0], 0, 0) + dot(self.tables[1], other[0], 0, 0),
                dot(self.tables[0], mine[1][:, :wanted], 0, 0)
                + dot(self.tables[1], other[1][:, :wanted], 0, 0),
            ],
            axis=1,
        )

    def back(self, grads, plus):
        first, second = grads[:, : self.cut], grads[:, self.cut :]
        mine, other = [
            dot(first, half[0], 1, 1) + dot(second, half[1], 1, 1) for half in self.weights
        ]
        block = self.home.width // self.home.doc_size
        return join_cores(mine, other, plus, block, self.core)

    def tables_back(self, which, query_part, key_part):
        width = self.home.width
        grads = jnp.concatenate([query_part, key_part], axis=1)
        half = self.weights[which]
        return dot(half[0], grads[:, : self.cut], 1, 1) + dot(
            half[1][:, : 2 * width - self.cut], grads[:, self.cut :], 1, 1
        )


def flips(size, bit):
    return [(index, index ^ bit) for index in range(size)]


class Scatter:
    def __init__(self, home, colors, apart):
        self.home = home
        self.apart = apart
        self.hold = 0
        self.done = []
        places = list(range(home.doc_size.bit_length() - 2))
        self.orders = [places[::-1], places]
        self.left = [places[::-1], places[::-1]]
        self.kept, self.got = [], []
        for color, pieces in enumerate(colors):
            place = self.next_place(color)
            self.kept.append([kept for _, kept in pieces])
            self.got.append([self.exchange(sent, place) for sent, _ in pieces])

    def next_place(self, color):
        place = self.orders[color].pop(0)
        self.left[color] = [item for item in self.left[color] if item != place]
        return place

    def exchange(self, sent, place):
        return lax.ppermute(sent, "doc", flips(self.home.doc_size, 2 << place))

    def send(self):
        ctx = lax.axis_index("ctx")
        self.kept, self.got = [], []
        if self.orders[0]:
            for color, value in enumerate(self.values):
                leading, chips, block, columns = value.shape
                before = self.left[color]
                place = self.next_place(color)
                axis = before.index(place)
                split = value.reshape(leading, 1 << axis, 2, -1, block, columns)
                mine = (lax.axis_index("doc") >> (1 + place)) & 1
                shape = (leading, chips // 2, block, columns)
                kept = lax.dynamic_index_in_dim(split, mine, 2, keepdims=False)
                sent = lax.dynamic_index_in_dim(split, 1 - mine, 2, keepdims=False)
                self.kept.append([kept.reshape(shape)])
                self.got.append([self.exchange(sent.reshape(shape), place)])
            return
        count = 1 if self.apart else len(self.values)
        now, self.values = self.values[:count], self.values[count:]
        size = self.home.ctx_size
        wide = jnp.concatenate(
            [value[at, 0] for value in now for at in range(value.shape[0])], axis=-1
        )
        wide = wide.reshape(size, wide.shape[0] // size, wide.shape[1])
        self.last = lax.dynamic_index_in_dim(wide, ctx, 0, keepdims=False)
        for far in range(1, size):
            sent = lax.dynamic_index_in_dim(wide, ctx ^ far, 0, keepdims=False)
            self.got.append(lax.ppermute(sent, "ctx", flips(size, far)))

    def advance(self):
        if not self.kept:
            total = self.last.astype(F32)
            for piece in self.got:
                total = total + piece.astype(F32)
            self.done.append(total)
            self.got = None
            if self.values:
                self.send()
            return
        self.values = [
            jnp.concatenate(
                [
                    (kept.astype(F32) + got.astype(F32)).astype(BF16)
                    for kept, got in zip(keeps, gots)
                ],
                axis=0,
            )
            for keeps, gots in zip(self.kept, self.got)
        ]
        self.send()

    def result(self):
        return self.done[0] if len(self.done) == 1 else jnp.concatenate(self.done, axis=1)


class Offload:
    def __init__(self, packed, axis, after=None):
        self.axis = axis
        self.packed = packed
        self.after = after
        if after is None:
            self.start()

    def start(self, values=()):
        if self.after is not None:
            self.packed, self.after.value, values = lax.optimization_barrier(
                (self.packed, self.after.value, values)
            )
        self.value = lax.psum_scatter(
            self.packed, BOTH, scatter_dimension=self.axis, tiled=True
        )
        return values

    def result(self):
        return self.value.astype(F32)


class Flight:
    def __init__(self):
        self.moving = []
        self.waiting = []

    def add(self, scatter):
        self.moving.append(scatter)

    def tick(self, values):
        self.moving = [item for item in self.moving if item.got is not None]
        ready = [item for item in self.moving if item.hold <= 0]
        got = [item.got for item in ready]
        values, got = lax.optimization_barrier((values, got))
        for item in self.moving:
            item.hold -= 1
        for item, piece in zip(ready, got):
            item.got = piece
            item.advance()
        self.moving = [item for item in self.moving if item.got is not None]
        return values


def layer_forward(home, flight, rows_in, rows_low, first, rest, fetch_next, lookups):
    width = rows_in.shape[1]
    gains, biases = first.gains, first.biases
    row_halves = home.halves(rows_low)
    qkv = (first.project(row_halves) + biases[:3].reshape(1, -1)).astype(BF16)
    qkv = fetch_next(flight.tick(qkv))
    other_kv = home.fetch(qkv[:, width:])
    rel_both = first.relative().astype(BF16)
    rel_query = rel_both[:, :width].reshape(2, BUCKETS, width)
    rel_key = rel_both[:, width:].reshape(2, BUCKETS, width)
    mixed, prob = attend(qkv, other_kv, rel_key, rel_query, lookups)
    mixed = flight.tick(mixed)
    rest = unpack_rest(rest)
    first_sum = rows_in + (dot(mixed, rest["out"], 1, 0) + biases[3])
    first_norm = norm_rows(first_sum, gains[0], biases[5])
    norm_low = first_norm.astype(BF16)
    hidden_pre = [
        dot(norm_low, panel, 1, 0) + first.b_in[part : part + 1]
        for part, panel in enumerate(rest["w_in"])
    ]
    active = [exact_gelu(item).astype(BF16) for item in hidden_pre]
    active = flight.tick(active)
    down_rows = biases[4]
    for item, panel in zip(active, rest["down"]):
        down_rows = down_rows + dot(item, panel, 1, 0)
    second_sum = first_norm + down_rows
    result = norm_rows(second_sum, gains[1], biases[6])
    result = flight.tick(result)
    kept = dict(
        rows_low=rows_low,
        row_halves=row_halves,
        qkv=qkv,
        other_kv=other_kv,
        rel_key=rel_key,
        rel_query=rel_query,
        prob=prob,
        mixed=mixed,
        first_sum=first_sum,
        norm_low=norm_low,
        hidden_pre=hidden_pre,
        active=active,
        second_sum=second_sum,
    )
    return result, kept, rest


class WholeSum:
    def __init__(self, home, lefts, grads, place):
        self.home, self.lefts, self.grads = home, lefts, grads
        self.place = place
        self.block = home.width // home.doc_size
        self.core = lax.axis_index("doc") % 2
        self.direct = self.block % LANES == 0
        if self.direct:
            sent = half_product(home, lefts, grads)
        else:
            whole = jnp.stack(
                [dot(left, item, 0, 0).astype(BF16) for left in lefts for item in grads]
            )
            self.whole = whole.reshape(
                whole.shape[0], home.doc_size // 2, 2, self.block, whole.shape[2]
            )
            sent = lax.dynamic_index_in_dim(self.whole, 1 - self.core, 2, keepdims=False)
        self.got = lax.ppermute(sent, "doc", flips(home.doc_size, 1))

    def finish(self):
        if self.direct:
            return half_product(self.home, self.lefts, self.grads, self.got, self.place)
        kept = lax.dynamic_index_in_dim(self.whole, self.core, 2, keepdims=False)
        return split_chips((kept.astype(F32) + self.got.astype(F32)).astype(BF16), self.place)


def split_chips(total, place):
    leading, chips, block, columns = total.shape
    split = total.reshape(leading, chips >> (place + 1), 2, 1 << place, block, columns)
    mine = (lax.axis_index("doc") >> (1 + place)) & 1
    sent = lax.dynamic_index_in_dim(split, 1 - mine, 2, keepdims=False)
    kept = lax.dynamic_index_in_dim(split, mine, 2, keepdims=False)
    shape = (leading, chips // 2, block, columns)
    return sent.reshape(shape), kept.reshape(shape)


class CoreSum:
    def __init__(self, home, terms):
        self.terms = terms
        self.got = lax.ppermute(self.product(1).astype(BF16), "doc", flips(home.doc_size, 1))

    def product(self, which):
        total = None
        for halves, grads, axis in self.terms:
            piece = dot(halves[which], grads, axis, 0)
            total = piece if total is None else total + piece
        return total

    def finish(self):
        return (self.product(0) + self.got.astype(F32)).astype(BF16)


def layer_backward(home, flight, grad_out, kept, first_weights, weights, lookups, offload):
    width = grad_out.shape[1]
    gains, biases = first_weights.gains, first_weights.biases
    top = home.doc_size.bit_length() - 3

    _, second_pull = jax.vjp(norm_rows, kept["second_sum"], gains[1], biases[6])
    grad_second, grad_gain_two, grad_offset_two = second_pull(grad_out)
    grad_down = grad_second.astype(BF16)
    if not offload:
        sum_down = WholeSum(home, kept["active"], [grad_down], top)
    grad_hidden = [
        (dot(grad_down, panel, 1, 1) * gelu_slope(item)).astype(BF16)
        for panel, item in zip(weights["down"], kept["hidden_pre"])
    ]
    if offload:
        grad_hidden, grad_down = flight.tick((grad_hidden, grad_down))
    else:
        grad_hidden, grad_down, sum_down.got = flight.tick((grad_hidden, grad_down, sum_down.got))
        sum_in = WholeSum(home, [kept["norm_low"]], grad_hidden, 0)
    grad_first_norm = grad_second
    for item, panel in zip(grad_hidden, weights["w_in"]):
        grad_first_norm = grad_first_norm + dot(item, panel, 1, 1)
    _, first_pull = jax.vjp(norm_rows, kept["first_sum"], gains[0], biases[5])
    grad_first, grad_gain_one, grad_offset_one = first_pull(grad_first_norm)
    grad_att = grad_first.astype(BF16)
    grad_mixed = dot(grad_att, weights["out"], 1, 1).astype(BF16)
    if offload:
        parts = len(grad_hidden)
        panels = panel_products(
            [*kept["active"], kept["norm_low"], kept["mixed"]],
            [grad_down, *grad_hidden, grad_att],
            [(part, 0) for part in range(parts)]
            + [(parts, 1 + part) for part in range(parts)]
            + [(parts + 1, parts + 1)],
        )
        early = Offload(panels, 0)
        grad_mixed = flight.tick(grad_mixed)
    else:
        sum_out = WholeSum(home, [kept["mixed"]], [grad_att], 0)
        halves_down = sum_down.finish()
        grad_mixed, halves_down, sum_in.got, sum_out.got = flight.tick(
            (grad_mixed, halves_down, sum_in.got, sum_out.got)
        )
        while flight.waiting:
            grad_mixed = flight.waiting.pop(0).start(grad_mixed)
        early = Scatter(home, [[halves_down], [sum_in.finish(), sum_out.finish()]], True)
        flight.add(early)

    pairs = width // PAIR
    found = []
    moved = []
    cuts = [0, pairs] if offload else [0, pairs // 2, 3 * pairs // 4, pairs]
    for first, count in zip(cuts, [after - at for at, after in zip(cuts, cuts[1:])]):
        grad_query, grad_kv, grad_rel = attend_back(
            kept["qkv"],
            kept["other_kv"],
            grad_mixed,
            kept["prob"],
            kept["rel_key"],
            kept["rel_query"],
            lookups,
            first,
            count,
        )
        grad_query, grad_kv, grad_rel, grad_mixed = flight.tick(
            (grad_query, grad_kv, grad_rel, grad_mixed)
        )
        moved.append(home.give_back([grad_kv[chunk] for chunk in range(1, grad_kv.shape[0])]))
        found.append((grad_query, grad_kv[0], grad_rel))

    own = []
    for (_, grad_kv, _), pieces in zip(found, moved):
        total = grad_kv.astype(F32)
        for piece in pieces:
            total = total + piece.astype(F32)
        own.append(total.astype(BF16))
    grad_qkv = jnp.concatenate(
        [item[0] for item in found] + [item[0] for item in own] + [item[1] for item in own], axis=1
    )
    rel_both = [jnp.concatenate([item[2][kind] for item in found], axis=1) for kind in range(2)]
    bias_sums = jnp.sum(grad_qkv.astype(F32), axis=0).reshape(3, width)
    small = jnp.concatenate(
        [
            grad_gain_one[None],
            grad_gain_two[None],
            bias_sums,
            jnp.sum(grad_att.astype(F32), axis=0)[None],
            jnp.sum(grad_down.astype(F32), axis=0)[None],
            grad_offset_one[None],
            grad_offset_two[None],
            *[jnp.sum(item.astype(F32), axis=0)[None] for item in grad_hidden],
        ],
        axis=0,
    )
    small_rows = small.shape[0]
    small = jnp.pad(small, ((0, pad_lanes(small_rows) - small_rows), (0, 0))).astype(BF16)

    if offload:
        rel_wide = jnp.concatenate(rel_both, axis=1)
        grad_qk = dot(kept["rows_low"], grad_qkv[:, : 2 * width], 0, 0) + dot(
            home.join_rows(*first_weights.tables), rel_wide, 1, 0
        )
        grad_v = dot(kept["rows_low"], grad_qkv[:, 2 * width :], 0, 0)
        found_tables = home.join_rows(
            *[first_weights.tables_back(which, *rel_both).astype(BF16) for which in range(2)]
        )
        late = Offload(
            jnp.concatenate(
                [grad_qk.astype(BF16), grad_v.astype(BF16), found_tables, small.T], axis=1
            ),
            0,
            early,
        )
        flight.waiting.append(late)
        grad_rows = flight.tick(first_weights.back(grad_qkv, grad_first))
        return grad_rows, (early, late)
    small_halves = home.halves(small)

    def small_half(which):
        found_tables = first_weights.tables_back(which, rel_both[0], rel_both[1])
        return jnp.concatenate([found_tables, small_halves[which].astype(F32).T], axis=1)

    small_got = lax.ppermute(small_half(1).astype(BF16), "doc", flips(home.doc_size, 1))
    row_halves = kept["row_halves"]
    sum_qk = CoreSum(
        home,
        [
            (row_halves, grad_qkv[:, : 2 * width], 0),
            (first_weights.tables, jnp.concatenate(rel_both, axis=1), 1),
        ],
    )
    sum_v = CoreSum(home, [(row_halves, grad_qkv[:, 2 * width :], 0)])
    grad_rows = first_weights.back(grad_qkv, grad_first)
    grad_rows, sum_qk.got, sum_v.got, small_got = flight.tick(
        (grad_rows, sum_qk.got, sum_v.got, small_got)
    )
    small_sum = (small_half(0) + small_got.astype(F32)).astype(BF16)
    half_qk, half_v = sum_qk.finish(), sum_v.finish()
    cut = 7 * width // 4
    half_rest = jnp.concatenate([half_qk[:, cut:], half_v, small_sum], axis=1)

    def by_chip(half):
        return half.reshape(1, home.doc_size // 2, -1, half.shape[1])

    late = Scatter(
        home,
        [[split_chips(by_chip(half_qk[:, :cut]), top)], [split_chips(by_chip(half_rest), 0)]],
        False,
    )
    flight.add(late)
    return grad_rows, (early, late)


def collect(home, scatters, width, hidden):
    devices = home.doc_size * home.ctx_size
    early, late = (item.result() for item in scatters)
    shard = early.shape[0]
    down = jnp.concatenate([early[:, at : at + width] for at in range(0, hidden, width)], axis=0)
    grad_in = to_device_order(early[:, hidden : 2 * hidden], devices, shard)
    grad_out = early[:, 2 * hidden :]
    qkv = late[:, : 3 * width]
    small = late[:, 3 * width :]
    table_cols = 2 * BUCKETS
    tables = small[:, :table_cols].T.reshape(2, BUCKETS, shard)
    rows = small[:, table_cols:].T
    gains, biases = rows[:2], rows[2:9]
    b_in = rows[9 : 9 + hidden // width].reshape(-1)
    return qkv, grad_out, grad_in, down, tables, gains, biases, b_in


def body(
    mesh_shape,
    layer_input,
    text_count,
    coords,
    w_qkv,
    w_out,
    w_in,
    w_down,
    rel_tables,
    ln_gains,
    biases,
    b_in,
    cotangent,
):
    doc_size, ctx_size = mesh_shape["doc"], mesh_shape["ctx"]
    device_count = doc_size * ctx_size
    local_docs, block_rows, width = layer_input.shape
    layer_count = w_qkv.shape[0]
    hidden = w_in.shape[2]
    home = Home(mesh_shape, local_docs, block_rows, width)

    cut = 3 * width // 2
    firsts = [
        pack_first(w_qkv[layer], rel_tables[layer], ln_gains[layer], biases[layer], b_in[layer])
        for layer in range(layer_count)
    ]
    packed = [
        pack_rest(device_count, w_out[layer], w_in[layer], w_down[layer])
        for layer in range(layer_count)
    ]

    core = lax.axis_index("doc") % 2
    doc_here = lax.axis_index("ctx") // home.span
    facts = jnp.concatenate([coords.reshape(local_docs, -1), text_count[:, None]], axis=1)
    other_facts = lax.ppermute(facts, "doc", flips(doc_size, 1))
    mine = jnp.where(
        doc_here // local_docs == core,
        lax.dynamic_index_in_dim(facts, doc_here % local_docs, 0, keepdims=False),
        lax.dynamic_index_in_dim(other_facts, doc_here % local_docs, 0, keepdims=False),
    )
    place = (jnp.arange(home.seq, dtype=jnp.int32) + home.position() * home.rows) % home.seq

    def turned(values):
        twice = jnp.concatenate([values, values])
        return lax.dynamic_slice_in_dim(twice, home.position() * home.rows, home.seq)

    lookups = make_lookups(
        turned(mine[: home.seq]),
        turned(mine[home.seq : 2 * home.seq]),
        mine[2 * home.seq],
        place,
        home.rows,
    )

    arriving = home.to_home(layer_input)
    rests = [lax.all_gather(packed[0], BOTH, axis=1, tiled=True)]

    ahead = []

    def fetch_next(values):
        if len(rests) < layer_count:
            shard, block, values = lax.optimization_barrier(
                (packed[len(rests)], firsts[len(rests)], values)
            )
            rests.append(lax.all_gather(shard, BOTH, axis=1, tiled=True))
            ahead.append(Gather(home, block, cut))
        else:
            own, values = lax.optimization_barrier((cotangent, values))
            ahead.append(home.to_home(own))
        flight.add(ahead[-1])
        return values

    first_weights = []
    rest_weights = []
    kept_all = []
    outputs = []
    flight = Flight()
    ahead.append(Gather(home, firsts[0], cut))
    gather = ahead[0]
    arriving.got, gather.got, lookups = lax.optimization_barrier(
        (arriving.got, gather.got, lookups)
    )
    rows_low = arriving.result()
    current = rows_low.astype(F32)
    for layer in range(layer_count):
        first_weights.append(ahead[layer].finish())
        current, kept, rest = layer_forward(
            home,
            flight,
            current,
            rows_low,
            first_weights[layer],
            rests[layer],
            fetch_next,
            lookups,
        )
        rest_weights.append(rest)
        rows_low = current.astype(BF16)
        outputs.append(home.from_home(rows_low))
        outputs[-1].hold = 1 if layer + 1 < layer_count else 2
        flight.add(outputs[-1])
        kept_all.append(kept)
    grad_rows = ahead[-1].result().astype(F32)
    scatters = [None] * layer_count
    for layer in reversed(range(layer_count)):
        grad_rows, scatters[layer] = layer_backward(
            home,
            flight,
            grad_rows,
            kept_all[layer],
            first_weights[layer],
            rest_weights[layer],
            lookups,
            layer > 0,
        )
    grad_input = home.from_home(grad_rows.astype(BF16))
    flight.add(grad_input)
    while flight.moving:
        flight.tick(())
    totals = [collect(home, item, width, hidden) for item in scatters]

    def stack(member):
        return jnp.stack([totals[layer][member] for layer in range(layer_count)])

    return tuple(item.result() for item in (outputs[0], outputs[-1], grad_input)) + tuple(stack(member) for member in range(8))


def solution(mesh):
    placed = (
        P("doc", "ctx", None),
        P("doc"),
        P("doc", None, None),
        P(None, BOTH, None),
        P(None, BOTH, None),
        P(None, BOTH, None),
        P(None, BOTH, None),
        P(None, None, None, BOTH),
        P(None, None, BOTH),
        P(None, None, BOTH),
        P(None, BOTH),
        P("doc", "ctx", None),
    )
    return jax.shard_map(
        functools.partial(body, dict(mesh.shape)),
        mesh=mesh,
        in_specs=placed,
        out_specs=(
            P("doc", "ctx", None),
            P("doc", "ctx", None),
            P("doc", "ctx", None),
            P(None, BOTH, None),
            P(None, BOTH, None),
            P(None, BOTH, None),
            P(None, BOTH, None),
            P(None, None, None, BOTH),
            P(None, None, BOTH),
            P(None, None, BOTH),
            P(None, BOTH),
        ),
        check_vma=False,
    )
```

```python
import functools

import jax
import jax.numpy as jnp
from jax import lax
from jax.experimental import pallas as pl
from jax.experimental.pallas import tpu as pltpu
from jax.sharding import PartitionSpec as P

HEADS = 16
HEAD_DIM = 64
BUCKETS = 128
TEXT = 512
PATCH = 49
GRID_SIDE = 32
CELLS = GRID_SIDE * GRID_SIDE
LANES = 128
PAIR = 2 * HEAD_DIM
NORM_EPSILON = 1e-05
SCORE_SCALE = (3.0 * HEAD_DIM) ** (-0.5)
MASKED = -1e30
FIXED_TOP = 16000.0
BF16 = jnp.bfloat16
F32 = jnp.float32
BOTH = ("doc", "ctx")


def pad_lanes(count):
    return -(-count // LANES) * LANES


def norm_rows(values_in, scale_gain, offset):
    centered = values_in - jnp.mean(values_in, axis=-1, keepdims=True)
    spread = jnp.mean(centered * centered, axis=-1, keepdims=True)
    return centered * lax.rsqrt(spread + NORM_EPSILON) * scale_gain + offset


def below(values_in):
    return 0.5 * lax.erf(values_in * (0.5**0.5)) + 0.5


def exact_gelu(values_in):
    return values_in * below(values_in)


def gelu_slope(values_in):
    bell = jnp.exp(-0.5 * values_in * values_in) * ((0.5 / jnp.pi) ** 0.5)
    return below(values_in) + values_in * bell


def dot(left, right, left_axis, right_axis):
    return lax.dot_general(
        left, right, (((left_axis,), (right_axis,)), ((), ())), preferred_element_type=F32
    )


def lookup(table, index):
    return jnp.take_along_axis(table, index, axis=1, mode="promise_in_bounds")


def head_lanes(head, rows):
    lane = lax.broadcasted_iota(jnp.int32, (rows, PAIR), 1)
    return (lane >= head * HEAD_DIM) & (lane < (head + 1) * HEAD_DIM)


def keep_head(values, head):
    return jnp.where(head_lanes(head, values.shape[0]), values, jnp.zeros_like(values))


def keep_both(table):
    return jnp.concatenate([keep_head(table, 0), keep_head(table, 1)], axis=0)


def paired_lookup(tables, indices):
    top = [jnp.max(jnp.abs(table)) for table in tables]
    top = jnp.maximum(jnp.maximum(top[0], top[1]), 1e-30)
    fine = FIXED_TOP / top
    total = None
    for table, index in zip(tables, indices):
        steps = jnp.round(table * fine).astype(jnp.int32)
        both = steps[:, :BUCKETS] * 65536 + steps[:, BUCKETS:]
        found = lookup(both, index)
        total = found if total is None else total + found
    coarse = top / FIXED_TOP
    first = (total + 32768) >> 16
    second = (total << 16) >> 16
    return first.astype(F32) * coarse, second.astype(F32) * coarse


def attend_kernel(
    chunks,
    q_ref,
    *refs,
):
    k_refs = refs[:chunks]
    v_refs = refs[chunks : 2 * chunks]
    (
        rel_key_ref,
        rel_query_ref,
        index_linear_ref,
        index_planar_ref,
        turned_linear_ref,
        turned_planar_ref,
        mask_ref,
        mixed_ref,
        prob_ref,
        left_scr,
        right_scr,
        value_scr,
    ) = refs[2 * chunks :]
    rows = q_ref.shape[0]
    keys = rows * chunks
    keys_wide = right_scr.shape[0]
    rows_wide = left_scr.shape[1] - PAIR

    @pl.when(pl.program_id(0) == 0)
    def _():
        row_at = lax.broadcasted_iota(jnp.int32, (rows, rows_wide), 0)
        lane_at = lax.broadcasted_iota(jnp.int32, (rows, rows_wide), 1)
        left_scr[:, PAIR:] = jnp.where(row_at == lane_at, 1.0, 0.0).astype(BF16)
        right_scr[keys:, :] = jnp.zeros((keys_wide - keys, PAIR + rows_wide), BF16)
        value_scr[keys:, :] = jnp.zeros((keys_wide - keys, PAIR), BF16)

    for chunk in range(chunks):
        right_scr[chunk * rows : (chunk + 1) * rows, :PAIR] = k_refs[chunk][...]
        value_scr[chunk * rows : (chunk + 1) * rows, :] = v_refs[chunk][...]

    query = q_ref[...]
    key = right_scr[:keys, :PAIR]
    key_bias = paired_lookup(
        [dot(key, keep_both(rel_query_ref[kind]), 1, 1) for kind in range(2)],
        [turned_linear_ref[...], turned_planar_ref[...]],
    )
    query_bias = paired_lookup(
        [dot(query, keep_both(rel_key_ref[kind]), 1, 1) for kind in range(2)],
        [index_linear_ref[...], index_planar_ref[...]],
    )
    mixed = []
    for head in range(2):
        left_scr[:, :PAIR] = keep_head(query, head)
        right_scr[:keys, PAIR:] = key_bias[head].astype(BF16)
        raw = dot(left_scr[...], right_scr[...], 1, 1) + query_bias[head]
        scaled = raw * SCORE_SCALE + mask_ref[...]
        shifted = scaled - jnp.max(scaled, axis=-1, keepdims=True)
        exponent = jnp.exp(shifted)
        inverse = 1.0 / jnp.sum(exponent, axis=-1, keepdims=True)
        prob = (exponent * inverse).astype(BF16)
        prob_ref[head] = prob
        mixed.append(dot(prob, value_scr[...], 1, 0))
    mixed_ref[...] = jnp.where(head_lanes(1, rows), mixed[1], mixed[0]).astype(BF16)


def whole_spec(array):
    return pl.BlockSpec(array.shape, lambda step: (0,) * array.ndim)


def attend(qkv, other_kv, rel_key, rel_query, lookups):
    rows = qkv.shape[0]
    width = qkv.shape[1] // 3
    pairs = width // PAIR
    chunks = 1 + len(other_kv)
    keys_wide = pad_lanes(rows * chunks)
    rows_wide = pad_lanes(rows)

    def column(offset):
        return pl.BlockSpec((rows, PAIR), lambda step: (0, offset + step))

    rel_spec = pl.BlockSpec((2, BUCKETS, PAIR), lambda step: (0, 0, step))
    small = (
        lookups["index_linear"],
        lookups["index_planar"],
        lookups["turned_linear"],
        lookups["turned_planar"],
        lookups["mask"],
    )
    return pl.pallas_call(
        functools.partial(attend_kernel, chunks),
        grid=(pairs,),
        in_specs=[column(0), column(pairs)]
        + [column(0)] * (chunks - 1)
        + [column(2 * pairs)]
        + [column(pairs)] * (chunks - 1)
        + [rel_spec, rel_spec]
        + [whole_spec(item) for item in small],
        out_specs=[
            pl.BlockSpec((rows, PAIR), lambda step: (0, step)),
            pl.BlockSpec((2, rows, keys_wide), lambda step: (step, 0, 0)),
        ],
        out_shape=[
            jax.ShapeDtypeStruct((rows, width), BF16),
            jax.ShapeDtypeStruct((2 * pairs, rows, keys_wide), BF16),
        ],
        scratch_shapes=[
            pltpu.VMEM((rows, PAIR + rows_wide), BF16),
            pltpu.VMEM((keys_wide, PAIR + rows_wide), BF16),
            pltpu.VMEM((keys_wide, PAIR), BF16),
        ],
        compiler_params=pltpu.CompilerParams(vmem_limit_bytes=40 << 20),
        cost_estimate=pl.CostEstimate(
            flops=20 * rows * rows * chunks * width,
            bytes_accessed=4 * pairs * rows * keys_wide + 8 * rows * width,
            transcendentals=2 * pairs * rows * keys_wide,
        ),
        name="attend",
    )(qkv, qkv, *other_kv, qkv, *other_kv, rel_key, rel_query, *small)


def bucket_sums(cells, pos):
    spot = pos & (LANES - 1)
    part = pos >> 7
    total = jnp.zeros(spot.shape, F32)
    for chunk in range(CELLS // LANES):
        total = jnp.where(
            part == chunk, lookup(cells[:, chunk * LANES : (chunk + 1) * LANES], spot), total
        )
    lane = lax.broadcasted_iota(jnp.int32, total.shape, 1)
    total = total - jnp.where(lane < BUCKETS - 8, pltpu.roll(total, BUCKETS - 8, 1), 0.0)
    return total - jnp.where((lane & 7) < 7, pltpu.roll(total, BUCKETS - 1, 1), 0.0)


def band_sums(values, index, pos):
    spot = pos & (LANES - 1)
    part = pos >> 7
    total = jnp.zeros(spot.shape, F32)
    for chunk in range(values.shape[1] // LANES):
        total = jnp.where(
            part == chunk, lookup(values[:, chunk * LANES : (chunk + 1) * LANES], spot), total
        )
    low = jnp.sum(jnp.where(index == 0, values, 0.0), axis=-1, keepdims=True)
    high = jnp.sum(jnp.where(index == BUCKETS - 1, values, 0.0), axis=-1, keepdims=True)
    lane = lax.broadcasted_iota(jnp.int32, total.shape, 1)
    return jnp.where(lane == 0, low, jnp.where(lane == BUCKETS - 1, high, total))


def attend_back_kernel(
    chunks,
    q_ref,
    *refs,
):
    k_refs = refs[:chunks]
    v_refs = refs[chunks : 2 * chunks]
    (
        grad_ref,
        prob_ref,
        rel_key_ref,
        rel_query_ref,
        index_linear_ref,
        turned_linear_ref,
        key_cells_ref,
        row_cells_ref,
        planar_pos_ref,
        linear_pos_ref,
        turned_planar_pos_ref,
        turned_linear_pos_ref,
        grad_query_ref,
        grad_kv_ref,
        grad_rel_ref,
        key_scr,
        value_scr,
        raw_scr,
        low_scr,
        turned_scr,
        cell_scr,
    ) = refs[2 * chunks :]
    rows = q_ref.shape[0]
    keys = rows * chunks
    keys_wide = key_scr.shape[0]
    rows_wide = raw_scr.shape[0]

    @pl.when(pl.program_id(0) == 0)
    def _():
        key_scr[keys:, :] = jnp.zeros((keys_wide - keys, PAIR), BF16)
        value_scr[keys:, :] = jnp.zeros((keys_wide - keys, PAIR), BF16)
        raw_scr[rows:, :] = jnp.zeros((rows_wide - rows, keys_wide), F32)

    for chunk in range(chunks):
        key_scr[chunk * rows : (chunk + 1) * rows, :] = k_refs[chunk][...]
        value_scr[chunk * rows : (chunk + 1) * rows, :] = v_refs[chunk][...]

    found = []
    for head in range(2):
        query = keep_head(q_ref[...], head)
        grad = keep_head(grad_ref[...], head)
        raw_scr[:rows, :] = dot(grad, value_scr[...], 1, 1)
        prob = prob_ref[head].astype(F32)
        grad_prob = raw_scr[:rows, :]
        inner = jnp.sum(prob * grad_prob, axis=-1, keepdims=True)
        grad_raw = (prob * (grad_prob - inner) * SCORE_SCALE).astype(BF16)
        low_scr[...] = grad_raw
        raw_scr[:rows, :] = grad_raw.astype(F32)

        cell_scr[:rows, :] = dot(low_scr[...], key_cells_ref[...], 1, 0)
        planar = bucket_sums(cell_scr[:rows, :], planar_pos_ref[...])
        linear = band_sums(raw_scr[:rows, :], index_linear_ref[...], linear_pos_ref[...])
        row_bucket = jnp.concatenate([linear.astype(BF16), planar.astype(BF16)], axis=1)
        rel_key = keep_head(rel_key_ref[...].reshape(2 * BUCKETS, PAIR), head)
        rel_query = keep_head(rel_query_ref[...].reshape(2 * BUCKETS, PAIR), head)
        grad_query = dot(low_scr[...], key_scr[...], 1, 0) + dot(row_bucket, rel_key, 1, 0)
        grad_rel_key = dot(row_bucket, query, 0, 0)

        turned_scr[...] = raw_scr[...].T[:keys]
        turned_low = turned_scr[...].astype(BF16)
        cell_scr[...] = dot(turned_low, row_cells_ref[...], 1, 0)
        planar = bucket_sums(cell_scr[...], turned_planar_pos_ref[...])
        linear = band_sums(turned_scr[...], turned_linear_ref[...], turned_linear_pos_ref[...])
        key_bucket = jnp.concatenate([linear.astype(BF16), planar.astype(BF16)], axis=1)
        grad_key = dot(turned_low[:, :rows], query, 1, 0) + dot(key_bucket, rel_query, 1, 0)
        grad_value = dot(prob_ref[head], grad, 0, 0)[:keys]
        grad_rel_query = dot(key_bucket, key_scr[:keys, :], 0, 0)
        found.append((grad_query, grad_key, grad_value, grad_rel_query, grad_rel_key))

    def joined(member):
        first, second = found[0][member], found[1][member]
        return jnp.where(head_lanes(1, first.shape[0]), second, first).astype(BF16)

    grad_query_ref[...] = joined(0)
    grad_key, grad_value = joined(1), joined(2)
    for chunk in range(chunks):
        grad_kv_ref[chunk, 0] = grad_key[chunk * rows : (chunk + 1) * rows]
        grad_kv_ref[chunk, 1] = grad_value[chunk * rows : (chunk + 1) * rows]
    grad_rel_ref[0] = joined(3)
    grad_rel_ref[1] = joined(4)


def attend_back(qkv, other_kv, grad_mixed, prob, rel_key, rel_query, lookups, first, count):
    rows = qkv.shape[0]
    width = qkv.shape[1] // 3
    pairs = width // PAIR
    chunks = 1 + len(other_kv)
    keys = rows * chunks
    keys_wide = pad_lanes(keys)
    rows_wide = pad_lanes(rows)
    part = count * PAIR

    def column(offset):
        return pl.BlockSpec((rows, PAIR), lambda step: (0, offset + first + step))

    rel_spec = pl.BlockSpec((2, BUCKETS, PAIR), lambda step: (0, 0, first + step))
    small = (
        lookups["index_linear"],
        lookups["turned_linear"],
        lookups["key_cells"],
        lookups["row_cells"],
        lookups["planar_pos"],
        lookups["linear_pos"],
        lookups["turned_planar_pos"],
        lookups["turned_linear_pos"],
    )
    return pl.pallas_call(
        functools.partial(attend_back_kernel, chunks),
        grid=(count,),
        in_specs=[column(0), column(pairs)]
        + [column(0)] * (chunks - 1)
        + [column(2 * pairs)]
        + [column(pairs)] * (chunks - 1)
        + [
            column(0),
            pl.BlockSpec((2, rows, keys_wide), lambda step: (first + step, 0, 0)),
            rel_spec,
            rel_spec,
        ]
        + [whole_spec(item) for item in small],
        out_specs=[
            pl.BlockSpec((rows, PAIR), lambda step: (0, step)),
            pl.BlockSpec((chunks, 2, rows, PAIR), lambda step: (0, 0, 0, step)),
            pl.BlockSpec((2, 2 * BUCKETS, PAIR), lambda step: (0, 0, step)),
        ],
        out_shape=[
            jax.ShapeDtypeStruct((rows, part), BF16),
            jax.ShapeDtypeStruct((chunks, 2, rows, part), BF16),
            jax.ShapeDtypeStruct((2, 2 * BUCKETS, part), BF16),
        ],
        scratch_shapes=[
            pltpu.VMEM((keys_wide, PAIR), BF16),
            pltpu.VMEM((keys_wide, PAIR), BF16),
            pltpu.VMEM((rows_wide, keys_wide), F32),
            pltpu.VMEM((rows, keys_wide), BF16),
            pltpu.VMEM((keys, rows_wide), F32),
            pltpu.VMEM((keys, CELLS), F32),
        ],
        compiler_params=pltpu.CompilerParams(vmem_limit_bytes=56 << 20),
        cost_estimate=pl.CostEstimate(
            flops=80 * rows * rows * chunks * part,
            bytes_accessed=4 * count * rows * keys_wide + 24 * rows * part,
            transcendentals=0,
        ),
        name="attend_back",
    )(qkv, qkv, *other_kv, qkv, *other_kv, grad_mixed, prob, rel_key, rel_query, *small)


def make_lookups(cells_x, cells_y, count, place, row_count):
    seq_len = place.shape[0]
    keys_wide = pad_lanes(seq_len)
    rows_wide = pad_lanes(row_count)
    half_range = BUCKETS // 2

    def wide(values, total):
        return jnp.pad(values, ((0, total - values.shape[0]),))

    key_place, key_x, key_y = (wide(item, keys_wide) for item in (place, cells_x, cells_y))
    row_place, row_x, row_y = (item[:row_count] for item in (place, cells_x, cells_y))
    wide_place, wide_x, wide_y = (wide(item, rows_wide) for item in (row_place, row_x, row_y))

    def linear(i, j):
        return jnp.clip(i - j, -half_range, half_range - 1) + half_range

    def planar(ix, iy, jx, jy):
        return (jnp.clip(ix - jx, -8, 7) + 8) * 8 + jnp.clip(iy - jy, -4, 3) + 4

    out = {}
    out["index_linear"] = linear(row_place[:, None], key_place[None, :])
    out["index_planar"] = planar(row_x[:, None], row_y[:, None], key_x[None, :], key_y[None, :])
    out["turned_linear"] = linear(wide_place[None, :], place[:, None])
    out["turned_planar"] = planar(
        wide_x[None, :], wide_y[None, :], cells_x[:, None], cells_y[:, None]
    )
    valid = (place < count) | ((place >= TEXT) & (place < TEXT + PATCH))
    out["mask"] = jnp.pad(
        jnp.where(valid, 0.0, MASKED).astype(F32),
        ((0, keys_wide - seq_len),),
        constant_values=MASKED,
    )[None]
    key_live = jnp.arange(keys_wide) < seq_len
    row_live = jnp.arange(rows_wide) < row_count
    cell = jnp.arange(CELLS, dtype=jnp.int32)
    cell_x, cell_y = cell // GRID_SIDE, cell % GRID_SIDE
    out["key_cells"] = (
        key_live[:, None] & (key_x[:, None] <= cell_x) & (key_y[:, None] <= cell_y)
    ).astype(BF16)
    out["row_cells"] = (
        row_live[:, None] & (wide_x[:, None] >= cell_x) & (wide_y[:, None] >= cell_y)
    ).astype(BF16)
    bucket = jnp.arange(BUCKETS, dtype=jnp.int32)
    bucket_x, bucket_y = bucket // 8, bucket % 8
    top = GRID_SIDE - 1
    to_x = jnp.where(bucket_x == 0, top, jnp.minimum(row_x[:, None] - bucket_x + 8, top))
    to_y = jnp.where(bucket_y == 0, top, jnp.minimum(row_y[:, None] - bucket_y + 4, top))
    out["planar_pos"] = jnp.where((to_x >= 0) & (to_y >= 0), to_x * GRID_SIDE + to_y, -1)
    from_x = jnp.where(bucket_x == 0, 0, jnp.maximum(cells_x[:, None] + bucket_x - 8, 0))
    from_y = jnp.where(bucket_y == 0, 0, jnp.maximum(cells_y[:, None] + bucket_y - 4, 0))
    out["turned_planar_pos"] = jnp.where(
        (from_x <= top) & (from_y <= top), from_x * GRID_SIDE + from_y, -1
    )
    first_place = place[0]
    target = row_place[:, None] - bucket + half_range
    out["linear_pos"] = jnp.where(
        (target >= 0) & (target < seq_len), (target - first_place) % seq_len, -1
    )
    source = place[:, None] + bucket - half_range - first_place
    out["turned_linear_pos"] = jnp.where((source >= 0) & (source < row_count), source, -1)
    return out


def split_kernel(block, core_ref, values_ref, mine_ref, other_ref):
    first_core = core_ref[0] == 0
    mine, other = [], []
    for start in range(0, values_ref.shape[1], 2 * block):
        first = values_ref[:, start : start + block]
        second = values_ref[:, start + block : start + 2 * block]
        mine.append(jnp.where(first_core, first, second))
        other.append(jnp.where(first_core, second, first))
    mine_ref[...] = jnp.concatenate(mine, axis=1)
    other_ref[...] = jnp.concatenate(other, axis=1)


def split_cores(values, block, core):
    rows, columns = values.shape
    step = min(columns, 8 * max(block, LANES))
    half = jax.ShapeDtypeStruct((rows, columns // 2), values.dtype)
    return pl.pallas_call(
        functools.partial(split_kernel, block),
        grid=(columns // step,),
        in_specs=[
            pl.BlockSpec(memory_space=pltpu.SMEM),
            pl.BlockSpec((rows, step), lambda at: (0, at)),
        ],
        out_specs=[pl.BlockSpec((rows, step // 2), lambda at: (0, at))] * 2,
        out_shape=[half, half],
        cost_estimate=pl.CostEstimate(
            flops=0, bytes_accessed=4 * rows * columns, transcendentals=0
        ),
        name="split_cores",
    )(core.reshape(1), values)


def product_kernel(left_count, grad_count, steps, own, *refs):
    picks_ref = refs[0]
    lefts = refs[1 : 1 + left_count]
    grads = refs[1 + left_count : 1 + left_count + grad_count]
    outs = refs[1 + left_count + grad_count :]
    del picks_ref
    at = pl.program_id(0)
    for lead in range(left_count * grad_count):
        found = dot(lefts[lead % left_count][...], grads[lead % grad_count][...], 0, 0)
        if not own:
            outs[0][lead, 0] = found.astype(BF16)
            continue
        got_ref, sent_ref, kept_ref = outs
        total = (found + got_ref[lead, 0].astype(F32)).astype(BF16)

        @pl.when(at < steps // 2)
        def _():
            sent_ref[lead, 0] = total

        @pl.when(at >= steps // 2)
        def _():
            kept_ref[lead, 0] = total


def half_product(home, lefts, grads, got=None, place=None):
    count = lefts[0].shape[0]
    columns = grads[0].shape[1]
    leading = len(lefts) * len(grads)
    chips = home.doc_size // 2
    block = home.width // home.doc_size
    own = got is not None
    doc = lax.axis_index("doc")
    core = doc % 2
    mine = (doc >> (1 + place)) & 1 if own else core
    picks = jnp.stack([core if own else 1 - core, mine]).astype(jnp.int32)

    def chip(at, picks_ref):
        if not own:
            return at
        half = chips // 2
        inner = jnp.where(at < half, at, at - half)
        bit = jnp.where(at < half, 1 - picks_ref[1], picks_ref[1])
        low = inner & ((1 << place) - 1)
        return ((inner >> place) << (place + 1)) | (bit << place) | low

    left_spec = pl.BlockSpec(
        (count, block), lambda at, picks_ref: (0, chip(at, picks_ref) * 2 + picks_ref[0])
    )
    piece = (leading, 1, block, columns)
    in_specs = [left_spec] * len(lefts) + [
        pl.BlockSpec(item.shape, lambda at, picks_ref: (0, 0)) for item in grads
    ]
    operands = [*lefts, *grads]
    if own:
        in_specs.append(pl.BlockSpec(piece, lambda at, picks_ref: (0, chip(at, picks_ref), 0, 0)))
        operands.append(got)
        half = chips // 2
        out_specs = [
            pl.BlockSpec(piece, lambda at, picks_ref: (0, jnp.minimum(at, half - 1), 0, 0)),
            pl.BlockSpec(piece, lambda at, picks_ref: (0, jnp.maximum(at - half, 0), 0, 0)),
        ]
        out_shape = [jax.ShapeDtypeStruct((leading, half, block, columns), BF16)] * 2
    else:
        out_specs = pl.BlockSpec(piece, lambda at, picks_ref: (0, at, 0, 0))
        out_shape = jax.ShapeDtypeStruct((leading, chips, block, columns), BF16)
    return pl.pallas_call(
        functools.partial(product_kernel, len(lefts), len(grads), chips, own),
        grid_spec=pltpu.PrefetchScalarGridSpec(
            num_scalar_prefetch=1, grid=(chips,), in_specs=in_specs, out_specs=out_specs
        ),
        out_shape=out_shape,
        compiler_params=pltpu.CompilerParams(vmem_limit_bytes=40 << 20),
        cost_estimate=pl.CostEstimate(
            flops=2 * leading * chips * block * count * columns,
            bytes_accessed=(6 if own else 2) * leading * chips * block * columns,
            transcendentals=0,
        ),
        name="half_product",
    )(picks, *operands)


def panels_kernel(picks, left_count, *refs):
    lefts, grads, out_ref = refs[:left_count], refs[left_count:-1], refs[-1]
    for panel, (left, right) in enumerate(picks):

        @pl.when(pl.program_id(0) == panel)
        def _():
            out_ref[...] = dot(lefts[left][...], grads[right][...], 0, 0).astype(BF16)


def panel_products(lefts, grads, picks):
    width, columns = lefts[0].shape[1], grads[0].shape[1]
    count = lefts[0].shape[0]
    return pl.pallas_call(
        functools.partial(panels_kernel, picks, len(lefts)),
        grid=(len(picks),),
        in_specs=[
            pl.BlockSpec(item.shape, lambda at: (0, 0), pipeline_mode=pl.Buffered(1))
            for item in (*lefts, *grads)
        ],
        out_specs=pl.BlockSpec((width, columns), lambda at: (0, at)),
        out_shape=jax.ShapeDtypeStruct((width, columns * len(picks)), BF16),
        compiler_params=pltpu.CompilerParams(vmem_limit_bytes=48 << 20),
        cost_estimate=pl.CostEstimate(
            flops=2 * len(picks) * width * count * columns,
            bytes_accessed=2 * len(picks) * width * columns,
            transcendentals=0,
        ),
        name="panel_products",
    )(*lefts, *grads)


def join_kernel(block, core_ref, mine_ref, other_ref, plus_ref, out_ref):
    first_core = core_ref[0] == 0
    pieces = []
    for start in range(0, mine_ref.shape[1], block):
        mine, other = mine_ref[:, start : start + block], other_ref[:, start : start + block]
        pieces.append(jnp.where(first_core, mine, other))
        pieces.append(jnp.where(first_core, other, mine))
    out_ref[...] = jnp.concatenate(pieces, axis=1) + plus_ref[...]


def join_cores(mine, other, plus, block, core):
    rows, columns = plus.shape
    step = min(columns, 4 * max(block, LANES))
    half = pl.BlockSpec((rows, step // 2), lambda at: (0, at))
    whole = pl.BlockSpec((rows, step), lambda at: (0, at))
    return pl.pallas_call(
        functools.partial(join_kernel, block),
        grid=(columns // step,),
        in_specs=[pl.BlockSpec(memory_space=pltpu.SMEM), half, half, whole],
        out_specs=whole,
        out_shape=jax.ShapeDtypeStruct(plus.shape, F32),
        cost_estimate=pl.CostEstimate(
            flops=0, bytes_accessed=12 * rows * columns, transcendentals=0
        ),
        name="join_cores",
    )(core.reshape(1), mine, other, plus)


class Move:
    def __init__(self, got, join, hold=0):
        self.hold = hold
        self.got = got
        self.join = join
        self.value = None

    def advance(self):
        self.value = self.join(self.got)
        self.got = None

    def result(self):
        if self.got is not None:
            self.advance()
        return self.value


class Home:
    def __init__(self, mesh_shape, local_docs, block_rows, width):
        self.width = width
        self.doc_size = mesh_shape["doc"]
        self.ctx_size = mesh_shape["ctx"]
        self.block = block_rows
        self.docs = 2 * local_docs
        self.span = self.ctx_size // self.docs
        self.group = 2 * self.span
        self.rows = 2 * block_rows
        self.seq = block_rows * self.ctx_size

    def flat(self, doc, ctx):
        return doc * self.ctx_size + ctx

    def move_pairs(self, turn):
        pairs = []
        for pair in range(self.doc_size // 2):
            for core in range(2):
                for block in range(self.ctx_size):
                    slot = (block + turn) % 2
                    doc = 2 * core + slot
                    place = block // 2
                    target = self.flat(
                        2 * pair + place // self.span, doc * self.span + place % self.span
                    )
                    pairs.append((self.flat(2 * pair + core, block), target))
        return pairs

    def to_home(self, local):
        ctx = lax.axis_index("ctx")
        swap = ((ctx // self.span) % 2) == 1
        pieces = []
        for turn in range(2):
            piece = lax.dynamic_index_in_dim(local, (ctx + turn) % 2, 0, keepdims=False)
            pieces.append(lax.ppermute(piece, BOTH, self.move_pairs(turn)))

        def join(got):
            low_half = jnp.where(swap, got[1], got[0])
            high_half = jnp.where(swap, got[0], got[1])
            return jnp.concatenate([low_half, high_half], axis=0)

        return Move(pieces, join)

    def from_home(self, rows):
        ctx = lax.axis_index("ctx")
        doc_here = ctx // self.span
        swap = (ctx % 2) == 1
        halves = rows.reshape(2, self.block, rows.shape[1])
        pieces = []
        for turn in range(2):
            piece = lax.dynamic_index_in_dim(halves, (doc_here + turn) % 2, 0, keepdims=False)
            back = [(target, source) for source, target in self.move_pairs(turn)]
            pieces.append(lax.ppermute(piece, BOTH, back))

        def join(got):
            first = jnp.where(swap, got[1], got[0])
            second = jnp.where(swap, got[0], got[1])
            return jnp.stack([first, second]).astype(F32)

        return Move(pieces, join)

    def halves(self, values):
        core = lax.axis_index("doc") % 2
        return split_cores(values, self.width // self.doc_size, core)

    def join_rows(self, mine, other):
        core = lax.axis_index("doc") % 2
        columns = mine.shape[1]
        mine, other = (item.reshape(self.doc_size // 2, 1, -1, columns) for item in (mine, other))
        both = jnp.concatenate(
            [jnp.where(core == 0, mine, other), jnp.where(core == 0, other, mine)], axis=1
        )
        return both.reshape(-1, columns)

    def core_join(self, mine, other, core):
        block = self.width // self.doc_size
        pieces = []
        for start in range(0, mine.shape[1], block):
            first, second = mine[:, start : start + block], other[:, start : start + block]
            pieces.append(jnp.where(core == 0, first, second))
            pieces.append(jnp.where(core == 0, second, first))
        return jnp.concatenate(pieces, axis=1)

    def position(self):
        core = lax.axis_index("doc") % 2
        return core * self.span + lax.axis_index("ctx") % self.span

    def ring_pairs(self, shift):
        pairs = []
        for doc in range(self.doc_size):
            for ctx in range(self.ctx_size):
                place = (doc % 2) * self.span + ctx % self.span
                other = (place + shift) % self.group
                pairs.append(
                    (
                        self.flat(doc, ctx),
                        self.flat(
                            doc - doc % 2 + other // self.span,
                            ctx - ctx % self.span + other % self.span,
                        ),
                    )
                )
        return pairs

    def fetch(self, values):
        return [
            lax.ppermute(values, BOTH, self.ring_pairs(-shift)) for shift in range(1, self.group)
        ]

    def give_back(self, pieces):
        return [
            lax.ppermute(piece, BOTH, self.ring_pairs(shift))
            for shift, piece in enumerate(pieces, 1)
        ]


def to_device_order(columns, devices, shard):
    rows, hidden = columns.shape
    split = columns.reshape(rows, hidden // (devices * shard), devices, shard)
    return split.transpose(0, 2, 1, 3).reshape(rows, hidden)


def pack_first(w_qkv, tables, gains, biases, b_in):
    shard = w_qkv.shape[0]
    small = jnp.concatenate(
        [tables.reshape(-1, shard).T, gains.T, biases.T, b_in.reshape(-1, shard).T], axis=1
    )
    small = jnp.pad(small, ((0, 0), (0, pad_lanes(small.shape[1]) - small.shape[1])))
    return jnp.concatenate([w_qkv, small], axis=1)


def pack_rest(devices, w_out, w_in, w_down):
    shard, width = w_out.shape
    split = w_in.reshape(shard, devices, -1, shard).transpose(2, 0, 1, 3)
    return jnp.concatenate(
        [w_out[None], split.reshape(-1, shard, width), w_down.reshape(-1, shard, width)]
    )


def unpack_rest(packed):
    parts = (packed.shape[0] - 1) // 2
    return dict(
        out=packed[0],
        w_in=[packed[1 + part] for part in range(parts)],
        down=[packed[1 + parts + part] for part in range(parts)],
    )


class Gather:
    def __init__(self, home, block, cut):
        self.home = home
        self.hold = 0
        self.values = [block[None]]
        self.cut = cut
        high = [1 << at for at in range(1, home.doc_size.bit_length() - 1)]
        self.high = high
        self.orders = [list(high), list(reversed(high))]
        self.seen = [[], []]
        self.steps = [("ctx", 0)] + [("doc", at) for at in range(len(high))] + [("core", 0)]
        self.send()

    def send(self):
        kind, at = self.step = self.steps.pop(0)
        if kind == "doc" and len(self.values) == 1:
            value = self.values[0]
            self.values = [value[:, :, : self.cut], value[:, :, self.cut :]]
        doc_size = self.home.doc_size
        if kind == "ctx":
            size = self.home.ctx_size
            self.got = [
                lax.ppermute(self.values[0], "ctx", flips(size, far)) for far in range(1, size)
            ]
            return
        if kind == "doc":
            pairs = [("doc", flips(doc_size, order[at])) for order in self.orders]
        else:
            pairs = [("doc", flips(doc_size, 1))] * 2
        self.got = [
            lax.ppermute(value, *pair) for value, pair in zip(self.values, pairs)
        ]

    def joined(self, own, got, mine, axis):
        return jnp.stack(
            [jnp.where(mine == 0, own, got), jnp.where(mine == 0, got, own)], axis=axis
        )

    def advance(self):
        kind, at = self.step
        if kind == "ctx":
            mine = lax.axis_index("ctx")
            near = self.values + self.got
            size = self.home.ctx_size
            rows = []
            for place in range(size):
                found = near[place]
                for here in range(1, size):
                    found = jnp.where(mine == here, near[place ^ here], found)
                rows.append(found)
            self.values = [jnp.concatenate(rows, axis=0)]
        elif kind == "doc":
            values = []
            for color in range(2):
                bit = self.orders[color][at]
                mine = (lax.axis_index("doc") // bit) % 2
                axis = sum(1 for other in self.seen[color] if other > bit)
                self.seen[color].append(bit)
                values.append(self.joined(self.values[color], self.got[color], mine, axis))
            self.values = values
        else:
            self.other = [self.flat(value) for value in self.got]
            self.mine = [self.flat(value) for value in self.values]
            self.got = None
            return
        self.send()

    def flat(self, value):
        return value.reshape(-1, value.shape[-1])

    def finish(self):
        while self.got is not None:
            self.advance()
        return First(self)


class First:
    def __init__(self, gather):
        home = self.home = gather.home
        self.core = lax.axis_index("doc") % 2
        width = home.width
        cut = gather.cut
        self.cut = cut
        left = 3 * width - cut
        self.weights = [
            (half[0], half[1][:, :left]) for half in (gather.mine, gather.other)
        ]
        small = [half[1][:, left:] for half in (gather.mine, gather.other)]
        table_cols = 2 * BUCKETS
        self.tables = [half[:, :table_cols] for half in small]
        rows = [half[:, table_cols:].astype(F32).T for half in small]
        rows = home.core_join(rows[0], rows[1], self.core)
        self.gains = rows[:2]
        self.biases = rows[2:9]
        self.b_in = rows[9:]

    def project(self, rows):
        mine, other = rows
        return jnp.concatenate(
            [
                dot(mine, first, 1, 0) + dot(other, second, 1, 0)
                for first, second in zip(*self.weights)
            ],
            axis=1,
        )

    def relative(self):
        width = self.home.width
        cut = self.cut
        mine, other = self.weights
        wanted = 2 * width - cut
        return jnp.concatenate(
            [
                dot(self.tables[0], mine[0], 0, 0) + dot(self.tables[1], other[0], 0, 0),
                dot(self.tables[0], mine[1][:, :wanted], 0, 0)
                + dot(self.tables[1], other[1][:, :wanted], 0, 0),
            ],
            axis=1,
        )

    def back(self, grads, plus):
        first, second = grads[:, : self.cut], grads[:, self.cut :]
        mine, other = [
            dot(first, half[0], 1, 1) + dot(second, half[1], 1, 1) for half in self.weights
        ]
        block = self.home.width // self.home.doc_size
        return join_cores(mine, other, plus, block, self.core)

    def tables_back(self, which, query_part, key_part):
        width = self.home.width
        grads = jnp.concatenate([query_part, key_part], axis=1)
        half = self.weights[which]
        return dot(half[0], grads[:, : self.cut], 1, 1) + dot(
            half[1][:, : 2 * width - self.cut], grads[:, self.cut :], 1, 1
        )


def flips(size, bit):
    return [(index, index ^ bit) for index in range(size)]


class Scatter:
    def __init__(self, home, colors, apart):
        self.home = home
        self.apart = apart
        self.hold = 0
        self.done = []
        places = list(range(home.doc_size.bit_length() - 2))
        self.orders = [places[::-1], places]
        self.left = [places[::-1], places[::-1]]
        self.kept, self.got = [], []
        for color, pieces in enumerate(colors):
            place = self.next_place(color)
            self.kept.append([kept for _, kept in pieces])
            self.got.append([self.exchange(sent, place) for sent, _ in pieces])

    def next_place(self, color):
        place = self.orders[color].pop(0)
        self.left[color] = [item for item in self.left[color] if item != place]
        return place

    def exchange(self, sent, place):
        return lax.ppermute(sent, "doc", flips(self.home.doc_size, 2 << place))

    def send(self):
        ctx = lax.axis_index("ctx")
        self.kept, self.got = [], []
        if self.orders[0]:
            for color, value in enumerate(self.values):
                leading, chips, block, columns = value.shape
                before = self.left[color]
                place = self.next_place(color)
                axis = before.index(place)
                split = value.reshape(leading, 1 << axis, 2, -1, block, columns)
                mine = (lax.axis_index("doc") >> (1 + place)) & 1
                shape = (leading, chips // 2, block, columns)
                kept = lax.dynamic_index_in_dim(split, mine, 2, keepdims=False)
                sent = lax.dynamic_index_in_dim(split, 1 - mine, 2, keepdims=False)
                self.kept.append([kept.reshape(shape)])
                self.got.append([self.exchange(sent.reshape(shape), place)])
            return
        count = 1 if self.apart else len(self.values)
        now, self.values = self.values[:count], self.values[count:]
        size = self.home.ctx_size
        wide = jnp.concatenate(
            [value[at, 0] for value in now for at in range(value.shape[0])], axis=-1
        )
        wide = wide.reshape(size, wide.shape[0] // size, wide.shape[1])
        self.last = lax.dynamic_index_in_dim(wide, ctx, 0, keepdims=False)
        for far in range(1, size):
            sent = lax.dynamic_index_in_dim(wide, ctx ^ far, 0, keepdims=False)
            self.got.append(lax.ppermute(sent, "ctx", flips(size, far)))

    def advance(self):
        if not self.kept:
            total = self.last.astype(F32)
            for piece in self.got:
                total = total + piece.astype(F32)
            self.done.append(total)
            self.got = None
            if self.values:
                self.send()
            return
        self.values = [
            jnp.concatenate(
                [
                    (kept.astype(F32) + got.astype(F32)).astype(BF16)
                    for kept, got in zip(keeps, gots)
                ],
                axis=0,
            )
            for keeps, gots in zip(self.kept, self.got)
        ]
        self.send()

    def result(self):
        return self.done[0] if len(self.done) == 1 else jnp.concatenate(self.done, axis=1)


class Offload:
    def __init__(self, packed, axis, after=None):
        self.axis = axis
        self.packed = packed
        self.after = after
        if after is None:
            self.start()

    def start(self, values=()):
        if self.after is not None:
            self.packed, self.after.value, values = lax.optimization_barrier(
                (self.packed, self.after.value, values)
            )
        self.value = lax.psum_scatter(
            self.packed, BOTH, scatter_dimension=self.axis, tiled=True
        )
        return values

    def result(self):
        return self.value.astype(F32)


class Flight:
    def __init__(self):
        self.moving = []
        self.waiting = []

    def add(self, scatter):
        self.moving.append(scatter)

    def tick(self, values):
        self.moving = [item for item in self.moving if item.got is not None]
        ready = [item for item in self.moving if item.hold <= 0]
        got = [item.got for item in ready]
        values, got = lax.optimization_barrier((values, got))
        for item in self.moving:
            item.hold -= 1
        for item, piece in zip(ready, got):
            item.got = piece
            item.advance()
        self.moving = [item for item in self.moving if item.got is not None]
        return values


def layer_forward(home, flight, rows_in, rows_low, first, rest, fetch_next, lookups):
    width = rows_in.shape[1]
    gains, biases = first.gains, first.biases
    row_halves = home.halves(rows_low)
    qkv = (first.project(row_halves) + biases[:3].reshape(1, -1)).astype(BF16)
    qkv = fetch_next(flight.tick(qkv))
    other_kv = home.fetch(qkv[:, width:])
    rel_both = first.relative().astype(BF16)
    rel_query = rel_both[:, :width].reshape(2, BUCKETS, width)
    rel_key = rel_both[:, width:].reshape(2, BUCKETS, width)
    mixed, prob = attend(qkv, other_kv, rel_key, rel_query, lookups)
    mixed = flight.tick(mixed)
    rest = unpack_rest(rest)
    first_sum = rows_in + (dot(mixed, rest["out"], 1, 0) + biases[3])
    first_norm = norm_rows(first_sum, gains[0], biases[5])
    norm_low = first_norm.astype(BF16)
    hidden_pre = [
        dot(norm_low, panel, 1, 0) + first.b_in[part : part + 1]
        for part, panel in enumerate(rest["w_in"])
    ]
    active = [exact_gelu(item).astype(BF16) for item in hidden_pre]
    active = flight.tick(active)
    down_rows = biases[4]
    for item, panel in zip(active, rest["down"]):
        down_rows = down_rows + dot(item, panel, 1, 0)
    second_sum = first_norm + down_rows
    result = norm_rows(second_sum, gains[1], biases[6])
    result = flight.tick(result)
    kept = dict(
        rows_low=rows_low,
        row_halves=row_halves,
        qkv=qkv,
        other_kv=other_kv,
        rel_key=rel_key,
        rel_query=rel_query,
        prob=prob,
        mixed=mixed,
        first_sum=first_sum,
        norm_low=norm_low,
        hidden_pre=hidden_pre,
        active=active,
        second_sum=second_sum,
    )
    return result, kept, rest


class WholeSum:
    def __init__(self, home, lefts, grads, place):
        self.home, self.lefts, self.grads = home, lefts, grads
        self.place = place
        self.block = home.width // home.doc_size
        self.core = lax.axis_index("doc") % 2
        self.direct = self.block % LANES == 0
        if self.direct:
            sent = half_product(home, lefts, grads)
        else:
            whole = jnp.stack(
                [dot(left, item, 0, 0).astype(BF16) for left in lefts for item in grads]
            )
            self.whole = whole.reshape(
                whole.shape[0], home.doc_size // 2, 2, self.block, whole.shape[2]
            )
            sent = lax.dynamic_index_in_dim(self.whole, 1 - self.core, 2, keepdims=False)
        self.got = lax.ppermute(sent, "doc", flips(home.doc_size, 1))

    def finish(self):
        if self.direct:
            return half_product(self.home, self.lefts, self.grads, self.got, self.place)
        kept = lax.dynamic_index_in_dim(self.whole, self.core, 2, keepdims=False)
        return split_chips((kept.astype(F32) + self.got.astype(F32)).astype(BF16), self.place)


def split_chips(total, place):
    leading, chips, block, columns = total.shape
    split = total.reshape(leading, chips >> (place + 1), 2, 1 << place, block, columns)
    mine = (lax.axis_index("doc") >> (1 + place)) & 1
    sent = lax.dynamic_index_in_dim(split, 1 - mine, 2, keepdims=False)
    kept = lax.dynamic_index_in_dim(split, mine, 2, keepdims=False)
    shape = (leading, chips // 2, block, columns)
    return sent.reshape(shape), kept.reshape(shape)


class CoreSum:
    def __init__(self, home, terms):
        self.terms = terms
        self.got = lax.ppermute(self.product(1).astype(BF16), "doc", flips(home.doc_size, 1))

    def product(self, which):
        total = None
        for halves, grads, axis in self.terms:
            piece = dot(halves[which], grads, axis, 0)
            total = piece if total is None else total + piece
        return total

    def finish(self):
        return (self.product(0) + self.got.astype(F32)).astype(BF16)


def layer_backward(home, flight, grad_out, kept, first_weights, weights, lookups, offload):
    width = grad_out.shape[1]
    gains, biases = first_weights.gains, first_weights.biases
    top = home.doc_size.bit_length() - 3

    _, second_pull = jax.vjp(norm_rows, kept["second_sum"], gains[1], biases[6])
    grad_second, grad_gain_two, grad_offset_two = second_pull(grad_out)
    grad_down = grad_second.astype(BF16)
    if not offload:
        sum_down = WholeSum(home, kept["active"], [grad_down], top)
    grad_hidden = [
        (dot(grad_down, panel, 1, 1) * gelu_slope(item)).astype(BF16)
        for panel, item in zip(weights["down"], kept["hidden_pre"])
    ]
    if offload:
        grad_hidden, grad_down = flight.tick((grad_hidden, grad_down))
    else:
        grad_hidden, grad_down, sum_down.got = flight.tick((grad_hidden, grad_down, sum_down.got))
        sum_in = WholeSum(home, [kept["norm_low"]], grad_hidden, 0)
    grad_first_norm = grad_second
    for item, panel in zip(grad_hidden, weights["w_in"]):
        grad_first_norm = grad_first_norm + dot(item, panel, 1, 1)
    _, first_pull = jax.vjp(norm_rows, kept["first_sum"], gains[0], biases[5])
    grad_first, grad_gain_one, grad_offset_one = first_pull(grad_first_norm)
    grad_att = grad_first.astype(BF16)
    grad_mixed = dot(grad_att, weights["out"], 1, 1).astype(BF16)
    if offload:
        parts = len(grad_hidden)
        panels = panel_products(
            [*kept["active"], kept["norm_low"], kept["mixed"]],
            [grad_down, *grad_hidden, grad_att],
            [(part, 0) for part in range(parts)]
            + [(parts, 1 + part) for part in range(parts)]
            + [(parts + 1, parts + 1)],
        )
        early = Offload(panels, 0)
        grad_mixed = flight.tick(grad_mixed)
    else:
        sum_out = WholeSum(home, [kept["mixed"]], [grad_att], 0)
        halves_down = sum_down.finish()
        grad_mixed, halves_down, sum_in.got, sum_out.got = flight.tick(
            (grad_mixed, halves_down, sum_in.got, sum_out.got)
        )
        while flight.waiting:
            grad_mixed = flight.waiting.pop(0).start(grad_mixed)
        early = Scatter(home, [[halves_down], [sum_in.finish(), sum_out.finish()]], False)
        flight.add(early)

    pairs = width // PAIR
    found = []
    moved = []
    cuts = [0, pairs] if offload else [0, pairs // 2, pairs]
    for first, count in zip(cuts, [after - at for at, after in zip(cuts, cuts[1:])]):
        grad_query, grad_kv, grad_rel = attend_back(
            kept["qkv"],
            kept["other_kv"],
            grad_mixed,
            kept["prob"],
            kept["rel_key"],
            kept["rel_query"],
            lookups,
            first,
            count,
        )
        grad_query, grad_kv, grad_rel, grad_mixed = flight.tick(
            (grad_query, grad_kv, grad_rel, grad_mixed)
        )
        moved.append(home.give_back([grad_kv[chunk] for chunk in range(1, grad_kv.shape[0])]))
        found.append((grad_query, grad_kv[0], grad_rel))

    own = []
    for (_, grad_kv, _), pieces in zip(found, moved):
        total = grad_kv.astype(F32)
        for piece in pieces:
            total = total + piece.astype(F32)
        own.append(total.astype(BF16))
    grad_qkv = jnp.concatenate(
        [item[0] for item in found] + [item[0] for item in own] + [item[1] for item in own], axis=1
    )
    rel_both = [jnp.concatenate([item[2][kind] for item in found], axis=1) for kind in range(2)]
    bias_sums = jnp.sum(grad_qkv.astype(F32), axis=0).reshape(3, width)
    small = jnp.concatenate(
        [
            grad_gain_one[None],
            grad_gain_two[None],
            bias_sums,
            jnp.sum(grad_att.astype(F32), axis=0)[None],
            jnp.sum(grad_down.astype(F32), axis=0)[None],
            grad_offset_one[None],
            grad_offset_two[None],
            *[jnp.sum(item.astype(F32), axis=0)[None] for item in grad_hidden],
        ],
        axis=0,
    )
    small_rows = small.shape[0]
    small = jnp.pad(small, ((0, pad_lanes(small_rows) - small_rows), (0, 0))).astype(BF16)

    if offload:
        rel_wide = jnp.concatenate(rel_both, axis=1)
        grad_qk = dot(kept["rows_low"], grad_qkv[:, : 2 * width], 0, 0) + dot(
            home.join_rows(*first_weights.tables), rel_wide, 1, 0
        )
        grad_v = dot(kept["rows_low"], grad_qkv[:, 2 * width :], 0, 0)
        found_tables = home.join_rows(
            *[first_weights.tables_back(which, *rel_both).astype(BF16) for which in range(2)]
        )
        late = Offload(
            jnp.concatenate(
                [grad_qk.astype(BF16), grad_v.astype(BF16), found_tables, small.T], axis=1
            ),
            0,
            early,
        )
        flight.waiting.append(late)
        grad_rows = flight.tick(first_weights.back(grad_qkv, grad_first))
        return grad_rows, (early, late)
    small_halves = home.halves(small)

    def small_half(which):
        found_tables = first_weights.tables_back(which, rel_both[0], rel_both[1])
        return jnp.concatenate([found_tables, small_halves[which].astype(F32).T], axis=1)

    small_got = lax.ppermute(small_half(1).astype(BF16), "doc", flips(home.doc_size, 1))
    row_halves = kept["row_halves"]
    sum_qk = CoreSum(
        home,
        [
            (row_halves, grad_qkv[:, : 2 * width], 0),
            (first_weights.tables, jnp.concatenate(rel_both, axis=1), 1),
        ],
    )
    sum_v = CoreSum(home, [(row_halves, grad_qkv[:, 2 * width :], 0)])
    grad_rows = first_weights.back(grad_qkv, grad_first)
    grad_rows, sum_qk.got, sum_v.got, small_got = flight.tick(
        (grad_rows, sum_qk.got, sum_v.got, small_got)
    )
    small_sum = (small_half(0) + small_got.astype(F32)).astype(BF16)
    half_qk, half_v = sum_qk.finish(), sum_v.finish()
    cut = 7 * width // 4
    half_rest = jnp.concatenate([half_qk[:, cut:], half_v, small_sum], axis=1)

    def by_chip(half):
        return half.reshape(1, home.doc_size // 2, -1, half.shape[1])

    late = Scatter(
        home,
        [[split_chips(by_chip(half_qk[:, :cut]), top)], [split_chips(by_chip(half_rest), 0)]],
        False,
    )
    flight.add(late)
    return grad_rows, (early, late)


def collect(home, scatters, width, hidden):
    devices = home.doc_size * home.ctx_size
    early, late = (item.result() for item in scatters)
    shard = early.shape[0]
    down = jnp.concatenate([early[:, at : at + width] for at in range(0, hidden, width)], axis=0)
    grad_in = to_device_order(early[:, hidden : 2 * hidden], devices, shard)
    grad_out = early[:, 2 * hidden :]
    qkv = late[:, : 3 * width]
    small = late[:, 3 * width :]
    table_cols = 2 * BUCKETS
    tables = small[:, :table_cols].T.reshape(2, BUCKETS, shard)
    rows = small[:, table_cols:].T
    gains, biases = rows[:2], rows[2:9]
    b_in = rows[9 : 9 + hidden // width].reshape(-1)
    return qkv, grad_out, grad_in, down, tables, gains, biases, b_in


def body(
    mesh_shape,
    layer_input,
    text_count,
    coords,
    w_qkv,
    w_out,
    w_in,
    w_down,
    rel_tables,
    ln_gains,
    biases,
    b_in,
    cotangent,
):
    doc_size, ctx_size = mesh_shape["doc"], mesh_shape["ctx"]
    device_count = doc_size * ctx_size
    local_docs, block_rows, width = layer_input.shape
    layer_count = w_qkv.shape[0]
    hidden = w_in.shape[2]
    home = Home(mesh_shape, local_docs, block_rows, width)

    cut = 3 * width // 2
    firsts = [
        pack_first(w_qkv[layer], rel_tables[layer], ln_gains[layer], biases[layer], b_in[layer])
        for layer in range(layer_count)
    ]
    packed = [
        pack_rest(device_count, w_out[layer], w_in[layer], w_down[layer])
        for layer in range(layer_count)
    ]

    core = lax.axis_index("doc") % 2
    doc_here = lax.axis_index("ctx") // home.span
    facts = jnp.concatenate([coords.reshape(local_docs, -1), text_count[:, None]], axis=1)
    other_facts = lax.ppermute(facts, "doc", flips(doc_size, 1))
    mine = jnp.where(
        doc_here // local_docs == core,
        lax.dynamic_index_in_dim(facts, doc_here % local_docs, 0, keepdims=False),
        lax.dynamic_index_in_dim(other_facts, doc_here % local_docs, 0, keepdims=False),
    )
    place = (jnp.arange(home.seq, dtype=jnp.int32) + home.position() * home.rows) % home.seq

    def turned(values):
        twice = jnp.concatenate([values, values])
        return lax.dynamic_slice_in_dim(twice, home.position() * home.rows, home.seq)

    lookups = make_lookups(
        turned(mine[: home.seq]),
        turned(mine[home.seq : 2 * home.seq]),
        mine[2 * home.seq],
        place,
        home.rows,
    )

    arriving = home.to_home(layer_input)
    rests = [lax.all_gather(packed[0], BOTH, axis=1, tiled=True)]

    ahead = []

    def fetch_next(values):
        if len(rests) < layer_count:
            shard, block, values = lax.optimization_barrier(
                (packed[len(rests)], firsts[len(rests)], values)
            )
            rests.append(lax.all_gather(shard, BOTH, axis=1, tiled=True))
            ahead.append(Gather(home, block, cut))
        else:
            own, values = lax.optimization_barrier((cotangent, values))
            ahead.append(home.to_home(own))
        flight.add(ahead[-1])
        return values

    first_weights = []
    rest_weights = []
    kept_all = []
    outputs = []
    flight = Flight()
    ahead.append(Gather(home, firsts[0], cut))
    gather = ahead[0]
    arriving.got, gather.got, lookups = lax.optimization_barrier(
        (arriving.got, gather.got, lookups)
    )
    rows_low = arriving.result()
    current = rows_low.astype(F32)
    for layer in range(layer_count):
        first_weights.append(ahead[layer].finish())
        current, kept, rest = layer_forward(
            home,
            flight,
            current,
            rows_low,
            first_weights[layer],
            rests[layer],
            fetch_next,
            lookups,
        )
        rest_weights.append(rest)
        rows_low = current.astype(BF16)
        outputs.append(home.from_home(rows_low))
        outputs[-1].hold = 1 if layer + 1 < layer_count else 2
        flight.add(outputs[-1])
        kept_all.append(kept)
    grad_rows = ahead[-1].result().astype(F32)
    scatters = [None] * layer_count
    for layer in reversed(range(layer_count)):
        grad_rows, scatters[layer] = layer_backward(
            home,
            flight,
            grad_rows,
            kept_all[layer],
            first_weights[layer],
            rest_weights[layer],
            lookups,
            layer > 0,
        )
    grad_input = home.from_home(grad_rows.astype(BF16))
    flight.add(grad_input)
    while flight.moving:
        flight.tick(())
    totals = [collect(home, item, width, hidden) for item in scatters]

    def stack(member):
        return jnp.stack([totals[layer][member] for layer in range(layer_count)])

    return tuple(item.result() for item in (outputs[0], outputs[-1], grad_input)) + tuple(stack(member) for member in range(8))


def solution(mesh):
    placed = (
        P("doc", "ctx", None),
        P("doc"),
        P("doc", None, None),
        P(None, BOTH, None),
        P(None, BOTH, None),
        P(None, BOTH, None),
        P(None, BOTH, None),
        P(None, None, None, BOTH),
        P(None, None, BOTH),
        P(None, None, BOTH),
        P(None, BOTH),
        P("doc", "ctx", None),
    )
    return jax.shard_map(
        functools.partial(body, dict(mesh.shape)),
        mesh=mesh,
        in_specs=placed,
        out_specs=(
            P("doc", "ctx", None),
            P("doc", "ctx", None),
            P("doc", "ctx", None),
            P(None, BOTH, None),
            P(None, BOTH, None),
            P(None, BOTH, None),
            P(None, BOTH, None),
            P(None, None, None, BOTH),
            P(None, None, BOTH),
            P(None, None, BOTH),
            P(None, BOTH),
        ),
        check_vma=False,
    )
```
